256 devices in a mesh: dp: 4 (over y), mp: 16 (over x, z_lo), section: 4 (over z_hi, core).
Axes of the slice: x: 4, y: 4, z: 8 (z_hi: 2, z_lo: 4; z = z_hi * 4 + z_lo), core: 2. Of those that a mesh axis runs over, the one named last changes fastest.
Arguments:
- hidden_in: bfloat16 [64, 2560], P('dp', 'mp'), may hold values from -6 to 6
- lengths: int32 [64], P('dp'), may hold values from 0 to 7
- slots: int32 [64], P('dp'), may hold values from 0 to 71, as said below
- norm_gain: float32 [4, 2560], P('section'), may hold values from 0.5 to 1.5
- w_zxo: bfloat16 [4, 3, 5120, 2560], P('section', None, 'dp', 'mp'), may hold values from -0.125 to 0.125
- w_bcdt: bfloat16 [4, 336, 2560], P('section', 'dp', 'mp'), may hold values from -0.125 to 0.125
- conv_x_weight: float32 [4, 4, 5120], P('section', None, 'mp'), may hold values from -0.5 to 0.5
- conv_bc_weight: float32 [4, 4, 256], P('section'), may hold values from -0.5 to 0.5
- conv_x_pool: bfloat16 [4, 72, 3, 5120], P('section', 'dp', None, 'mp'), may hold values from -6 to 6
- conv_bc_pool: bfloat16 [4, 72, 3, 256], P('section', 'dp'), may hold values from -6 to 6
- state_pool: float32 [4, 72, 80, 64, 128], P('section', 'dp', 'mp'), may hold values from -1 to 1
- a_rate: float32 [4, 80], P('section', 'mp'), may hold values from 1 to 16
- dt_bias: float32 [4, 80], P('section', 'mp'), may hold values from -3 to 0
- skip_gain: float32 [4, 80], P('section', 'mp'), may hold values from 0.5 to 1.5
- gate_gain: float32 [4, 5120], P('section', 'mp'), may hold values from 0.5 to 1.5
Outputs:
- hidden_out: bfloat16 [4, 64, 2560], P('section', 'dp', 'mp')
- state_out: float32 [4, 64, 80, 64, 128], P('section', 'dp', 'mp')
The draws below stay inside these ranges and needn't reach their ends.
Inputs may be any that keep to these rules, and one draw needn't show every extreme that they name: The sequences of the d-th block of 16 name distinct slots, all from d * 18 to (d + 1) * 18 - 1.
All inputs are finite; a program needn't handle non-finite values.
Results may differ from the reference program's by a relative error of at most 0.025.
Values may be sent and summed in bfloat16 or wider, within the bound.
A program may use at most 128 MiB of HBM per device.

```python
import math
import jax
import jax.numpy as jnp
from jax import lax

D = 2560
H = 80
P_SIZE = 64
N = 128
SEQ_DEV = 16
SLOTS_DEV = 18
DI = 5120
LAYERS = 4
SEQ = 64
SLOTS = 72


def draw_slots(key, part):
    blocks = SEQ // SEQ_DEV
    block_keys = jax.random.split(key, blocks)

    def one_block(block_key, block_index):
        chosen = jax.random.permutation(block_key, SLOTS_DEV)[:SEQ_DEV].astype(jnp.int32)
        return chosen + block_index * SLOTS_DEV
    return jax.vmap(one_block)(block_keys, jnp.arange(blocks, dtype=jnp.int32)).reshape(SEQ).astype(jnp.int32)


def touch_ends(entries, stream_key, smallest, high):
    extent = entries.shape
    index_at = [jax.random.randint(jax.random.fold_in(stream_key, axis), (), 0, extent[axis]) for axis in range(len(extent))]
    entries = entries.at[tuple(index_at)].set(smallest)
    longest = extent.index(max(extent))
    index_at[longest] = (index_at[longest] + 1) % extent[longest]
    return entries.at[tuple(index_at)].set(high)


def block_levels(rng, shape, cuts, low, top_value):
    factor_of, own = 1.0, jax.random.fold_in(rng, 6)
    for dim, blocks in cuts:
        steps = jnp.exp(jax.random.uniform(jax.random.fold_in(own, dim), (blocks,), jnp.float32, low / len(cuts), top_value / len(cuts)))
        factor_of = factor_of * jnp.repeat(steps, shape[dim] // blocks).reshape([-1 if axis == dim else 1 for axis in range(len(shape))])
    return factor_of


def bell_draw(rng, shape, spread, reach, cuts=(), kind=jnp.bfloat16):
    values = jax.random.normal(rng, shape, jnp.float32) * spread
    if len(cuts) > 0:
        values = block_levels(rng, shape, cuts, -0.22, 0.18) * values
    return jnp.clip(values, min=-reach, max=reach).astype(kind)


def setup_inputs(seed: int = 0) -> dict:
    arg_keys = jax.random.split(jax.random.key(seed), 16)
    return {
        "hidden_in": bell_draw(arg_keys[0], (SEQ, D), 1.0, 6.0, ((0, 4), (1, 16))),
        "lengths": touch_ends(jax.random.randint(arg_keys[1], (SEQ,), 0, 8), jax.random.fold_in(arg_keys[1], 1), 0, 7).astype(jnp.int32),
        "slots": draw_slots(jax.random.fold_in(arg_keys[15], 71), 0),
        "norm_gain": jnp.clip(1.0 + 0.1 * jax.random.normal(arg_keys[3], (LAYERS, D), jnp.float32), 0.5, 1.5),
        "w_zxo": bell_draw(arg_keys[4], (LAYERS, 3, DI, D), D ** -0.5, 0.125, ((0, 4), (2, 4), (3, 16))),
        "w_bcdt": bell_draw(arg_keys[5], (LAYERS, 2 * N + H, D), D ** -0.5, 0.125, ((0, 4), (1, 4), (2, 16))),
        "conv_x_weight": jnp.clip(jax.random.uniform(arg_keys[6], (LAYERS, 4, DI), jnp.float32, -0.5, 0.5) * block_levels(arg_keys[6], (LAYERS, 4, DI), ((0, 4), (2, 16)), -0.4, 0.0), -0.5, 0.5),
        "conv_bc_weight": jnp.clip(jax.random.uniform(arg_keys[7], (LAYERS, 4, 2 * N), jnp.float32, -0.5, 0.5) * block_levels(arg_keys[7], (LAYERS, 4, 2 * N), ((0, 4),), -0.4, 0.0), -0.5, 0.5),
        "conv_x_pool": bell_draw(arg_keys[8], (LAYERS, SLOTS, 3, DI), 1.0, 6.0, ((0, 4), (1, 4), (3, 16))),
        "conv_bc_pool": bell_draw(arg_keys[9], (LAYERS, SLOTS, 3, 2 * N), 1.0, 6.0, ((0, 4), (1, 4))),
        "state_pool": bell_draw(arg_keys[10], (LAYERS, SLOTS, H, P_SIZE, N), 0.15, 1.0, ((0, 4), (1, 4), (2, 16)), jnp.float32),
        "a_rate": jnp.clip(jnp.exp(math.log(16.0) - 2.7725887 * jax.random.uniform(arg_keys[11], (LAYERS, H), jnp.float32) ** block_levels(arg_keys[11], (LAYERS, H), ((0, 4), (1, 16)), -0.2, 0.2)), 1.0, 16.0),
        "dt_bias": jnp.clip(-3.0 + 3.0 * jax.random.uniform(arg_keys[12], (LAYERS, H), jnp.float32) ** block_levels(arg_keys[12], (LAYERS, H), ((0, 4), (1, 16)), -0.2, 0.2), -3.0, 0.0),
        "skip_gain": jnp.clip(0.5 + 1.0 * jax.random.uniform(arg_keys[13], (LAYERS, H), jnp.float32) ** block_levels(arg_keys[13], (LAYERS, H), ((0, 4), (1, 16)), -0.2, 0.2), 0.5, 1.5),
        "gate_gain": jnp.clip(1.0 + 0.1 * jax.random.normal(arg_keys[14], (LAYERS, DI), jnp.float32), 0.5, 1.5),
    }


epsilon = 1e-05

def project(inputs, weights):
    return lax.dot_general(inputs, weights, (((1,), (1,)), ((), ())), preferred_element_type=jnp.float32)

def convolve(history, current, kernel, tap_mask):
    past_sum = lax.optimization_barrier(jnp.sum(history.astype(jnp.float32) * tap_mask[:, :, None] * kernel[None, :3, :], axis=1))
    return jax.nn.silu(past_sum + current * kernel[3][None, :])

def reference(hidden_in, lengths, slots, norm_gain, w_zxo, w_bcdt, conv_x_weight, conv_bc_weight, conv_x_pool, conv_bc_pool, state_pool, a_rate, dt_bias, skip_gain, gate_gain):
    tap_mask = (lengths[:, None] >= (3 - jnp.arange(3, dtype=jnp.int32))[None, :]).astype(jnp.float32)
    alive = (lengths > 0).astype(jnp.float32)
    hidden = hidden_in
    hiddens = []
    states = []
    for layer_index in range(LAYERS):
        residual = hidden.astype(jnp.float32)
        normed_in = (residual * lax.rsqrt(lax.optimization_barrier(jnp.mean(residual * residual, axis=1, keepdims=True)) + epsilon) * norm_gain[layer_index][None, :]).astype(jnp.bfloat16)
        gate_proj = project(normed_in, w_zxo[layer_index, 0])
        inner_proj = project(normed_in, w_zxo[layer_index, 1])
        small_proj = project(normed_in, w_bcdt[layer_index])
        step_raw = small_proj[:, 2 * N:]
        conv_x = convolve(jnp.take(conv_x_pool[layer_index], slots, axis=0), inner_proj, conv_x_weight[layer_index], tap_mask)
        conv_bc = convolve(jnp.take(conv_bc_pool[layer_index], slots, axis=0), small_proj[:, :2 * N], conv_bc_weight[layer_index], tap_mask)
        conv_b = conv_bc[:, :N]
        conv_c = conv_bc[:, N:]
        step_size = jax.nn.softplus(step_raw + dt_bias[layer_index][None, :])
        decay_rate = jnp.exp(-step_size * a_rate[layer_index][None, :])
        old_state = jnp.take(state_pool[layer_index], slots, axis=0) * alive[:, None, None, None]
        inner_heads = conv_x.reshape(SEQ, H, P_SIZE)
        new_state = decay_rate[:, :, None, None] * old_state + (step_size[:, :, None] * inner_heads)[:, :, :, None] * conv_b[:, None, None, :]
        read_out = jnp.einsum('bhpn,bn->bhp', new_state, conv_c, precision=lax.Precision.HIGHEST) + skip_gain[layer_index][None, :, None] * inner_heads
        gated = read_out.reshape(SEQ, H * P_SIZE) * jax.nn.silu(gate_proj)
        normed = (gated * lax.rsqrt(lax.optimization_barrier(jnp.mean(gated * gated, axis=1, keepdims=True)) + epsilon) * gate_gain[layer_index][None, :]).astype(jnp.bfloat16)
        summed = jnp.dot(normed, w_zxo[layer_index, 2], preferred_element_type=jnp.float32)
        hidden = (residual + summed).astype(jnp.bfloat16)
        hiddens.append(hidden)
        states.append(new_state)
    return (jnp.stack(hiddens), jnp.stack(states))
```

```python
import functools

import jax
import jax.numpy as jnp
from jax import lax
from jax.experimental import pallas as pl
from jax.experimental.pallas import tpu as pltpu
from jax.sharding import PartitionSpec as P

EPS = 1e-05
F32 = jnp.float32
BF16 = jnp.bfloat16
LANES = 128


def silu(v):
    return v * (1.0 / (1.0 + jnp.exp(-v)))


def softplus(v):
    return jnp.maximum(v, 0.0) + jnp.log1p(jnp.exp(-jnp.abs(v)))


def halves(v):
    top = v.astype(BF16).astype(F32)
    return top, v - top


def iota(shape, dim):
    return lax.broadcasted_iota(jnp.int32, shape, dim)


def mm(a, b):
    return lax.dot_general(a, b, (((1,), (0,)), ((), ())), preferred_element_type=F32)


def mm_t(a, b):
    return lax.dot_general(a, b, (((1,), (1,)), ((), ())), preferred_element_type=F32)


def kernel(
    size,
    len_s,
    slot_s,
    rate_s,
    bias_s,
    skip_s,
    hid_h,
    gain_h,
    w_h,
    wb_h,
    cxw_h,
    cbw_h,
    cxp_h,
    cbp_h,
    st_h,
    gg_h,
    hid_o,
    st_o,
    hid,
    gain,
    w,
    wb,
    cxw,
    cbw,
    cxp,
    cbp,
    st,
    gg,
    wg,
    perm,
    wsmall,
    h,
    past_x,
    past_b,
    alive,
    expand,
    old16,
    wide_b,
    wide_c,
    outer_l,
    outer_t,
    new,
    hid_new,
    send_s,
    send_m,
    send_b,
    send_c,
    recv_x,
    recv_s,
    recv_m,
    recv_b,
    recv_c,
    recv_h,
    recv_o,
    load_sem,
    store_sem,
    out_sem,
    send_sem,
    x_sem,
    w_sem,
    s_sem,
    m_sem,
    b_sem,
    c_sem,
    h_sem,
    o_sem,
):
    nd, nm, ns, rows, feat, chan, head, small, bcw, slots_dev, width, inner = size
    ratio = nm // nd
    pairs = ratio // 2
    d = lax.axis_index("dp")
    m = lax.axis_index("mp")
    sec = lax.axis_index("section")
    home = m // ratio
    mine = lax.rem(m, ratio)
    odd = lax.rem(mine, 2) == 1
    on_home = home == d
    per_dp = small // nd
    all_rows = nd * rows
    heads_dev = chan // head
    first = sec == 0
    last = sec == ns - 1

    srcs = (
        (hid_h, hid),
        (gain_h, gain),
        (wb_h, wb),
        (w_h, w),
        (cxw_h, cxw),
        (cbw_h, cbw),
        (cxp_h, cxp),
        (cbp_h, cbp),
        (st_h, st),
        (gg_h, gg),
    )
    loads = [
        pltpu.make_async_copy(src, dst, load_sem.at[i]) for i, (src, dst) in enumerate(srcs)
    ]
    for copy in loads:
        copy.start()

    barrier = pltpu.get_barrier_semaphore()

    def tell(dp, mp, section=None):
        where = {"dp": dp, "mp": mp}
        if section is not None:
            where["section"] = section
        pl.semaphore_signal(
            barrier, inc=1, device_id=where, device_id_type=pl.DeviceIdType.MESH
        )

    for i in range(nm):

        @pl.when(jnp.logical_not(on_home & (m == i)))
        def _():
            tell(home, i)

    for i in range(nd):
        for j in range(ratio):

            @pl.when(jnp.logical_not((d == i) & (m == d * ratio + j)))
            def _():
                tell(i, d * ratio + j)

    for k in range(1, nd):
        tell(lax.rem(d + k, nd), m)

    @pl.when(sec > 0)
    def _():
        for k in range(nd):
            tell(k, m, sec - 1)

    own = jnp.where(on_home, 1, 0)
    pl.semaphore_wait(
        barrier, 2 * (nm - own) + nd - 1 + jnp.where(sec < ns - 1, nd, 0)
    )

    sent = []

    def send(src, dst, recv, where, self_too=None, only=None):
        sem = send_sem.at[len(sent)]
        copy = pltpu.make_async_remote_copy(
            src_ref=src,
            dst_ref=dst,
            send_sem=sem,
            recv_sem=recv,
            device_id=where,
            device_id_type=pl.DeviceIdType.MESH,
        )
        if only is not None:

            @pl.when(only)
            def _():
                copy.start()

            sent.append((copy, only))
        elif self_too is None:
            copy.start()
            sent.append((copy, None))
        else:

            @pl.when(jnp.logical_not(self_too))
            def _():
                copy.start()

            @pl.when(self_too)
            def _():
                pltpu.make_async_copy(src, dst, recv).start()

            sent.append((copy, jnp.logical_not(self_too)))

    def arrived(ref, sem):
        pltpu.make_async_copy(ref, ref, sem).wait()

    loads[0].wait()
    loads[2].wait()
    group_w = wg.shape[2]
    wg[d] = jnp.zeros((feat, group_w), BF16)
    wg[d, :, 0:per_dp] = wb[...]
    my_rows = pl.ds(pl.multiple_of(d * rows, rows), rows)
    for k in range(1, nd):
        there = {"dp": lax.rem(d + k, nd), "mp": m}
        send(wg.at[d], wg.at[d], w_sem.at[d], there)
    for k in range(1, nd):
        there = {"dp": lax.rem(d + k, nd), "mp": m}
        send(hid, recv_x.at[my_rows], x_sem.at[d], there)
    recv_x[my_rows, :] = hid[...]

    col = iota(perm.shape, 1)
    row = iota(perm.shape, 0)
    group = row // group_w
    inside = row - group * group_w
    perm[...] = jnp.where(
        (inside < per_dp) & (col == group * per_dp + inside), 1.0, 0.0
    ).astype(BF16)
    lane_of = iota((LANES, chan), 1) // head
    expand[...] = jnp.where(
        iota((LANES, chan), 0) == m * heads_dev + lane_of, 1.0, 0.0
    ).astype(BF16)
    wide_b[...] = jnp.zeros_like(wide_b)
    wide_c[...] = jnp.zeros_like(wide_c)
    outer_l[...] = jnp.zeros_like(outer_l)
    loads[1].wait()
    offset = m * feat
    base = offset // LANES
    gain_w = gain[:, pl.ds(pl.multiple_of(base * LANES, LANES), 2 * LANES)]
    gain_w = jnp.broadcast_to(gain_w, (8, 2 * LANES))
    gain_w = pltpu.roll(
        gain_w, lax.rem(2 * LANES - (offset - base * LANES), 2 * LANES), 1
    )
    gain_row = gain_w[0:1, 0:feat]

    for k in range(1, nd):
        i = lax.rem(d + k, nd)
        arrived(wg.at[i], w_sem.at[i])
    total = mm(wg[0], perm[0:group_w, :])
    for i in range(1, nd):
        total += mm(wg[i], perm[i * group_w : (i + 1) * group_w, :])
    wsmall[...] = total.astype(BF16)
    for k in range(1, nd):
        i = lax.rem(d + k, nd)
        block = pl.ds(pl.multiple_of(i * rows, rows), rows)
        arrived(recv_x.at[block], x_sem.at[i])

    def prepare():
        for copy in loads[4:9]:
            copy.wait()
        tap = iota((3, 1), 0)
        taps_x = cxw[0:3, :]
        taps_b = cbw[0:3, :]

        def one(s, carry):
            slot = jnp.clip(slot_s[s] - d * slots_dev, 0, slots_dev - 1)
            seen = (tap + len_s[s] >= 3).astype(F32)
            past_x[pl.ds(s, 1), :] = jnp.sum(
                cxp[slot].astype(F32) * seen * taps_x, axis=0, keepdims=True
            )
            past_b[pl.ds(s, 1), :] = jnp.sum(
                cbp[slot].astype(F32) * seen * taps_b, axis=0, keepdims=True
            )
            alive[pl.ds(s, 1), :] = jnp.full(
                (1, LANES), jnp.where(len_s[s] > 0, 1.0, 0.0), F32
            )
            old16[s] = st[slot].astype(BF16)
            return carry

        lax.fori_loop(0, rows, one, 0)

    @pl.when(first)
    def _():
        h[...] = recv_x[...]

    @pl.when(jnp.logical_not(first))
    def _():
        prepare()
        arrived(recv_h, h_sem.at[0])
        acc = None
        for i in range(nd):
            arrived(recv_c.at[i], c_sem.at[i])
            part = recv_c[i].astype(F32)
            acc = part if acc is None else acc + part
        lane = iota(acc.shape, 1)
        squares = jnp.sum(
            jnp.where((lane == feat) | (lane == feat + 1), acc, 0.0), axis=1, keepdims=True
        )
        scale = lax.rsqrt(squares / inner + EPS)
        h[...] = (recv_h[...].astype(F32) + acc[:, 0:feat] * scale).astype(BF16)

    value = h[...].astype(F32)
    squares = jnp.sum(value * value, axis=1, keepdims=True)
    v = (value * gain_row).astype(BF16)
    out = mm(v, wsmall[...])
    high, low = halves(squares)
    lane = iota(out.shape, 1)
    out = jnp.where(lane == small, high, jnp.where(lane == small + 1, low, out))
    send_s[...] = out.astype(BF16)
    for k in range(nd):
        i = lax.rem(d + k, nd)
        block = pl.ds(pl.multiple_of(i * rows, rows), rows)
        for j in range(ratio):
            there = {"dp": i, "mp": d * ratio + j}
            send(
                send_s.at[block],
                recv_s.at[m],
                s_sem.at[m],
                there,
                (i == d) & (m == d * ratio + j),
            )
    loads[3].wait()
    pair = 2 * chan
    window = 3 * LANES
    for p in range(pairs):
        cols = slice(p * pair, (p + 1) * pair)
        send_m[0, :, cols] = mm(v, w[1, :, cols]).astype(BF16)
        send_m[1, :, cols] = mm(v, w[0, :, cols]).astype(BF16)
        for k in range(nd):
            i = lax.rem(d + k, nd)
            block = pl.ds(pl.multiple_of(i * rows, rows), rows)
            for e in range(2):
                j = 2 * p + e
                start = p * pair + e * (pair - window)
                there = {"dp": i, "mp": d * ratio + j}
                send(
                    send_m.at[:, block, start : start + window],
                    recv_m.at[m],
                    m_sem.at[m],
                    there,
                    (i == d) & (m == d * ratio + j),
                )

    more = jnp.logical_not(last)
    after = jnp.minimum(sec + 1, ns - 1)
    send(h, recv_h, h_sem.at[0], {"dp": d, "mp": m, "section": after}, only=more)

    @pl.when(first)
    def _():
        prepare()

    loads[9].wait()
    per_head = iota((1, chan), 1) // head
    rate_row = jnp.zeros((1, chan), F32)
    bias_row = jnp.zeros((1, chan), F32)
    skip_row = jnp.zeros((1, chan), F32)
    for i in range(heads_dev):
        rate_row = jnp.where(per_head == i, rate_s[0, i], rate_row)
        bias_row = jnp.where(per_head == i, bias_s[0, i], bias_row)
        skip_row = jnp.where(per_head == i, skip_s[0, i], skip_row)

    acc = None
    for i in range(nm):
        arrived(recv_s.at[i], s_sem.at[i])
        part = recv_s[i].astype(F32)
        acc = part if acc is None else acc + part
    lane = iota(acc.shape, 1)
    squares = jnp.sum(
        jnp.where((lane == small) | (lane == small + 1), acc, 0.0), axis=1, keepdims=True
    )
    scale = lax.rsqrt(squares / width + EPS)
    conv_b = silu(past_b[...] + acc[:, 0:bcw] * scale * cbw[3:4, :])
    b_cur = conv_b[:, 0 : bcw // 2]
    c_cur = conv_b[:, bcw // 2 :]
    high, low = halves(acc[:, bcw:])
    raw = mm(high.astype(BF16), expand[...]) + mm(low.astype(BF16), expand[...])
    step = softplus(raw * scale + bias_row)
    decay = jnp.exp(-step * rate_row) * alive[:, 0:1]
    c_high, c_low = halves(c_cur)
    c_two = jnp.concatenate([c_high, c_low], axis=0).astype(BF16)
    c_row = lax.rem(iota((2 * rows, 1), 0), rows)

    def ask(s, carry):
        return carry + mm_t(jnp.where(c_row == s, c_two, jnp.zeros_like(c_two)), old16[s])

    both = lax.fori_loop(0, rows, ask, jnp.zeros((2 * rows, chan), F32), unroll=4)
    read = both[0:rows] + both[rows:]
    bc_dot = jnp.sum(b_cur * c_cur, axis=1, keepdims=True)

    acc = None
    for i in range(nm):
        arrived(recv_m.at[i], m_sem.at[i])
        part = recv_m[i].astype(F32)
        acc = part if acc is None else acc + part
    acc_i, acc_g = acc[0], acc[1]
    acc_i = jnp.where(odd, pltpu.roll(acc_i, chan, 1), acc_i)[:, 0:chan]
    acc_g = jnp.where(odd, pltpu.roll(acc_g, chan, 1), acc_g)[:, 0:chan]
    x = silu(past_x[...] + acc_i * scale * cxw[3:4, :])
    sx = step * x
    gated = (decay * read + sx * bc_dot + skip_row * x) * silu(acc_g * scale)
    squares = jnp.sum(gated * gated, axis=1, keepdims=True)
    wide_b[:, 0:chan] = gated * gg[...]
    full = wide_b[...]
    high, low = halves(squares)
    lane = iota(full.shape, 1)
    full = jnp.where(lane == chan, high, jnp.where(lane == chan + 1, low, full))
    full = jnp.where(odd, pltpu.roll(full, window - chan, 1), full)
    send_b[...] = full.astype(BF16)
    for k in range(nm):
        i = lax.rem(m + k, nm)
        there = {"dp": home, "mp": i}
        send(
            send_b,
            recv_b.at[mine, my_rows],
            b_sem.at[mine * nd + d],
            there,
            on_home & (m == i),
        )

    s_high, s_low = halves(sx)
    d_high, d_low = halves(decay)
    b_high, b_low = halves(b_cur)
    outer_l[0:rows, 0:chan] = s_high
    outer_l[rows : 2 * rows, 0:chan] = s_high
    outer_l[2 * rows : 3 * rows, 0:chan] = s_low
    outer_l[3 * rows : 4 * rows, 0:chan] = d_high
    outer_l[4 * rows : 5 * rows, 0:chan] = d_low
    outer_t[...] = jnp.transpose(outer_l[...])[0:chan, :].astype(BF16)
    zero = jnp.zeros((rows, LANES), F32)
    one_ = jnp.ones((rows, LANES), F32)
    right = jnp.concatenate(
        [
            jnp.concatenate([b_high, b_low, b_high, zero, zero], axis=0),
            jnp.concatenate([zero, zero, zero, one_, one_], axis=0),
        ],
        axis=1,
    )
    right = jnp.concatenate(
        [right, jnp.zeros((LANES - 5 * rows, 2 * LANES), F32)], axis=0
    ).astype(BF16)
    r_row = lax.rem(iota((LANES, 1), 0), rows)

    def update(s, carry):
        slot = jnp.clip(slot_s[s] - d * slots_dev, 0, slots_dev - 1)
        both = mm(outer_t[...], jnp.where(r_row == s, right, jnp.zeros_like(right)))
        new[s] = both[:, LANES:] * st[slot] + both[:, 0:LANES]
        pltpu.make_async_copy(new.at[s], st_o.at[s], store_sem.at[s]).start()
        return carry

    lax.fori_loop(0, rows // 2, update, 0)

    out = jnp.zeros((all_rows, feat), F32)
    squares = jnp.zeros((all_rows, 1), F32)
    lane = iota((all_rows, LANES), 1)
    for p in range(pairs):
        for e in range(2):
            for i in range(nd):
                arrived(
                    recv_b.at[2 * p + e, i * rows : (i + 1) * rows],
                    b_sem.at[(2 * p + e) * nd + i],
                )
        even_t = recv_b[2 * p, :, 2 * LANES : 3 * LANES].astype(F32)
        odd_t = recv_b[2 * p + 1, :, 0:LANES].astype(F32)
        gap = chan - 2 * LANES
        squares += jnp.sum(
            jnp.where((lane == gap) | (lane == gap + 1), even_t, 0.0)
            + jnp.where(lane < 2, odd_t, 0.0),
            axis=1,
            keepdims=True,
        )
        middle = jnp.where(lane < gap, even_t, odd_t).astype(BF16)
        at = p * pair
        out += mm_t(recv_b[2 * p, :, 0 : 2 * LANES], w[2, :, at : at + 2 * LANES])
        out += mm_t(middle, w[2, :, at + 2 * LANES : at + 3 * LANES])
        out += mm_t(recv_b[2 * p + 1, :, LANES:window], w[2, :, at + 3 * LANES : at + pair])
    wide_c[:, 0:feat] = out
    full = wide_c[...]
    high, low = halves(squares)
    lane = iota(full.shape, 1)
    full = jnp.where(lane == feat, high, jnp.where(lane == feat + 1, low, full))
    send_c[...] = full.astype(BF16)

    for k in range(nd):
        there = {"dp": lax.rem(d + k, nd), "mp": m, "section": after}
        send(send_c, recv_c.at[d], c_sem.at[d], there, only=more)
    for k in range(1, nd):
        i = lax.rem(d + k, nd)
        block = pl.ds(pl.multiple_of(i * rows, rows), rows)
        send(send_c.at[block], recv_o.at[d], o_sem.at[d], {"dp": i, "mp": m})
    recv_o[d] = send_c[my_rows, :]

    lax.fori_loop(rows // 2, rows, update, 0)

    for k in range(1, nd):
        i = lax.rem(d + k, nd)
        arrived(recv_o.at[i], o_sem.at[i])
    acc = recv_o[0].astype(F32)
    for i in range(1, nd):
        acc += recv_o[i].astype(F32)
    lane = iota(acc.shape, 1)
    squares = jnp.sum(
        jnp.where((lane == feat) | (lane == feat + 1), acc, 0.0), axis=1, keepdims=True
    )
    scale = lax.rsqrt(squares / inner + EPS)
    hid_new[...] = (h[my_rows, :].astype(F32) + acc[:, 0:feat] * scale).astype(BF16)
    result = pltpu.make_async_copy(hid_new, hid_o, out_sem.at[0])
    result.start()

    for copy, cond in sent:
        if cond is None:
            copy.wait_send()
        else:

            @pl.when(cond)
            def _():
                copy.wait_send()

    def drain(s, carry):
        pltpu.make_async_copy(new.at[s], st_o.at[s], store_sem.at[s]).wait()
        return carry

    lax.fori_loop(0, rows, drain, 0)
    result.wait()


def local(
    hidden_in,
    lengths,
    slots,
    norm_gain,
    w_zxo,
    w_bcdt,
    conv_x_weight,
    conv_bc_weight,
    conv_x_pool,
    conv_bc_pool,
    state_pool,
    a_rate,
    dt_bias,
    skip_gain,
    gate_gain,
):
    nd, nm, ns = (lax.axis_size(name) for name in ("dp", "mp", "section"))
    rows, feat = hidden_in.shape
    width = norm_gain.shape[1]
    chan_dp = w_zxo.shape[2]
    per_dp = w_bcdt.shape[1]
    slots_dev, heads_dev, head, state = state_pool.shape[1:]
    chan = heads_dev * head
    bcw = conv_bc_weight.shape[2]
    small = per_dp * nd
    small_pad = -(-(small + 2) // LANES) * LANES
    group_w = -(-per_dp // LANES) * LANES
    ratio = nm // nd
    all_rows = nd * rows
    window = 3 * LANES
    size = (
        nd, nm, ns, rows, feat, chan, head, small, bcw, slots_dev, width, chan * nm,
    )
    operands = (
        lengths,
        slots,
        a_rate,
        dt_bias,
        skip_gain,
        hidden_in,
        norm_gain,
        jnp.swapaxes(w_zxo[0], 1, 2),
        jnp.swapaxes(w_bcdt[0], 0, 1),
        conv_x_weight[0],
        conv_bc_weight[0],
        conv_x_pool[0],
        conv_bc_pool[0],
        state_pool.reshape(slots_dev, chan, state),
        gate_gain,
    )
    sends = 2 * (nd - 1) + 2 * nd * ratio + nm + 2 * nd
    dma = pltpu.SemaphoreType.DMA
    scratch = (
        [pltpu.VMEM(a.shape, a.dtype) for a in operands[5:]]
        + [
            pltpu.VMEM((nd, feat, group_w), BF16),
            pltpu.VMEM((nd * group_w, small_pad), BF16),
            pltpu.VMEM((feat, small_pad), BF16),
            pltpu.VMEM((all_rows, feat), BF16),
            pltpu.VMEM((rows, chan), F32),
            pltpu.VMEM((rows, bcw), F32),
            pltpu.VMEM((rows, LANES), F32),
            pltpu.VMEM((LANES, chan), BF16),
            pltpu.VMEM((rows, chan, state), BF16),
            pltpu.VMEM((rows, window), F32),
            pltpu.VMEM((all_rows, 2 * LANES), F32),
            pltpu.VMEM((LANES, window), F32),
            pltpu.VMEM((chan, LANES), BF16),
            pltpu.VMEM((rows, chan, state), F32),
            pltpu.VMEM((rows, feat), BF16),
        ]
        + [
            pltpu.VMEM((all_rows, small_pad), BF16),
            pltpu.VMEM((2, all_rows, chan_dp), BF16),
            pltpu.VMEM((rows, window), BF16),
            pltpu.VMEM((all_rows, 2 * LANES), BF16),
        ]
        + [
            pltpu.VMEM((all_rows, feat), BF16),
            pltpu.VMEM((nm, rows, small_pad), BF16),
            pltpu.VMEM((nm, 2, rows, window), BF16),
            pltpu.VMEM((ratio, all_rows, window), BF16),
            pltpu.VMEM((nd, all_rows, 2 * LANES), BF16),
            pltpu.VMEM((all_rows, feat), BF16),
            pltpu.VMEM((nd, rows, 2 * LANES), BF16),
        ]
        + [
            dma((10,)),
            dma((rows,)),
            dma((1,)),
            dma((sends,)),
            dma((nd,)),
            dma((nd,)),
            dma((nm,)),
            dma((nm,)),
            dma((nd * ratio,)),
            dma((nd,)),
            dma((1,)),
            dma((nd,)),
        ]
    )
    hidden, states = pl.pallas_call(
        functools.partial(kernel, size),
        out_shape=(
            jax.ShapeDtypeStruct((rows, feat), BF16),
            jax.ShapeDtypeStruct((rows, chan, state), F32),
        ),
        in_specs=[pl.BlockSpec(memory_space=pltpu.SMEM)] * 5
        + [pl.BlockSpec(memory_space=pl.ANY)] * 10,
        out_specs=(
            pl.BlockSpec(memory_space=pl.ANY),
            pl.BlockSpec(memory_space=pl.ANY),
        ),
        scratch_shapes=scratch,
        compiler_params=pltpu.CompilerParams(
            collective_id=0, has_side_effects=True, vmem_limit_bytes=48 << 20
        ),
    )(*operands)
    return (
        hidden[None],
        states.reshape(1, rows, heads_dev, head, state),
    )


def solution(mesh):
    placed = (
        P("dp", "mp"),
        P("dp"),
        P("dp"),
        P("section", None),
        P("section", None, "dp", "mp"),
        P("section", "dp", "mp"),
        P("section", None, "mp"),
        P("section", None, None),
        P("section", "dp", None, "mp"),
        P("section", "dp", None, None),
        P("section", "dp", "mp", None, None),
        P("section", "mp"),
        P("section", "mp"),
        P("section", "mp"),
        P("section", "mp"),
    )
    return jax.shard_map(
        local,
        mesh=mesh,
        in_specs=placed,
        out_specs=(P("section", "dp", "mp"), P("section", "dp", "mp", None, None)),
        check_vma=False,
    )
```

```python
import functools

import jax
import jax.numpy as jnp
from jax import lax
from jax.experimental import pallas as pl
from jax.experimental.pallas import tpu as pltpu
from jax.sharding import PartitionSpec as P

EPS = 1e-05
F32 = jnp.float32
BF16 = jnp.bfloat16
LANES = 128


def silu(v):
    return v * (1.0 / (1.0 + jnp.exp(-v)))


def softplus(v):
    return jnp.maximum(v, 0.0) + jnp.log1p(jnp.exp(-jnp.abs(v)))


def halves(v):
    top = v.astype(BF16).astype(F32)
    return top, v - top


def iota(shape, dim):
    return lax.broadcasted_iota(jnp.int32, shape, dim)


def mm(a, b):
    return lax.dot_general(a, b, (((1,), (0,)), ((), ())), preferred_element_type=F32)


def mm_t(a, b):
    return lax.dot_general(a, b, (((1,), (1,)), ((), ())), preferred_element_type=F32)


def kernel(
    size,
    len_h,
    slot_h,
    rate_h,
    bias_h,
    skip_h,
    hid_h,
    gain_h,
    w_h,
    wb_h,
    cxw_h,
    cbw_h,
    cxp_h,
    cbp_h,
    st_h,
    gg_h,
    hid_o,
    st_o,
    len_s,
    slot_s,
    rate_s,
    bias_s,
    skip_s,
    hid,
    gain,
    w,
    wb,
    cxw,
    cbw,
    cxp,
    cbp,
    st,
    gg,
    wg,
    perm,
    wsmall,
    h,
    past_x,
    past_b,
    alive,
    expand,
    old16,
    wide_b,
    wide_c,
    outer_l,
    outer_t,
    new,
    hid_new,
    send_s,
    send_m,
    send_b,
    send_c,
    recv_x,
    recv_s,
    recv_m,
    recv_b,
    recv_c,
    recv_h,
    recv_o,
    load_sem,
    store_sem,
    out_sem,
    send_sem,
    x_sem,
    w_sem,
    s_sem,
    m_sem,
    b_sem,
    c_sem,
    h_sem,
    o_sem,
):
    nd, nm, ns, rows, feat, chan, head, small, bcw, slots_dev, width, inner = size
    ratio = nm // nd
    pairs = ratio // 2
    d = lax.axis_index("dp")
    m = lax.axis_index("mp")
    sec = lax.axis_index("section")
    home = m // ratio
    mine = lax.rem(m, ratio)
    odd = lax.rem(mine, 2) == 1
    on_home = home == d
    per_dp = small // nd
    all_rows = nd * rows
    heads_dev = chan // head
    first = sec == 0
    last = sec == ns - 1

    srcs = (
        (hid_h, hid),
        (gain_h, gain),
        (wb_h, wb),
        (w_h, w),
        (cxw_h, cxw),
        (cbw_h, cbw),
        (cxp_h, cxp),
        (cbp_h, cbp),
        (st_h, st),
        (gg_h, gg),
        (len_h, len_s),
        (slot_h, slot_s),
        (rate_h, rate_s),
        (bias_h, bias_s),
        (skip_h, skip_s),
    )
    loads = [
        pltpu.make_async_copy(src, dst, load_sem.at[i]) for i, (src, dst) in enumerate(srcs)
    ]
    for copy in loads:
        copy.start()

    barrier = pltpu.get_barrier_semaphore()

    def tell(dp, mp, section=None):
        where = {"dp": dp, "mp": mp}
        if section is not None:
            where["section"] = section
        pl.semaphore_signal(
            barrier, inc=1, device_id=where, device_id_type=pl.DeviceIdType.MESH
        )

    for i in range(nm):

        @pl.when(jnp.logical_not(on_home & (m == i)))
        def _():
            tell(home, i)

    for i in range(nd):
        for j in range(ratio):

            @pl.when(jnp.logical_not((d == i) & (m == d * ratio + j)))
            def _():
                tell(i, d * ratio + j)

    for k in range(1, nd):
        tell(lax.rem(d + k, nd), m)
    for k in range(1, nm):
        tell(d, lax.rem(m + k, nm))

    @pl.when(sec > 0)
    def _():
        for k in range(nd):
            tell(k, m, sec - 1)

    own = jnp.where(on_home, 1, 0)
    pl.semaphore_wait(
        barrier, 2 * (nm - own) + nd - 1 + nm - 1 + jnp.where(sec < ns - 1, nd, 0)
    )

    sent = []

    def send(src, dst, recv, where, self_too=None, only=None):
        sem = send_sem.at[len(sent)]
        copy = pltpu.make_async_remote_copy(
            src_ref=src,
            dst_ref=dst,
            send_sem=sem,
            recv_sem=recv,
            device_id=where,
            device_id_type=pl.DeviceIdType.MESH,
        )
        if only is not None:

            @pl.when(only)
            def _():
                copy.start()

            sent.append((copy, only))
        elif self_too is None:
            copy.start()
            sent.append((copy, None))
        else:

            @pl.when(jnp.logical_not(self_too))
            def _():
                copy.start()

            @pl.when(self_too)
            def _():
                pltpu.make_async_copy(src, dst, recv).start()

            sent.append((copy, jnp.logical_not(self_too)))

    def arrived(ref, sem):
        pltpu.make_async_copy(ref, ref, sem).wait()

    loads[0].wait()
    loads[2].wait()
    group_w = wg.shape[2]
    wg[d] = jnp.zeros((feat, group_w), BF16)
    wg[d, :, 0:per_dp] = wb[...]
    my_rows = pl.ds(pl.multiple_of(d * rows, rows), rows)
    for k in range(1, nd):
        there = {"dp": lax.rem(d + k, nd), "mp": m}
        send(wg.at[d], wg.at[d], w_sem.at[d], there)
    for k in range(1, nd):
        there = {"dp": lax.rem(d + k, nd), "mp": m}
        send(hid, recv_x.at[my_rows], x_sem.at[d], there)
    recv_x[my_rows, :] = hid[...]

    col = iota(perm.shape, 1)
    row = iota(perm.shape, 0)
    group = row // group_w
    inside = row - group * group_w
    perm[...] = jnp.where(
        (inside < per_dp) & (col == group * per_dp + inside), 1.0, 0.0
    ).astype(BF16)
    lane_of = iota((LANES, chan), 1) // head
    expand[...] = jnp.where(
        iota((LANES, chan), 0) == m * heads_dev + lane_of, 1.0, 0.0
    ).astype(BF16)
    wide_b[...] = jnp.zeros_like(wide_b)
    wide_c[...] = jnp.zeros_like(wide_c)
    outer_l[...] = jnp.zeros_like(outer_l)
    loads[1].wait()
    offset = m * feat
    base = offset // LANES
    gain_w = gain[:, pl.ds(pl.multiple_of(base * LANES, LANES), 2 * LANES)]
    gain_w = jnp.broadcast_to(gain_w, (8, 2 * LANES))
    gain_w = pltpu.roll(
        gain_w, lax.rem(2 * LANES - (offset - base * LANES), 2 * LANES), 1
    )
    gain_row = gain_w[0:1, 0:feat]

    for k in range(1, nd):
        i = lax.rem(d + k, nd)
        arrived(wg.at[i], w_sem.at[i])
    total = mm(wg[0], perm[0:group_w, :])
    for i in range(1, nd):
        total += mm(wg[i], perm[i * group_w : (i + 1) * group_w, :])
    wsmall[...] = total.astype(BF16)
    for k in range(1, nd):
        i = lax.rem(d + k, nd)
        block = pl.ds(pl.multiple_of(i * rows, rows), rows)
        arrived(recv_x.at[block], x_sem.at[i])

    def prepare():
        for copy in loads[4:9] + loads[10:]:
            copy.wait()
        tap = iota((3, 1), 0)
        taps_x = cxw[0:3, :]
        taps_b = cbw[0:3, :]

        def one(s, carry):
            slot = jnp.clip(slot_s[s] - d * slots_dev, 0, slots_dev - 1)
            seen = (tap + len_s[s] >= 3).astype(F32)
            past_x[pl.ds(s, 1), :] = jnp.sum(
                cxp[slot].astype(F32) * seen * taps_x, axis=0, keepdims=True
            )
            past_b[pl.ds(s, 1), :] = jnp.sum(
                cbp[slot].astype(F32) * seen * taps_b, axis=0, keepdims=True
            )
            alive[pl.ds(s, 1), :] = jnp.full(
                (1, LANES), jnp.where(len_s[s] > 0, 1.0, 0.0), F32
            )
            old16[s] = st[slot].astype(BF16)
            return carry

        lax.fori_loop(0, rows, one, 0)

    @pl.when(first)
    def _():
        h[...] = recv_x[...]

    @pl.when(jnp.logical_not(first))
    def _():
        prepare()
        arrived(recv_h, h_sem.at[0])
        acc = None
        for i in range(nd):
            arrived(recv_c.at[i], c_sem.at[i])
            part = recv_c[i].astype(F32)
            acc = part if acc is None else acc + part
        lane = iota(acc.shape, 1)
        squares = jnp.sum(
            jnp.where((lane == feat) | (lane == feat + 1), acc, 0.0), axis=1, keepdims=True
        )
        scale = lax.rsqrt(squares / inner + EPS)
        h[...] = (recv_h[...].astype(F32) + acc[:, 0:feat] * scale).astype(BF16)

    value = h[my_rows, :].astype(F32)
    squares = jnp.sum(value * value, axis=1, keepdims=True)
    out = mm((value * gain_row).astype(BF16), wsmall[...])
    high, low = halves(squares)
    lane = iota(out.shape, 1)
    out = jnp.where(lane == small, high, jnp.where(lane == small + 1, low, out))
    send_s[...] = out.astype(BF16)
    for k in range(1, nm):
        there = {"dp": d, "mp": lax.rem(m + k, nm)}
        send(send_s, recv_s.at[m], s_sem.at[m], there)
    recv_s[m] = send_s[...]
    v = (h[...].astype(F32) * gain_row).astype(BF16)
    loads[3].wait()
    pair = 2 * chan
    two = 2 * LANES
    gap = chan - two
    window = 3 * LANES
    lane = iota((all_rows, LANES), 1)
    for p in range(pairs):
        at = p * pair
        cols = slice(at, at + pair)
        inner_p = mm(v, w[1, :, cols])
        gate_p = mm(v, w[0, :, cols])
        inner_t = inner_p[:, two:window]
        gate_t = pltpu.roll(gate_p[:, two:window], gap, 1)
        send_m[2 * p, :, 0:two] = inner_p[:, 0:two].astype(BF16)
        send_m[2 * p, :, two : 2 * two] = gate_p[:, 0:two].astype(BF16)
        send_m[2 * p, :, 2 * two :] = jnp.where(lane < gap, inner_t, gate_t).astype(BF16)
        send_m[2 * p + 1, :, 0:two] = inner_p[:, window:].astype(BF16)
        send_m[2 * p + 1, :, two : 2 * two] = gate_p[:, window:].astype(BF16)
        send_m[2 * p + 1, :, 2 * two :] = jnp.where(lane < gap, gate_t, inner_t).astype(BF16)
        for k in (2, 1, 3, 0) if nd == 4 else range(nd):
            i = lax.rem(d + k, nd)
            block = pl.ds(pl.multiple_of(i * rows, rows), rows)
            for e in range(2):
                j = 2 * p + e
                there = {"dp": i, "mp": d * ratio + j}
                send(
                    send_m.at[j, block],
                    recv_m.at[m],
                    m_sem.at[m],
                    there,
                    (i == d) & (m == d * ratio + j),
                )

    more = jnp.logical_not(last)
    after = jnp.minimum(sec + 1, ns - 1)
    send(h, recv_h, h_sem.at[0], {"dp": d, "mp": m, "section": after}, only=more)

    @pl.when(first)
    def _():
        prepare()

    loads[9].wait()
    per_head = iota((1, chan), 1) // head
    rate_row = jnp.zeros((1, chan), F32)
    bias_row = jnp.zeros((1, chan), F32)
    skip_row = jnp.zeros((1, chan), F32)
    for i in range(heads_dev):
        rate_row = jnp.where(per_head == i, rate_s[0, i], rate_row)
        bias_row = jnp.where(per_head == i, bias_s[0, i], bias_row)
        skip_row = jnp.where(per_head == i, skip_s[0, i], skip_row)

    acc = None
    for k in range(nm):
        i = lax.rem(m + k, nm)
        if k > 0:
            arrived(recv_s.at[i], s_sem.at[i])
        part = recv_s[i].astype(F32)
        acc = part if acc is None else acc + part
    lane = iota(acc.shape, 1)
    squares = jnp.sum(
        jnp.where((lane == small) | (lane == small + 1), acc, 0.0), axis=1, keepdims=True
    )
    scale = lax.rsqrt(squares / width + EPS)
    conv_b = silu(past_b[...] + acc[:, 0:bcw] * scale * cbw[3:4, :])
    b_cur = conv_b[:, 0 : bcw // 2]
    c_cur = conv_b[:, bcw // 2 :]
    high, low = halves(acc[:, bcw:])
    raw = mm(high.astype(BF16), expand[...]) + mm(low.astype(BF16), expand[...])
    step = softplus(raw * scale + bias_row)
    decay = jnp.exp(-step * rate_row) * alive[:, 0:1]
    c_high, c_low = halves(c_cur)
    c_two = jnp.concatenate([c_high, c_low], axis=0).astype(BF16)
    c_row = lax.rem(iota((2 * rows, 1), 0), rows)

    def ask(s, carry):
        return carry + mm_t(jnp.where(c_row == s, c_two, jnp.zeros_like(c_two)), old16[s])

    both = lax.fori_loop(0, rows, ask, jnp.zeros((2 * rows, chan), F32), unroll=4)
    read = both[0:rows] + both[rows:]
    bc_dot = jnp.sum(b_cur * c_cur, axis=1, keepdims=True)

    acc = None
    for i in range(nm):
        arrived(recv_m.at[i], m_sem.at[i])
        part = recv_m[i].astype(F32)
        acc = part if acc is None else acc + part
    tile = acc[:, 2 * two :]
    other = pltpu.roll(tile, gap, 1)

    def in_order(part, edge):
        before = jnp.concatenate([edge, part], axis=1)
        after = jnp.concatenate([part, edge], axis=1)
        return jnp.where(odd, pltpu.roll(before, chan, 1), after)[:, 0:chan]

    acc_i = in_order(acc[:, 0:two], tile)
    acc_g = in_order(acc[:, two : 2 * two], other)
    x = silu(past_x[...] + acc_i * scale * cxw[3:4, :])
    sx = step * x
    gated = (decay * read + sx * bc_dot + skip_row * x) * silu(acc_g * scale)
    squares = jnp.sum(gated * gated, axis=1, keepdims=True)
    wide_b[:, 0:chan] = gated * gg[...]
    full = wide_b[...]
    high, low = halves(squares)
    lane = iota(full.shape, 1)
    full = jnp.where(lane == chan, high, jnp.where(lane == chan + 1, low, full))
    full = jnp.where(odd, pltpu.roll(full, window - chan, 1), full)
    send_b[...] = full.astype(BF16)
    for k in range(nm):
        i = lax.rem(m + k, nm)
        there = {"dp": home, "mp": i}
        send(
            send_b,
            recv_b.at[mine, my_rows],
            b_sem.at[mine * nd + d],
            there,
            on_home & (m == i),
        )

    s_high, s_low = halves(sx)
    d_high, d_low = halves(decay)
    b_high, b_low = halves(b_cur)
    outer_l[0:rows, 0:chan] = s_high
    outer_l[rows : 2 * rows, 0:chan] = s_high
    outer_l[2 * rows : 3 * rows, 0:chan] = s_low
    outer_l[3 * rows : 4 * rows, 0:chan] = d_high
    outer_l[4 * rows : 5 * rows, 0:chan] = d_low
    outer_t[...] = jnp.transpose(outer_l[...])[0:chan, :].astype(BF16)
    zero = jnp.zeros((rows, LANES), F32)
    one_ = jnp.ones((rows, LANES), F32)
    right = jnp.concatenate(
        [
            jnp.concatenate([b_high, b_low, b_high, zero, zero], axis=0),
            jnp.concatenate([zero, zero, zero, one_, one_], axis=0),
        ],
        axis=1,
    )
    right = jnp.concatenate(
        [right, jnp.zeros((LANES - 5 * rows, 2 * LANES), F32)], axis=0
    ).astype(BF16)
    r_row = lax.rem(iota((LANES, 1), 0), rows)

    def update(s, carry):
        slot = jnp.clip(slot_s[s] - d * slots_dev, 0, slots_dev - 1)
        both = mm(outer_t[...], jnp.where(r_row == s, right, jnp.zeros_like(right)))
        new[s] = both[:, LANES:] * st[slot] + both[:, 0:LANES]
        pltpu.make_async_copy(new.at[s], st_o.at[s], store_sem.at[s]).start()
        return carry

    lax.fori_loop(0, rows // 2, update, 0)

    out = jnp.zeros((all_rows, feat), F32)
    squares = jnp.zeros((all_rows, 1), F32)
    lane = iota((all_rows, LANES), 1)
    for p in range(pairs):
        for e in range(2):
            for i in range(nd):
                arrived(
                    recv_b.at[2 * p + e, i * rows : (i + 1) * rows],
                    b_sem.at[(2 * p + e) * nd + i],
                )
        even_t = recv_b[2 * p, :, 2 * LANES : 3 * LANES].astype(F32)
        odd_t = recv_b[2 * p + 1, :, 0:LANES].astype(F32)
        squares += jnp.sum(
            jnp.where((lane == gap) | (lane == gap + 1), even_t, 0.0)
            + jnp.where(lane < 2, odd_t, 0.0),
            axis=1,
            keepdims=True,
        )
        middle = jnp.where(lane < gap, even_t, odd_t).astype(BF16)
        at = p * pair
        out += mm_t(recv_b[2 * p, :, 0 : 2 * LANES], w[2, :, at : at + 2 * LANES])
        out += mm_t(middle, w[2, :, at + 2 * LANES : at + 3 * LANES])
        out += mm_t(recv_b[2 * p + 1, :, LANES:window], w[2, :, at + 3 * LANES : at + pair])
    wide_c[:, 0:feat] = out
    full = wide_c[...]
    high, low = halves(squares)
    lane = iota(full.shape, 1)
    full = jnp.where(lane == feat, high, jnp.where(lane == feat + 1, low, full))
    send_c[...] = full.astype(BF16)

    for k in range(nd):
        there = {"dp": lax.rem(d + k, nd), "mp": m, "section": after}
        send(send_c, recv_c.at[d], c_sem.at[d], there, only=more)
    for k in range(1, nd):
        i = lax.rem(d + k, nd)
        block = pl.ds(pl.multiple_of(i * rows, rows), rows)
        send(send_c.at[block], recv_o.at[d], o_sem.at[d], {"dp": i, "mp": m})
    recv_o[d] = send_c[my_rows, :]

    lax.fori_loop(rows // 2, rows, update, 0)

    for k in range(1, nd):
        i = lax.rem(d + k, nd)
        arrived(recv_o.at[i], o_sem.at[i])
    acc = recv_o[0].astype(F32)
    for i in range(1, nd):
        acc += recv_o[i].astype(F32)
    lane = iota(acc.shape, 1)
    squares = jnp.sum(
        jnp.where((lane == feat) | (lane == feat + 1), acc, 0.0), axis=1, keepdims=True
    )
    scale = lax.rsqrt(squares / inner + EPS)
    hid_new[...] = (h[my_rows, :].astype(F32) + acc[:, 0:feat] * scale).astype(BF16)
    result = pltpu.make_async_copy(hid_new, hid_o, out_sem.at[0])
    result.start()

    for copy, cond in sent:
        if cond is None:
            copy.wait_send()
        else:

            @pl.when(cond)
            def _():
                copy.wait_send()

    def drain(s, carry):
        pltpu.make_async_copy(new.at[s], st_o.at[s], store_sem.at[s]).wait()
        return carry

    lax.fori_loop(0, rows, drain, 0)
    result.wait()


def local(
    hidden_in,
    lengths,
    slots,
    norm_gain,
    w_zxo,
    w_bcdt,
    conv_x_weight,
    conv_bc_weight,
    conv_x_pool,
    conv_bc_pool,
    state_pool,
    a_rate,
    dt_bias,
    skip_gain,
    gate_gain,
):
    nd, nm, ns = (lax.axis_size(name) for name in ("dp", "mp", "section"))
    rows, feat = hidden_in.shape
    width = norm_gain.shape[1]
    chan_dp = w_zxo.shape[2]
    per_dp = w_bcdt.shape[1]
    slots_dev, heads_dev, head, state = state_pool.shape[1:]
    chan = heads_dev * head
    bcw = conv_bc_weight.shape[2]
    small = per_dp * nd
    small_pad = -(-(small + 2) // LANES) * LANES
    group_w = -(-per_dp // LANES) * LANES
    ratio = nm // nd
    all_rows = nd * rows
    window = 3 * LANES
    size = (
        nd, nm, ns, rows, feat, chan, head, small, bcw, slots_dev, width, chan * nm,
    )
    operands = (
        lengths,
        slots,
        a_rate,
        dt_bias,
        skip_gain,
        hidden_in,
        norm_gain,
        jnp.swapaxes(w_zxo[0], 1, 2),
        jnp.swapaxes(w_bcdt[0], 0, 1),
        conv_x_weight[0],
        conv_bc_weight[0],
        conv_x_pool[0],
        conv_bc_pool[0],
        state_pool.reshape(slots_dev, chan, state),
        gate_gain,
    )
    sends = 2 * (nd - 1) + nd * ratio + 2 * nm - 1 + 2 * nd
    dma = pltpu.SemaphoreType.DMA
    scratch = (
        [pltpu.SMEM(a.shape, a.dtype) for a in operands[:5]]
        + [pltpu.VMEM(a.shape, a.dtype) for a in operands[5:]]
        + [
            pltpu.VMEM((nd, feat, group_w), BF16),
            pltpu.VMEM((nd * group_w, small_pad), BF16),
            pltpu.VMEM((feat, small_pad), BF16),
            pltpu.VMEM((all_rows, feat), BF16),
            pltpu.VMEM((rows, chan), F32),
            pltpu.VMEM((rows, bcw), F32),
            pltpu.VMEM((rows, LANES), F32),
            pltpu.VMEM((LANES, chan), BF16),
            pltpu.VMEM((rows, chan, state), BF16),
            pltpu.VMEM((rows, window), F32),
            pltpu.VMEM((all_rows, 2 * LANES), F32),
            pltpu.VMEM((LANES, window), F32),
            pltpu.VMEM((chan, LANES), BF16),
            pltpu.VMEM((rows, chan, state), F32),
            pltpu.VMEM((rows, feat), BF16),
        ]
        + [
            pltpu.VMEM((rows, small_pad), BF16),
            pltpu.VMEM((ratio, all_rows, 2 * chan), BF16),
            pltpu.VMEM((rows, window), BF16),
            pltpu.VMEM((all_rows, 2 * LANES), BF16),
        ]
        + [
            pltpu.VMEM((all_rows, feat), BF16),
            pltpu.VMEM((nm, rows, small_pad), BF16),
            pltpu.VMEM((nm, rows, 2 * chan), BF16),
            pltpu.VMEM((ratio, all_rows, window), BF16),
            pltpu.VMEM((nd, all_rows, 2 * LANES), BF16),
            pltpu.VMEM((all_rows, feat), BF16),
            pltpu.VMEM((nd, rows, 2 * LANES), BF16),
        ]
        + [
            dma((15,)),
            dma((rows,)),
            dma((1,)),
            dma((sends,)),
            dma((nd,)),
            dma((nd,)),
            dma((nm,)),
            dma((nm,)),
            dma((nd * ratio,)),
            dma((nd,)),
            dma((1,)),
            dma((nd,)),
        ]
    )
    hidden, states = pl.pallas_call(
        functools.partial(kernel, size),
        out_shape=(
            jax.ShapeDtypeStruct((rows, feat), BF16),
            jax.ShapeDtypeStruct((rows, chan, state), F32),
        ),
        in_specs=[pl.BlockSpec(memory_space=pltpu.HBM)] * 5
        + [pl.BlockSpec(memory_space=pltpu.HBM)] * 10,
        out_specs=(
            pl.BlockSpec(memory_space=pl.ANY),
            pl.BlockSpec(memory_space=pl.ANY),
        ),
        scratch_shapes=scratch,
        compiler_params=pltpu.CompilerParams(
            collective_id=0, has_side_effects=True, vmem_limit_bytes=48 << 20
        ),
    )(*[pltpu.with_memory_space_constraint(a, pltpu.HBM) for a in operands])
    return (
        hidden[None],
        states.reshape(1, rows, heads_dev, head, state),
    )


def solution(mesh):
    placed = (
        P("dp", "mp"),
        P("dp"),
        P("dp"),
        P("section", None),
        P("section", None, "dp", "mp"),
        P("section", "dp", "mp"),
        P("section", None, "mp"),
        P("section", None, None),
        P("section", "dp", None, "mp"),
        P("section", "dp", None, None),
        P("section", "dp", "mp", None, None),
        P("section", "mp"),
        P("section", "mp"),
        P("section", "mp"),
        P("section", "mp"),
    )
    return jax.shard_map(
        local,
        mesh=mesh,
        in_specs=placed,
        out_specs=(P("section", "dp", "mp"), P("section", "dp", "mp", None, None)),
        check_vma=False,
    )
```

```python
import functools

import jax
import jax.numpy as jnp
from jax import lax
from jax.experimental import pallas as pl
from jax.experimental.pallas import tpu as pltpu
from jax.sharding import PartitionSpec as P

EPS = 1e-05
F32 = jnp.float32
BF16 = jnp.bfloat16
LANES = 128


def silu(v):
    return v * (1.0 / (1.0 + jnp.exp(-v)))


def softplus(v):
    return jnp.maximum(v, 0.0) + jnp.log1p(jnp.exp(-jnp.abs(v)))


def halves(v):
    top = v.astype(BF16).astype(F32)
    return top, v - top


def iota(shape, dim):
    return lax.broadcasted_iota(jnp.int32, shape, dim)


def mm(a, b):
    return lax.dot_general(a, b, (((1,), (0,)), ((), ())), preferred_element_type=F32)


def mm_t(a, b):
    return lax.dot_general(a, b, (((1,), (1,)), ((), ())), preferred_element_type=F32)


def kernel(
    size,
    len_h,
    slot_h,
    rate_h,
    bias_h,
    skip_h,
    hid_h,
    gain_h,
    w_h,
    wb_h,
    cxw_h,
    cbw_h,
    cxp_h,
    cbp_h,
    st_h,
    gg_h,
    hid_o,
    st_o,
    len_s,
    slot_s,
    rate_s,
    bias_s,
    skip_s,
    hid,
    gain,
    w,
    wb,
    cxw,
    cbw,
    cxp,
    cbp,
    st,
    gg,
    wg,
    perm,
    wsmall,
    h,
    past_x,
    past_b,
    alive,
    expand,
    old16,
    wide_b,
    wide_c,
    outer_l,
    outer_t,
    new,
    hid_new,
    send_s,
    send_m,
    send_b,
    send_c,
    recv_x,
    recv_s,
    recv_m,
    recv_b,
    recv_c,
    recv_h,
    recv_o,
    load_sem,
    store_sem,
    out_sem,
    send_sem,
    x_sem,
    w_sem,
    g_sem,
    s_sem,
    m_sem,
    b_sem,
    c_sem,
    h_sem,
    o_sem,
):
    nd, nm, ns, rows, feat, chan, head, small, bcw, slots_dev, width, inner = size
    ratio = nm // nd
    pairs = ratio // 2
    pair = 2 * chan
    two = 2 * LANES
    gap = chan - two
    window = 3 * LANES
    half = feat // 2
    d = lax.axis_index("dp")
    m = lax.axis_index("mp")
    sec = lax.axis_index("section")
    home = m // ratio
    mine = lax.rem(m, ratio)
    odd = lax.rem(mine, 2) == 1
    on_home = home == d
    per_dp = small // nd
    all_rows = nd * rows
    heads_dev = chan // head
    first = sec == 0
    later = sec > 0
    more = sec < ns - 1
    after = jnp.minimum(sec + 1, ns - 1)
    my_rows = pl.ds(pl.multiple_of(d * rows, rows), rows)
    far_first = (2, 1, 3, 0) if nd == 4 else tuple(range(nd))

    srcs = (
        (hid_h, hid),
        (gain_h, gain),
        (wb_h, wb),
        (w_h, w.at[d]),
        (cxw_h, cxw),
        (cbw_h, cbw),
        (cxp_h, cxp),
        (cbp_h, cbp),
        (st_h, st),
        (gg_h, gg),
        (len_h, len_s),
        (slot_h, slot_s),
        (rate_h, rate_s),
        (bias_h, bias_s),
        (skip_h, skip_s),
    )
    loads = [
        pltpu.make_async_copy(src, dst, load_sem.at[i]) for i, (src, dst) in enumerate(srcs)
    ]
    for copy in loads:
        copy.start()

    barrier = pltpu.get_barrier_semaphore()

    def tell(dp, mp, section=None):
        where = {"dp": dp, "mp": mp}
        if section is not None:
            where["section"] = section
        pl.semaphore_signal(
            barrier, inc=1, device_id=where, device_id_type=pl.DeviceIdType.MESH
        )

    for k in range(1, nd):
        tell(lax.rem(d + k, nd), m)
    for k in range(1, nm):
        tell(d, lax.rem(m + k, nm))

    @pl.when(first)
    def _():
        for i in range(nm):

            @pl.when(jnp.logical_not(on_home & (m == i)))
            def _():
                tell(home, i)

        for i in range(nd):
            for j in range(ratio):

                @pl.when(jnp.logical_not((d == i) & (m == d * ratio + j)))
                def _():
                    tell(i, d * ratio + j)

    @pl.when(sec == 1)
    def _():
        for k in range(nd):
            tell(k, m, 0)

    @pl.when(sec > 1)
    def _():
        tell(d, m, sec - 1)

    own = jnp.where(on_home, 1, 0)
    pl.semaphore_wait(
        barrier,
        nd
        - 1
        + nm
        - 1
        + jnp.where(first, 2 * (nm - own) + nd, jnp.where(more, 1, 0)),
    )

    count = 0
    bases = {}
    for name, n in (
        ("x", nd - 1),
        ("w", nd - 1),
        ("g", 8),
        ("s", nm - 1),
        ("m", nm),
        ("b", nm),
        ("c", nd),
        ("h", 1),
        ("o", nd - 1),
    ):
        bases[name] = count
        count += n

    def block_of(i):
        return pl.ds(pl.multiple_of(i * rows, rows), rows)

    def copies_x():
        for k in range(1, nd):
            there = {"dp": lax.rem(d + k, nd), "mp": m}
            yield hid, recv_x.at[my_rows], x_sem.at[d], there, None

    def copies_w():
        for k in range(1, nd):
            there = {"dp": lax.rem(d + k, nd), "mp": m}
            yield wg.at[d], wg.at[d], w_sem.at[d], there, None

    up = lax.rem(d + 1, nd)
    down = lax.rem(d + nd - 1, nd)
    across = lax.rem(d + 2, nd)

    parts = (slice(0, 2), slice(2, 3))

    def copies_g(part):
        at = parts[part]
        yield w.at[d, at], w.at[d, at], g_sem.at[part, 0], {"dp": up, "mp": m}, None
        if nd == 4:
            yield w.at[d, at], w.at[d, at], g_sem.at[part, 1], {"dp": down, "mp": m}, None

    def copies_g2(part, which):
        at = parts[part]
        if which == 0:
            block = w.at[down, at, 0:half]
            yield block, block, g_sem.at[part, 2], {"dp": up, "mp": m}, None
        else:
            block = w.at[up, at, half:feat]
            yield block, block, g_sem.at[part, 3], {"dp": down, "mp": m}, None

    def pass_on(part):
        at = parts[part]
        arrived(w.at[down, at], g_sem.at[part, 0])
        if nd == 4:
            start(bases["g"] + 4 * part + 2, copies_g2(part, 0))
            arrived(w.at[up, at], g_sem.at[part, 1])
            start(bases["g"] + 4 * part + 3, copies_g2(part, 1))

    def passed_on(part):
        at = parts[part]
        if nd == 4:
            arrived(w.at[across, at, 0:half], g_sem.at[part, 2])
            arrived(w.at[across, at, half:feat], g_sem.at[part, 3])

    def copies_s():
        for k in range(1, nm):
            there = {"dp": d, "mp": lax.rem(m + k, nm)}
            yield send_s, recv_s.at[m], s_sem.at[m], there, None

    def copies_m_first(p):
        for k in far_first:
            i = lax.rem(d + k, nd)
            for j in (2 * p, 2 * p + 1):
                there = {"dp": i, "mp": d * ratio + j}
                same = (i == d) & (m == d * ratio + j)
                yield send_m.at[j * nd + i], recv_m.at[m], m_sem.at[m], there, same

    def copies_m_later(k, p):
        i = lax.rem(home + k, nd)
        for j in (2 * p, 2 * p + 1):
            to = i * ratio + j
            yield send_m.at[to], recv_m.at[m], m_sem.at[m], {"dp": d, "mp": to}, to == m

    def copies_b_first():
        for k in range(nm):
            i = lax.rem(m + nm // 2 + k, nm)
            slot = mine * nd + d
            there = {"dp": home, "mp": i}
            yield send_b, recv_b.at[slot], b_sem.at[slot], there, on_home & (m == i)

    def copies_b_later():
        for k in range(nm):
            i = lax.rem(m + nm // 2 + k, nm)
            yield send_b, recv_b.at[m], b_sem.at[m], {"dp": d, "mp": i}, i == m

    def copies_c():
        for k in far_first:
            i = lax.rem(d + k, nd)
            there = {"dp": i, "mp": m, "section": after}
            yield send_c.at[i], recv_c.at[d], c_sem.at[d], there, None

    def copies_h(src):
        yield src, recv_h, h_sem.at[0], {"dp": d, "mp": m, "section": after}, None

    def copies_o():
        for k in range(1, nd):
            i = lax.rem(d + k, nd)
            yield send_c.at[i], recv_o.at[d], o_sem.at[d], {"dp": i, "mp": m}, None

    def remote(at, src, dst, recv, where):
        return pltpu.make_async_remote_copy(
            src_ref=src,
            dst_ref=dst,
            send_sem=send_sem.at[at],
            recv_sem=recv,
            device_id=where,
            device_id_type=pl.DeviceIdType.MESH,
        )

    def start(base, items):
        for n, (src, dst, recv, where, same) in enumerate(items):
            copy = remote(base + n, src, dst, recv, where)
            if same is None:
                copy.start()
            else:

                @pl.when(jnp.logical_not(same))
                def _():
                    copy.start()

                @pl.when(same)
                def _():
                    pltpu.make_async_copy(src, dst, recv).start()

    def finish(base, items):
        for n, (src, dst, recv, where, same) in enumerate(items):
            copy = remote(base + n, src, dst, recv, where)
            if same is None:
                copy.wait_send()
            else:

                @pl.when(jnp.logical_not(same))
                def _():
                    copy.wait_send()

    def arrived(ref, sem):
        pltpu.make_async_copy(ref, ref, sem).wait()

    loads[0].wait()

    @pl.when(first)
    def _():
        start(bases["x"], copies_x())

    loads[2].wait()
    group_w = wg.shape[2]
    wg[d] = jnp.zeros((feat, group_w), BF16)
    wg[d, :, 0:per_dp] = wb[...]
    start(bases["w"], copies_w())
    loads[3].wait()

    @pl.when(later)
    def _():
        start(bases["g"], copies_g(0))

    col = iota(perm.shape, 1)
    row = iota(perm.shape, 0)
    group = row // group_w
    inside = row - group * group_w
    perm[...] = jnp.where(
        (inside < per_dp) & (col == group * per_dp + inside), 1.0, 0.0
    ).astype(BF16)
    lane_of = iota((LANES, chan), 1) // head
    expand[...] = jnp.where(
        iota((LANES, chan), 0) == m * heads_dev + lane_of, 1.0, 0.0
    ).astype(BF16)
    wide_b[...] = jnp.zeros_like(wide_b)
    wide_c[...] = jnp.zeros_like(wide_c)
    outer_l[...] = jnp.zeros_like(outer_l)
    loads[1].wait()
    offset = m * feat
    base = offset // LANES
    gain_w = gain[:, pl.ds(pl.multiple_of(base * LANES, LANES), two)]
    gain_w = jnp.broadcast_to(gain_w, (8, two))
    gain_w = pltpu.roll(gain_w, lax.rem(two - (offset - base * LANES), two), 1)
    gain_row = gain_w[0:1, 0:feat]

    for k in range(1, nd):
        i = lax.rem(d + k, nd)
        arrived(wg.at[i], w_sem.at[i])
    total = mm(wg[0], perm[0:group_w, :])
    for i in range(1, nd):
        total += mm(wg[i], perm[i * group_w : (i + 1) * group_w, :])
    wsmall[...] = total.astype(BF16)

    def prepare():
        for copy in loads[4:9] + loads[10:]:
            copy.wait()
        tap = iota((3, 1), 0)
        taps_x = cxw[0:3, :]
        taps_b = cbw[0:3, :]

        def one(s, carry):
            slot = jnp.clip(slot_s[s] - d * slots_dev, 0, slots_dev - 1)
            seen = (tap + len_s[s] >= 3).astype(F32)
            past_x[pl.ds(s, 1), :] = jnp.sum(
                cxp[slot].astype(F32) * seen * taps_x, axis=0, keepdims=True
            )
            past_b[pl.ds(s, 1), :] = jnp.sum(
                cbp[slot].astype(F32) * seen * taps_b, axis=0, keepdims=True
            )
            alive[pl.ds(s, 1), :] = jnp.full(
                (1, LANES), jnp.where(len_s[s] > 0, 1.0, 0.0), F32
            )
            old16[s] = st[slot].astype(BF16)
            return carry

        lax.fori_loop(0, rows, one, 0)

    def after_norm(acc, residual):
        lane = iota(acc.shape, 1)
        squares = jnp.sum(
            jnp.where((lane == feat) | (lane == feat + 1), acc, 0.0), axis=1, keepdims=True
        )
        scale = lax.rsqrt(squares / inner + EPS)
        return (residual.astype(F32) + acc[:, 0:feat] * scale).astype(BF16)

    @pl.when(first)
    def _():
        h[...] = hid[...]

    @pl.when(later)
    def _():
        prepare()
        pass_on(0)
        start(bases["g"] + 4, copies_g(1))
        passed_on(0)
        arrived(recv_h, h_sem.at[0])

        @pl.when(sec == 1)
        def _():
            acc = None
            for i in range(nd):
                arrived(recv_c.at[i], c_sem.at[i])
                part = recv_c[i].astype(F32)
                acc = part if acc is None else acc + part
            h[...] = after_norm(acc, recv_h[...])

        @pl.when(sec > 1)
        def _():
            h[...] = recv_h[...]

    value = h[...].astype(F32)
    squares = jnp.sum(value * value, axis=1, keepdims=True)
    v = (value * gain_row).astype(BF16)
    out = mm(v, wsmall[...])
    high, low = halves(squares)
    lane = iota(out.shape, 1)
    out = jnp.where(lane == small, high, jnp.where(lane == small + 1, low, out))
    send_s[...] = out.astype(BF16)
    start(bases["s"], copies_s())
    recv_s[m] = send_s[...]

    def pack(inner_p, gate_p, even, other, shape):
        lane = iota((inner_p.shape[0], LANES), 1)
        inner_t = inner_p[:, two:window]
        gate_t = pltpu.roll(gate_p[:, two:window], gap, 1)
        for at, side, edge in (
            (even, slice(0, two), jnp.where(lane < gap, inner_t, gate_t)),
            (other, slice(window, pair), jnp.where(lane < gap, gate_t, inner_t)),
        ):
            send_m[at, :, 0:two] = inner_p[:, side].astype(BF16).reshape(*shape, two)
            send_m[at, :, two : 2 * two] = gate_p[:, side].astype(BF16).reshape(*shape, two)
            send_m[at, :, 2 * two :] = edge.astype(BF16).reshape(*shape, LANES)

    @pl.when(first)
    def _():
        for k in range(1, nd):
            i = lax.rem(d + k, nd)
            arrived(recv_x.at[block_of(i)], x_sem.at[i])
        recv_x[my_rows, :] = hid[...]
        v_all = (recv_x[...].astype(F32) * gain_row).astype(BF16)
        for p in range(pairs):
            cols = slice(p * pair, (p + 1) * pair)
            e = 2 * p * nd
            pack(
                mm(v_all, w[d, 1, :, cols]),
                mm(v_all, w[d, 0, :, cols]),
                slice(e, e + nd),
                slice(e + nd, e + 2 * nd),
                (nd, rows),
            )
            start(bases["m"] + e, copies_m_first(p))
        start(bases["h"], copies_h(h))
        prepare()

    @pl.when(later)
    def _():
        for n, k in enumerate(far_first):
            i = lax.rem(home + k, nd)
            for p in range(pairs):
                cols = slice(p * pair, (p + 1) * pair)
                e = i * ratio + 2 * p
                pack(mm(v, w[i, 1, :, cols]), mm(v, w[i, 0, :, cols]), e, e + 1, (rows,))
                start(bases["m"] + n * ratio + 2 * p, copies_m_later(k, p))
        pass_on(1)

    loads[9].wait()
    per_head = iota((1, chan), 1) // head
    rate_row = jnp.zeros((1, chan), F32)
    bias_row = jnp.zeros((1, chan), F32)
    skip_row = jnp.zeros((1, chan), F32)
    for i in range(heads_dev):
        rate_row = jnp.where(per_head == i, rate_s[0, i], rate_row)
        bias_row = jnp.where(per_head == i, bias_s[0, i], bias_row)
        skip_row = jnp.where(per_head == i, skip_s[0, i], skip_row)

    acc = None
    for k in range(nm):
        i = lax.rem(m + k, nm)
        if k > 0:
            arrived(recv_s.at[i], s_sem.at[i])
        part = recv_s[i].astype(F32)
        acc = part if acc is None else acc + part
    lane = iota(acc.shape, 1)
    squares = jnp.sum(
        jnp.where((lane == small) | (lane == small + 1), acc, 0.0), axis=1, keepdims=True
    )
    scale = lax.rsqrt(squares / width + EPS)
    conv_b = silu(past_b[...] + acc[:, 0:bcw] * scale * cbw[3:4, :])
    b_cur = conv_b[:, 0 : bcw // 2]
    c_cur = conv_b[:, bcw // 2 :]
    high, low = halves(acc[:, bcw:])
    raw = mm(high.astype(BF16), expand[...]) + mm(low.astype(BF16), expand[...])
    step = softplus(raw * scale + bias_row)
    decay = jnp.exp(-step * rate_row) * alive[:, 0:1]
    c_high, c_low = halves(c_cur)
    c_two = jnp.concatenate([c_high, c_low], axis=0).astype(BF16)
    c_row = lax.rem(iota((2 * rows, 1), 0), rows)

    def ask(s, carry):
        return carry + mm_t(jnp.where(c_row == s, c_two, jnp.zeros_like(c_two)), old16[s])

    both = lax.fori_loop(0, rows, ask, jnp.zeros((2 * rows, chan), F32), unroll=4)
    read = both[0:rows] + both[rows:]
    bc_dot = jnp.sum(b_cur * c_cur, axis=1, keepdims=True)

    acc = None
    for i in range(nm):
        arrived(recv_m.at[i], m_sem.at[i])
        part = recv_m[i].astype(F32)
        acc = part if acc is None else acc + part
    tile = acc[:, 2 * two :]
    other = pltpu.roll(tile, gap, 1)

    def in_order(part, edge):
        before = jnp.concatenate([edge, part], axis=1)
        behind = jnp.concatenate([part, edge], axis=1)
        return jnp.where(odd, pltpu.roll(before, chan, 1), behind)[:, 0:chan]

    acc_i = in_order(acc[:, 0:two], tile)
    acc_g = in_order(acc[:, two : 2 * two], other)
    x = silu(past_x[...] + acc_i * scale * cxw[3:4, :])
    sx = step * x
    gated = (decay * read + sx * bc_dot + skip_row * x) * silu(acc_g * scale)
    squares = jnp.sum(gated * gated, axis=1, keepdims=True)
    wide_b[:, 0:chan] = gated * gg[...]
    full = wide_b[...]
    high, low = halves(squares)
    lane = iota(full.shape, 1)
    full = jnp.where(lane == chan, high, jnp.where(lane == chan + 1, low, full))
    full = jnp.where(odd, pltpu.roll(full, window - chan, 1), full)
    send_b[...] = full.astype(BF16)

    @pl.when(first)
    def _():
        start(bases["b"], copies_b_first())

    @pl.when(later)
    def _():
        start(bases["b"], copies_b_later())

    s_high, s_low = halves(sx)
    d_high, d_low = halves(decay)
    b_high, b_low = halves(b_cur)
    outer_l[0:rows, 0:chan] = s_high
    outer_l[rows : 2 * rows, 0:chan] = s_high
    outer_l[2 * rows : 3 * rows, 0:chan] = s_low
    outer_l[3 * rows : 4 * rows, 0:chan] = d_high
    outer_l[4 * rows : 5 * rows, 0:chan] = d_low
    outer_t[...] = jnp.transpose(outer_l[...])[0:chan, :].astype(BF16)
    zero = jnp.zeros((rows, LANES), F32)
    one_ = jnp.ones((rows, LANES), F32)
    right = jnp.concatenate(
        [
            jnp.concatenate([b_high, b_low, b_high, zero, zero], axis=0),
            jnp.concatenate([zero, zero, zero, one_, one_], axis=0),
        ],
        axis=1,
    )
    right = jnp.concatenate(
        [right, jnp.zeros((LANES - 5 * rows, two), F32)], axis=0
    ).astype(BF16)
    r_row = lax.rem(iota((LANES, 1), 0), rows)

    def update(s, carry):
        slot = jnp.clip(slot_s[s] - d * slots_dev, 0, slots_dev - 1)
        both = mm(outer_t[...], jnp.where(r_row == s, right, jnp.zeros_like(right)))
        new[s] = both[:, LANES:] * st[slot] + both[:, 0:LANES]
        pltpu.make_async_copy(new.at[s], st_o.at[s], store_sem.at[s]).start()
        return carry

    lax.fori_loop(0, rows // 2, update, 0)

    def gathered(even_s, other_s, count):
        n = count * rows
        lane = iota((n, LANES), 1)
        even_t = recv_b[even_s, :, two:window].astype(F32).reshape(n, LANES)
        odd_t = recv_b[other_s, :, 0:LANES].astype(F32).reshape(n, LANES)
        squares = jnp.sum(
            jnp.where((lane == gap) | (lane == gap + 1), even_t, 0.0)
            + jnp.where(lane < 2, odd_t, 0.0),
            axis=1,
            keepdims=True,
        )
        middle = jnp.where(lane < gap, even_t, odd_t).astype(BF16)
        left = recv_b[even_s, :, 0:two].reshape(n, two)
        right = recv_b[other_s, :, LANES:window].reshape(n, two)
        return jnp.concatenate([left, middle, right], axis=1), squares

    def with_squares(out, squares, n):
        wide_c[0:n, 0:feat] = out
        full = wide_c[0:n, :]
        high, low = halves(squares)
        lane = iota(full.shape, 1)
        return jnp.where(lane == feat, high, jnp.where(lane == feat + 1, low, full))

    @pl.when(first)
    def _():
        out = jnp.zeros((all_rows, feat), F32)
        squares = jnp.zeros((all_rows, 1), F32)
        for p in range(pairs):
            e = 2 * p * nd
            for i in range(2 * nd):
                arrived(recv_b.at[e + i], b_sem.at[e + i])
            lhs, part = gathered(slice(e, e + nd), slice(e + nd, e + 2 * nd), nd)
            squares += part
            out += mm_t(lhs, w[d, 2, :, p * pair : (p + 1) * pair])
        full = with_squares(out, squares, all_rows)
        send_c[...] = full.astype(BF16).reshape(nd, rows, two)
        start(bases["c"], copies_c())
        start(bases["o"], copies_o())
        recv_o[d] = send_c[d]

    @pl.when(later)
    def _():
        passed_on(1)
        out = jnp.zeros((rows, feat), F32)
        squares = jnp.zeros((rows, 1), F32)
        for i in range(nd):
            for p in range(pairs):
                e = i * ratio + 2 * p
                arrived(recv_b.at[e], b_sem.at[e])
                arrived(recv_b.at[e + 1], b_sem.at[e + 1])
                lhs, part = gathered(e, e + 1, 1)
                squares += part
                out += mm_t(lhs, w[i, 2, :, p * pair : (p + 1) * pair])
        hid_new[...] = after_norm(with_squares(out, squares, rows), h[...])

        @pl.when(more)
        def _():
            start(bases["h"], copies_h(hid_new))

    lax.fori_loop(rows // 2, rows, update, 0)

    @pl.when(first)
    def _():
        for k in range(1, nd):
            i = lax.rem(d + k, nd)
            arrived(recv_o.at[i], o_sem.at[i])
        acc = recv_o[0].astype(F32)
        for i in range(1, nd):
            acc += recv_o[i].astype(F32)
        hid_new[...] = after_norm(acc, h[...])

    result = pltpu.make_async_copy(hid_new, hid_o, out_sem.at[0])
    result.start()

    finish(bases["w"], copies_w())
    finish(bases["s"], copies_s())

    @pl.when(first)
    def _():
        finish(bases["x"], copies_x())
        for p in range(pairs):
            finish(bases["m"] + 2 * p * nd, copies_m_first(p))
        finish(bases["h"], copies_h(h))
        finish(bases["b"], copies_b_first())
        finish(bases["c"], copies_c())
        finish(bases["o"], copies_o())

    @pl.when(later)
    def _():
        for part in (0, 1):
            finish(bases["g"] + 4 * part, copies_g(part))
            if nd == 4:
                finish(bases["g"] + 4 * part + 2, copies_g2(part, 0))
                finish(bases["g"] + 4 * part + 3, copies_g2(part, 1))
        for n, k in enumerate(far_first):
            for p in range(pairs):
                finish(bases["m"] + n * ratio + 2 * p, copies_m_later(k, p))
        finish(bases["b"], copies_b_later())

        @pl.when(more)
        def _():
            finish(bases["h"], copies_h(hid_new))

    def drain(s, carry):
        pltpu.make_async_copy(new.at[s], st_o.at[s], store_sem.at[s]).wait()
        return carry

    lax.fori_loop(0, rows, drain, 0)
    result.wait()


def local(
    hidden_in,
    lengths,
    slots,
    norm_gain,
    w_zxo,
    w_bcdt,
    conv_x_weight,
    conv_bc_weight,
    conv_x_pool,
    conv_bc_pool,
    state_pool,
    a_rate,
    dt_bias,
    skip_gain,
    gate_gain,
):
    nd, nm, ns = (lax.axis_size(name) for name in ("dp", "mp", "section"))
    rows, feat = hidden_in.shape
    width = norm_gain.shape[1]
    chan_dp = w_zxo.shape[2]
    per_dp = w_bcdt.shape[1]
    slots_dev, heads_dev, head, state = state_pool.shape[1:]
    chan = heads_dev * head
    bcw = conv_bc_weight.shape[2]
    small = per_dp * nd
    small_pad = -(-(small + 2) // LANES) * LANES
    group_w = -(-per_dp // LANES) * LANES
    ratio = nm // nd
    all_rows = nd * rows
    window = 3 * LANES
    size = (
        nd, nm, ns, rows, feat, chan, head, small, bcw, slots_dev, width, chan * nm,
    )
    operands = (
        lengths,
        slots,
        a_rate,
        dt_bias,
        skip_gain,
        hidden_in,
        norm_gain,
        jnp.swapaxes(w_zxo[0], 1, 2),
        jnp.swapaxes(w_bcdt[0], 0, 1),
        conv_x_weight[0],
        conv_bc_weight[0],
        conv_x_pool[0],
        conv_bc_pool[0],
        state_pool.reshape(slots_dev, chan, state),
        gate_gain,
    )
    sends = 4 * nd + 3 * nm + 5
    dma = pltpu.SemaphoreType.DMA
    scratch = (
        [pltpu.SMEM(a.shape, a.dtype) for a in operands[:5]]
        + [
            pltpu.VMEM((nd, *a.shape) if i == 7 else a.shape, a.dtype)
            for i, a in enumerate(operands)
            if i >= 5
        ]
        + [
            pltpu.VMEM((nd, feat, group_w), BF16),
            pltpu.VMEM((nd * group_w, small_pad), BF16),
            pltpu.VMEM((feat, small_pad), BF16),
            pltpu.VMEM((rows, feat), BF16),
            pltpu.VMEM((rows, chan), F32),
            pltpu.VMEM((rows, bcw), F32),
            pltpu.VMEM((rows, LANES), F32),
            pltpu.VMEM((LANES, chan), BF16),
            pltpu.VMEM((rows, chan, state), BF16),
            pltpu.VMEM((rows, window), F32),
            pltpu.VMEM((all_rows, 2 * LANES), F32),
            pltpu.VMEM((LANES, window), F32),
            pltpu.VMEM((chan, LANES), BF16),
            pltpu.VMEM((rows, chan, state), F32),
            pltpu.VMEM((rows, feat), BF16),
        ]
        + [
            pltpu.VMEM((rows, small_pad), BF16),
            pltpu.VMEM((nm, rows, 2 * chan), BF16),
            pltpu.VMEM((rows, window), BF16),
            pltpu.VMEM((nd, rows, 2 * LANES), BF16),
        ]
        + [
            pltpu.VMEM((all_rows, feat), BF16),
            pltpu.VMEM((nm, rows, small_pad), BF16),
            pltpu.VMEM((nm, rows, 2 * chan), BF16),
            pltpu.VMEM((nm, rows, window), BF16),
            pltpu.VMEM((nd, rows, 2 * LANES), BF16),
            pltpu.VMEM((rows, feat), BF16),
            pltpu.VMEM((nd, rows, 2 * LANES), BF16),
        ]
        + [
            dma((15,)),
            dma((rows,)),
            dma((1,)),
            dma((sends,)),
            dma((nd,)),
            dma((nd,)),
            dma((2, 4)),
            dma((nm,)),
            dma((nm,)),
            dma((nd * ratio,)),
            dma((nd,)),
            dma((1,)),
            dma((nd,)),
        ]
    )
    hidden, states = pl.pallas_call(
        functools.partial(kernel, size),
        out_shape=(
            jax.ShapeDtypeStruct((rows, feat), BF16),
            jax.ShapeDtypeStruct((rows, chan, state), F32),
        ),
        in_specs=[pl.BlockSpec(memory_space=pltpu.HBM)] * 5
        + [pl.BlockSpec(memory_space=pltpu.HBM)] * 10,
        out_specs=(
            pl.BlockSpec(memory_space=pl.ANY),
            pl.BlockSpec(memory_space=pl.ANY),
        ),
        scratch_shapes=scratch,
        compiler_params=pltpu.CompilerParams(
            collective_id=0, has_side_effects=True, vmem_limit_bytes=48 << 20
        ),
    )(*[pltpu.with_memory_space_constraint(a, pltpu.HBM) for a in operands])
    return (
        hidden[None],
        states.reshape(1, rows, heads_dev, head, state),
    )


def solution(mesh):
    placed = (
        P("dp", "mp"),
        P("dp"),
        P("dp"),
        P("section", None),
        P("section", None, "dp", "mp"),
        P("section", "dp", "mp"),
        P("section", None, "mp"),
        P("section", None, None),
        P("section", "dp", None, "mp"),
        P("section", "dp", None, None),
        P("section", "dp", "mp", None, None),
        P("section", "mp"),
        P("section", "mp"),
        P("section", "mp"),
        P("section", "mp"),
    )
    return jax.shard_map(
        local,
        mesh=mesh,
        in_specs=placed,
        out_specs=(P("section", "dp", "mp"), P("section", "dp", "mp", None, None)),
        check_vma=False,
    )
```

```python
import functools

import jax
import jax.numpy as jnp
from jax import lax
from jax.experimental import pallas as pl
from jax.experimental.pallas import tpu as pltpu
from jax.sharding import PartitionSpec as P

EPS = 1e-05
F32 = jnp.float32
BF16 = jnp.bfloat16
LANES = 128


def silu(v):
    return v * (1.0 / (1.0 + jnp.exp(-v)))


def softplus(v):
    return jnp.maximum(v, 0.0) + jnp.log1p(jnp.exp(-jnp.abs(v)))


def halves(v):
    top = v.astype(BF16).astype(F32)
    return top, v - top


def iota(shape, dim):
    return lax.broadcasted_iota(jnp.int32, shape, dim)


def mm(a, b):
    return lax.dot_general(a, b, (((1,), (0,)), ((), ())), preferred_element_type=F32)


def mm_t(a, b):
    return lax.dot_general(a, b, (((1,), (1,)), ((), ())), preferred_element_type=F32)


def kernel(
    size,
    len_h,
    slot_h,
    rate_h,
    bias_h,
    skip_h,
    hid_h,
    gain_h,
    w_h,
    wb_h,
    cxw_h,
    cbw_h,
    cxp_h,
    cbp_h,
    st_h,
    gg_h,
    hid_o,
    st_o,
    len_s,
    slot_s,
    rate_s,
    bias_s,
    skip_s,
    hid,
    gain,
    w,
    wb,
    cxw,
    cbw,
    cxp,
    cbp,
    st,
    gg,
    wg,
    perm,
    wsmall,
    h,
    past_x,
    past_b,
    alive,
    expand,
    old16,
    wide_b,
    wide_c,
    outer_l,
    outer_t,
    hid_new,
    send_s,
    send_m,
    send_b,
    send_c,
    recv_x,
    recv_s,
    recv_m,
    recv_b,
    recv_c,
    recv_h,
    recv_o,
    load_sem,
    send_sem,
    x_sem,
    w_sem,
    g_sem,
    s_sem,
    m_sem,
    b_sem,
    c_sem,
    h_sem,
    o_sem,
):
    nd, nm, ns, rows, feat, chan, head, small, bcw, slots_dev, width, inner = size
    ratio = nm // nd
    pairs = ratio // 2
    pair = 2 * chan
    two = 2 * LANES
    gap = chan - two
    window = 3 * LANES
    half = feat // 2
    d = lax.axis_index("dp")
    m = lax.axis_index("mp")
    sec = lax.axis_index("section")
    home = m // ratio
    mine = lax.rem(m, ratio)
    odd = lax.rem(mine, 2) == 1
    on_home = home == d
    per_dp = small // nd
    all_rows = nd * rows
    heads_dev = chan // head
    first = sec == 0
    later = sec > 0
    more = sec < ns - 1
    after = jnp.minimum(sec + 1, ns - 1)
    my_rows = pl.ds(pl.multiple_of(d * rows, rows), rows)
    far_first = (2, 1, 3, 0) if nd == 4 else tuple(range(nd))

    srcs = (
        (hid_h, hid),
        (gain_h, gain),
        (wb_h, wb),
        (w_h, w.at[d]),
        (cxw_h, cxw),
        (cbw_h, cbw),
        (cxp_h, cxp),
        (cbp_h, cbp),
        (st_h, st),
        (gg_h, gg),
        (len_h, len_s),
        (slot_h, slot_s),
        (rate_h, rate_s),
        (bias_h, bias_s),
        (skip_h, skip_s),
    )
    loads = [
        pltpu.make_async_copy(src, dst, load_sem.at[i]) for i, (src, dst) in enumerate(srcs)
    ]
    loads[0].start()
    loads[2].start()

    barrier = pltpu.get_barrier_semaphore()

    def tell(dp, mp, section=None):
        where = {"dp": dp, "mp": mp}
        if section is not None:
            where["section"] = section
        pl.semaphore_signal(
            barrier, inc=1, device_id=where, device_id_type=pl.DeviceIdType.MESH
        )

    for k in range(1, nd):
        tell(lax.rem(d + k, nd), m)
    for k in range(1, nm):
        tell(d, lax.rem(m + k, nm))

    @pl.when(first)
    def _():
        for i in range(nm):

            @pl.when(jnp.logical_not(on_home & (m == i)))
            def _():
                tell(home, i)

        for i in range(nd):
            for j in range(ratio):

                @pl.when(jnp.logical_not((d == i) & (m == d * ratio + j)))
                def _():
                    tell(i, d * ratio + j)

    @pl.when(sec == 1)
    def _():
        for k in range(nd):
            tell(k, m, 0)

    @pl.when(sec > 1)
    def _():
        tell(d, m, sec - 1)

    loads[3].start()
    for i in (1, *range(4, len(loads))):
        loads[i].start()

    own = jnp.where(on_home, 1, 0)
    pl.semaphore_wait(
        barrier,
        nd
        - 1
        + nm
        - 1
        + jnp.where(first, 2 * (nm - own) + nd, jnp.where(more, 1, 0)),
    )

    count = 0
    bases = {}
    for name, n in (
        ("x", nd - 1),
        ("w", nd - 1),
        ("g", 8),
        ("s", nm),
        ("m", nm),
        ("b", nm),
        ("c", nd),
        ("h", 1),
        ("o", nd - 1),
    ):
        bases[name] = count
        count += n

    def block_of(i):
        return pl.ds(pl.multiple_of(i * rows, rows), rows)

    def copies_x():
        for k in range(1, nd):
            there = {"dp": lax.rem(d + k, nd), "mp": m}
            yield hid, recv_x.at[my_rows], x_sem.at[d], there, None

    def copies_w():
        for k in range(1, nd):
            there = {"dp": lax.rem(d + k, nd), "mp": m}
            yield wg.at[d], wg.at[d], w_sem.at[d], there, None

    up = lax.rem(d + 1, nd)
    down = lax.rem(d + nd - 1, nd)
    across = lax.rem(d + 2, nd)

    parts = (slice(0, 2), slice(2, 3))

    def copies_g(part):
        at = parts[part]
        yield w.at[d, at], w.at[d, at], g_sem.at[part, 0], {"dp": up, "mp": m}, None
        if nd == 4:
            yield w.at[d, at], w.at[d, at], g_sem.at[part, 1], {"dp": down, "mp": m}, None

    def copies_g2(part, which):
        at = parts[part]
        if which == 0:
            block = w.at[down, at, 0:half]
            yield block, block, g_sem.at[part, 2], {"dp": up, "mp": m}, None
        else:
            block = w.at[up, at, half:feat]
            yield block, block, g_sem.at[part, 3], {"dp": down, "mp": m}, None

    def pass_on(part):
        at = parts[part]
        arrived(w.at[down, at], g_sem.at[part, 0])
        if nd == 4:
            start(bases["g"] + 4 * part + 2, copies_g2(part, 0))
            arrived(w.at[up, at], g_sem.at[part, 1])
            start(bases["g"] + 4 * part + 3, copies_g2(part, 1))

    def passed_on(part):
        at = parts[part]
        if nd == 4:
            arrived(w.at[across, at, 0:half], g_sem.at[part, 2])
            arrived(w.at[across, at, half:feat], g_sem.at[part, 3])

    others = sorted(range(1, nm), key=lambda k: abs(k - nm // 2))

    def copies_s():
        for k in others:
            there = {"dp": d, "mp": lax.rem(m + k, nm)}
            yield send_s, recv_s.at[m], s_sem.at[m], there, None

    def copies_m_first(p):
        for k in far_first:
            i = lax.rem(d + k, nd)
            for j in (2 * p, 2 * p + 1):
                there = {"dp": i, "mp": d * ratio + j}
                same = m == d * ratio + j if k == 0 else None
                yield send_m.at[j * nd + i], recv_m.at[m], m_sem.at[m], there, same

    def copies_m_later(k, p):
        i = lax.rem(home + k, nd)
        for j in (2 * p, 2 * p + 1):
            to = i * ratio + j
            same = to == m if k == 0 else None
            yield send_m.at[to], recv_m.at[m], m_sem.at[m], {"dp": d, "mp": to}, same

    def copies_b_first():
        for k in range(nm):
            i = lax.rem(m + nm // 2 + k, nm)
            slot = mine * nd + d
            there = {"dp": home, "mp": i}
            yield send_b, recv_b.at[slot], b_sem.at[slot], there, on_home & (m == i)

    def copies_b_later():
        for k in others:
            there = {"dp": d, "mp": lax.rem(m + k, nm)}
            yield send_b, recv_b.at[m], b_sem.at[m], there, None

    def copies_c():
        for k in far_first:
            i = lax.rem(d + k, nd)
            there = {"dp": i, "mp": m, "section": after}
            yield send_c.at[i], recv_c.at[d], c_sem.at[d], there, None

    def copies_h(src):
        yield src, recv_h, h_sem.at[0], {"dp": d, "mp": m, "section": after}, None

    def copies_o():
        for k in range(1, nd):
            i = lax.rem(d + k, nd)
            yield send_c.at[i], recv_o.at[d], o_sem.at[d], {"dp": i, "mp": m}, None

    def remote(at, src, dst, recv, where):
        return pltpu.make_async_remote_copy(
            src_ref=src,
            dst_ref=dst,
            send_sem=send_sem.at[at],
            recv_sem=recv,
            device_id=where,
            device_id_type=pl.DeviceIdType.MESH,
        )

    def start(base, items):
        for n, (src, dst, recv, where, same) in enumerate(items):
            copy = remote(base + n, src, dst, recv, where)
            if same is None:
                copy.start()
            else:

                @pl.when(jnp.logical_not(same))
                def _():
                    copy.start()

                @pl.when(same)
                def _():
                    pltpu.make_async_copy(src, dst, recv).start()

    def finish(base, items):
        for n, (src, dst, recv, where, same) in enumerate(items):
            copy = remote(base + n, src, dst, recv, where)
            if same is None:
                copy.wait_send()
            else:

                @pl.when(jnp.logical_not(same))
                def _():
                    copy.wait_send()

    def arrived(ref, sem):
        pltpu.make_async_copy(ref, ref, sem).wait()

    loads[0].wait()

    @pl.when(first)
    def _():
        start(bases["x"], copies_x())

    loads[2].wait()
    group_w = wg.shape[2]
    wg[d] = jnp.zeros((feat, group_w), BF16)
    wg[d, :, 0:per_dp] = wb[...]
    start(bases["w"], copies_w())
    loads[3].wait()

    @pl.when(later)
    def _():
        start(bases["g"], copies_g(0))

    col = iota(perm.shape, 1)
    row = iota(perm.shape, 0)
    group = row // group_w
    inside = row - group * group_w
    perm[...] = jnp.where(
        (inside < per_dp) & (col == group * per_dp + inside), 1.0, 0.0
    ).astype(BF16)
    lane_of = iota((LANES, chan), 1) // head
    expand[...] = jnp.where(
        iota((LANES, chan), 0) == m * heads_dev + lane_of, 1.0, 0.0
    ).astype(BF16)
    wide_b[...] = jnp.zeros_like(wide_b)
    wide_c[...] = jnp.zeros_like(wide_c)
    outer_l[...] = jnp.zeros_like(outer_l)
    loads[1].wait()
    offset = m * feat
    base = offset // LANES
    gain_w = gain[:, pl.ds(pl.multiple_of(base * LANES, LANES), two)]
    gain_w = jnp.broadcast_to(gain_w, (8, two))
    gain_w = pltpu.roll(gain_w, lax.rem(two - (offset - base * LANES), two), 1)
    gain_row = gain_w[0:1, 0:feat]

    def prepare():
        for copy in loads[4:9] + loads[10:]:
            copy.wait()
        tap = iota((3, 1), 0)
        taps_x = cxw[0:3, :]
        taps_b = cbw[0:3, :]

        def one(s, carry):
            slot = jnp.clip(slot_s[s] - d * slots_dev, 0, slots_dev - 1)
            seen = (tap + len_s[s] >= 3).astype(F32)
            past_x[pl.ds(s, 1), :] = jnp.sum(
                cxp[slot].astype(F32) * seen * taps_x, axis=0, keepdims=True
            )
            past_b[pl.ds(s, 1), :] = jnp.sum(
                cbp[slot].astype(F32) * seen * taps_b, axis=0, keepdims=True
            )
            alive[pl.ds(s, 1), :] = jnp.full(
                (1, LANES), jnp.where(len_s[s] > 0, 1.0, 0.0), F32
            )
            old16[s] = st[slot].astype(BF16)
            return carry

        lax.fori_loop(0, rows, one, 0)

    def after_norm(acc, residual):
        lane = iota(acc.shape, 1)
        squares = jnp.sum(
            jnp.where((lane == feat) | (lane == feat + 1), acc, 0.0), axis=1, keepdims=True
        )
        scale = lax.rsqrt(squares / inner + EPS)
        return (residual.astype(F32) + acc[:, 0:feat] * scale).astype(BF16)

    def pack(inner_p, gate_p, even, other, shape):
        lane = iota((inner_p.shape[0], LANES), 1)
        inner_t = inner_p[:, two:window]
        gate_t = pltpu.roll(gate_p[:, two:window], gap, 1)
        for at, side, edge in (
            (even, slice(0, two), jnp.where(lane < gap, inner_t, gate_t)),
            (other, slice(window, pair), jnp.where(lane < gap, gate_t, inner_t)),
        ):
            send_m[at, :, 0:two] = inner_p[:, side].astype(BF16).reshape(*shape, two)
            send_m[at, :, two : 2 * two] = gate_p[:, side].astype(BF16).reshape(*shape, two)
            send_m[at, :, 2 * two :] = edge.astype(BF16).reshape(*shape, LANES)

    def with_two(out, squares, at):
        high, low = halves(squares)
        lane = iota(out.shape, 1)
        return jnp.where(lane == at, high, jnp.where(lane == at + 1, low, out))

    def two_of(acc, at):
        lane = iota(acc.shape, 1)
        return jnp.sum(
            jnp.where((lane == at) | (lane == at + 1), acc, 0.0), axis=1, keepdims=True
        )

    def weights_small():
        for k in range(1, nd):
            i = lax.rem(d + k, nd)
            arrived(wg.at[i], w_sem.at[i])
        total = mm(wg[0], perm[0:group_w, :])
        for i in range(1, nd):
            total += mm(wg[i], perm[i * group_w : (i + 1) * group_w, :])
        wsmall[...] = total.astype(BF16)

    def start_small():
        value = h[...].astype(F32)
        squares = jnp.sum(value * value, axis=1, keepdims=True)
        v = (value * gain_row).astype(BF16)
        send_s[...] = with_two(mm(v, wsmall[...]), squares, small).astype(BF16)
        start(bases["s"], copies_s())
        pltpu.make_async_copy(send_s, recv_s.at[m], s_sem.at[m]).start()
        return v

    @pl.when(first)
    def _():
        for k in range(1, nd):
            i = lax.rem(d + k, nd)
            arrived(recv_x.at[block_of(i)], x_sem.at[i])
        recv_x[my_rows, :] = hid[...]
        h[...] = hid[...]
        v_all = (recv_x[...].astype(F32) * gain_row).astype(BF16)
        for p in range(pairs):
            cols = slice(p * pair, (p + 1) * pair)
            e = 2 * p * nd
            pack(
                mm(v_all, w[d, 1, :, cols]),
                mm(v_all, w[d, 0, :, cols]),
                slice(e, e + nd),
                slice(e + nd, e + 2 * nd),
                (nd, rows),
            )
            start(bases["m"] + e, copies_m_first(p))
        weights_small()
        start_small()
        start(bases["h"], copies_h(h))
        prepare()

    @pl.when(later)
    def _():
        weights_small()
        prepare()
        pass_on(0)
        start(bases["g"] + 4, copies_g(1))
        passed_on(0)
        arrived(recv_h, h_sem.at[0])

        @pl.when(sec == 1)
        def _():
            acc = None
            for i in range(nd):
                arrived(recv_c.at[i], c_sem.at[i])
                part = recv_c[i].astype(F32)
                acc = part if acc is None else acc + part
            h[...] = after_norm(acc, recv_h[...])

        @pl.when(sec > 1)
        def _():
            h[...] = recv_h[...]

        v = start_small()
        for n, k in enumerate(far_first):
            i = lax.rem(home + k, nd)
            for p in range(pairs):
                cols = slice(p * pair, (p + 1) * pair)
                e = i * ratio + 2 * p
                pack(mm(v, w[i, 1, :, cols]), mm(v, w[i, 0, :, cols]), e, e + 1, (rows,))
                start(bases["m"] + n * ratio + 2 * p, copies_m_later(k, p))
        pass_on(1)

    loads[9].wait()
    per_head = iota((1, chan), 1) // head
    rate_row = jnp.zeros((1, chan), F32)
    bias_row = jnp.zeros((1, chan), F32)
    skip_row = jnp.zeros((1, chan), F32)
    for i in range(heads_dev):
        rate_row = jnp.where(per_head == i, rate_s[0, i], rate_row)
        bias_row = jnp.where(per_head == i, bias_s[0, i], bias_row)
        skip_row = jnp.where(per_head == i, skip_s[0, i], skip_row)

    acc = None
    for i in range(nm):
        arrived(recv_s.at[i], s_sem.at[i])
        part = recv_s[i].astype(F32)
        acc = part if acc is None else acc + part
    squares = two_of(acc, small)
    scale = lax.rsqrt(squares / width + EPS)
    conv_b = silu(past_b[...] + acc[:, 0:bcw] * scale * cbw[3:4, :])
    b_cur = conv_b[:, 0 : bcw // 2]
    c_cur = conv_b[:, bcw // 2 :]
    high, low = halves(acc[:, bcw:])
    raw = mm(high.astype(BF16), expand[...]) + mm(low.astype(BF16), expand[...])
    step = softplus(raw * scale + bias_row)
    decay = jnp.exp(-step * rate_row) * alive[:, 0:1]
    c_high, c_low = halves(c_cur)
    c_two = jnp.concatenate([c_high, c_low], axis=0).astype(BF16)
    c_row = lax.rem(iota((2 * rows, 1), 0), rows)

    def ask(s, carry):
        return carry + mm_t(jnp.where(c_row == s, c_two, jnp.zeros_like(c_two)), old16[s])

    both = lax.fori_loop(0, rows, ask, jnp.zeros((2 * rows, chan), F32), unroll=4)
    read = both[0:rows] + both[rows:]
    bc_dot = jnp.sum(b_cur * c_cur, axis=1, keepdims=True)

    acc = None
    for i in range(nm):
        arrived(recv_m.at[i], m_sem.at[i])
        part = recv_m[i].astype(F32)
        acc = part if acc is None else acc + part
    tile = acc[:, 2 * two :]
    other = pltpu.roll(tile, gap, 1)

    def in_order(part, edge):
        before = jnp.concatenate([edge, part], axis=1)
        behind = jnp.concatenate([part, edge], axis=1)
        return jnp.where(odd, pltpu.roll(before, chan, 1), behind)[:, 0:chan]

    acc_i = in_order(acc[:, 0:two], tile)
    acc_g = in_order(acc[:, two : 2 * two], other)
    x = silu(past_x[...] + acc_i * scale * cxw[3:4, :])
    sx = step * x
    gated = (decay * read + sx * bc_dot + skip_row * x) * silu(acc_g * scale)
    squares = jnp.sum(gated * gated, axis=1, keepdims=True)
    wide_b[:, 0:chan] = gated * gg[...]
    full = wide_b[...]
    high, low = halves(squares)
    lane = iota(full.shape, 1)
    full = jnp.where(lane == chan, high, jnp.where(lane == chan + 1, low, full))
    full = jnp.where(odd, pltpu.roll(full, window - chan, 1), full)
    send_b[...] = full.astype(BF16)

    @pl.when(first)
    def _():
        start(bases["b"], copies_b_first())

    @pl.when(later)
    def _():
        start(bases["b"], copies_b_later())
        pltpu.make_async_copy(send_b, recv_b.at[m], b_sem.at[m]).start()

    s_high, s_low = halves(sx)
    d_high, d_low = halves(decay)
    b_high, b_low = halves(b_cur)
    outer_l[0:rows, 0:chan] = s_high
    outer_l[rows : 2 * rows, 0:chan] = s_high
    outer_l[2 * rows : 3 * rows, 0:chan] = s_low
    outer_l[3 * rows : 4 * rows, 0:chan] = d_high
    outer_l[4 * rows : 5 * rows, 0:chan] = d_low
    outer_t[...] = jnp.transpose(outer_l[...])[0:chan, :].astype(BF16)
    zero = jnp.zeros((rows, LANES), F32)
    one_ = jnp.ones((rows, LANES), F32)
    right = jnp.concatenate(
        [
            jnp.concatenate([b_high, b_low, b_high, zero, zero], axis=0),
            jnp.concatenate([zero, zero, zero, one_, one_], axis=0),
        ],
        axis=1,
    )
    right = jnp.concatenate(
        [right, jnp.zeros((LANES - 5 * rows, two), F32)], axis=0
    ).astype(BF16)
    r_row = lax.rem(iota((LANES, 1), 0), rows)

    def update(s, carry):
        slot = jnp.clip(slot_s[s] - d * slots_dev, 0, slots_dev - 1)
        both = mm(outer_t[...], jnp.where(r_row == s, right, jnp.zeros_like(right)))
        st_o[s] = both[:, LANES:] * st[slot] + both[:, 0:LANES]
        return carry

    before = jnp.where(more, rows // 2, rows)
    lax.fori_loop(0, before, update, 0)

    def gathered(even_s, other_s, count):
        n = count * rows
        lane = iota((n, LANES), 1)
        even_t = recv_b[even_s, :, two:window].astype(F32).reshape(n, LANES)
        odd_t = recv_b[other_s, :, 0:LANES].astype(F32).reshape(n, LANES)
        squares = jnp.sum(
            jnp.where((lane == gap) | (lane == gap + 1), even_t, 0.0)
            + jnp.where(lane < 2, odd_t, 0.0),
            axis=1,
            keepdims=True,
        )
        middle = jnp.where(lane < gap, even_t, odd_t).astype(BF16)
        left = recv_b[even_s, :, 0:two].reshape(n, two)
        right = recv_b[other_s, :, LANES:window].reshape(n, two)
        return jnp.concatenate([left, middle, right], axis=1), squares

    def with_squares(out, squares, n):
        wide_c[0:n, 0:feat] = out
        full = wide_c[0:n, :]
        high, low = halves(squares)
        lane = iota(full.shape, 1)
        return jnp.where(lane == feat, high, jnp.where(lane == feat + 1, low, full))

    @pl.when(first)
    def _():
        out = jnp.zeros((all_rows, feat), F32)
        squares = jnp.zeros((all_rows, 1), F32)
        for p in range(pairs):
            e = 2 * p * nd
            for i in range(2 * nd):
                arrived(recv_b.at[e + i], b_sem.at[e + i])
            lhs, part = gathered(slice(e, e + nd), slice(e + nd, e + 2 * nd), nd)
            squares += part
            out += mm_t(lhs, w[d, 2, :, p * pair : (p + 1) * pair])
        full = with_squares(out, squares, all_rows)
        send_c[...] = full.astype(BF16).reshape(nd, rows, two)
        start(bases["c"], copies_c())
        start(bases["o"], copies_o())
        recv_o[d] = send_c[d]

    @pl.when(later)
    def _():
        passed_on(1)
        out = jnp.zeros((rows, feat), F32)
        squares = jnp.zeros((rows, 1), F32)
        for i in range(nd):
            for p in range(pairs):
                e = i * ratio + 2 * p
                arrived(recv_b.at[e], b_sem.at[e])
                arrived(recv_b.at[e + 1], b_sem.at[e + 1])
                lhs, part = gathered(e, e + 1, 1)
                squares += part
                out += mm_t(lhs, w[i, 2, :, p * pair : (p + 1) * pair])
        hid_new[...] = after_norm(with_squares(out, squares, rows), h[...])

        @pl.when(more)
        def _():
            start(bases["h"], copies_h(hid_new))

    lax.fori_loop(before, rows, update, 0)

    @pl.when(first)
    def _():
        for k in range(1, nd):
            i = lax.rem(d + k, nd)
            arrived(recv_o.at[i], o_sem.at[i])
        acc = recv_o[0].astype(F32)
        for i in range(1, nd):
            acc += recv_o[i].astype(F32)
        hid_new[...] = after_norm(acc, h[...])

    hid_o[...] = hid_new[...]

    finish(bases["w"], copies_w())
    finish(bases["s"], copies_s())

    @pl.when(first)
    def _():
        finish(bases["x"], copies_x())
        for p in range(pairs):
            finish(bases["m"] + 2 * p * nd, copies_m_first(p))
        finish(bases["h"], copies_h(h))
        finish(bases["b"], copies_b_first())
        finish(bases["c"], copies_c())
        finish(bases["o"], copies_o())

    @pl.when(later)
    def _():
        for part in (0, 1):
            finish(bases["g"] + 4 * part, copies_g(part))
            if nd == 4:
                finish(bases["g"] + 4 * part + 2, copies_g2(part, 0))
                finish(bases["g"] + 4 * part + 3, copies_g2(part, 1))
        for n, k in enumerate(far_first):
            for p in range(pairs):
                finish(bases["m"] + n * ratio + 2 * p, copies_m_later(k, p))
        finish(bases["b"], copies_b_later())

        @pl.when(more)
        def _():
            finish(bases["h"], copies_h(hid_new))


def store(parts, hid_v, st_v, hid_o, st_o, sem):
    n = st_v.shape[0] // parts
    copies = [pltpu.make_async_copy(hid_v, hid_o, sem.at[parts])] + [
        pltpu.make_async_copy(
            st_v.at[i * n : (i + 1) * n], st_o.at[i * n : (i + 1) * n], sem.at[i]
        )
        for i in range(parts)
    ]
    for copy in copies:
        copy.start()
    for copy in copies:
        copy.wait()


def local(
    hidden_in,
    lengths,
    slots,
    norm_gain,
    w_zxo,
    w_bcdt,
    conv_x_weight,
    conv_bc_weight,
    conv_x_pool,
    conv_bc_pool,
    state_pool,
    a_rate,
    dt_bias,
    skip_gain,
    gate_gain,
):
    nd, nm, ns = (lax.axis_size(name) for name in ("dp", "mp", "section"))
    rows, feat = hidden_in.shape
    width = norm_gain.shape[1]
    chan_dp = w_zxo.shape[2]
    per_dp = w_bcdt.shape[1]
    slots_dev, heads_dev, head, state = state_pool.shape[1:]
    chan = heads_dev * head
    bcw = conv_bc_weight.shape[2]
    small = per_dp * nd
    small_pad = -(-(small + 2) // LANES) * LANES
    group_w = -(-per_dp // LANES) * LANES
    ratio = nm // nd
    all_rows = nd * rows
    window = 3 * LANES
    size = (
        nd, nm, ns, rows, feat, chan, head, small, bcw, slots_dev, width, chan * nm,
    )
    operands = (
        lengths,
        slots,
        a_rate,
        dt_bias,
        skip_gain,
        hidden_in,
        norm_gain,
        jnp.swapaxes(w_zxo[0], 1, 2),
        jnp.swapaxes(w_bcdt[0], 0, 1),
        conv_x_weight[0],
        conv_bc_weight[0],
        conv_x_pool[0],
        conv_bc_pool[0],
        state_pool.reshape(slots_dev, chan, state),
        gate_gain,
    )
    sends = 4 * nd + 3 * nm + 6
    dma = pltpu.SemaphoreType.DMA
    scratch = (
        [pltpu.SMEM(a.shape, a.dtype) for a in operands[:5]]
        + [
            pltpu.VMEM((nd, *a.shape) if i == 7 else a.shape, a.dtype)
            for i, a in enumerate(operands)
            if i >= 5
        ]
        + [
            pltpu.VMEM((nd, feat, group_w), BF16),
            pltpu.VMEM((nd * group_w, small_pad), BF16),
            pltpu.VMEM((feat, small_pad), BF16),
            pltpu.VMEM((rows, feat), BF16),
            pltpu.VMEM((rows, chan), F32),
            pltpu.VMEM((rows, bcw), F32),
            pltpu.VMEM((rows, LANES), F32),
            pltpu.VMEM((LANES, chan), BF16),
            pltpu.VMEM((rows, chan, state), BF16),
            pltpu.VMEM((rows, window), F32),
            pltpu.VMEM((all_rows, 2 * LANES), F32),
            pltpu.VMEM((LANES, window), F32),
            pltpu.VMEM((chan, LANES), BF16),
            pltpu.VMEM((rows, feat), BF16),
        ]
        + [
            pltpu.VMEM((rows, small_pad), BF16),
            pltpu.VMEM((nm, rows, 2 * chan), BF16),
            pltpu.VMEM((rows, window), BF16),
            pltpu.VMEM((nd, rows, 2 * LANES), BF16),
        ]
        + [
            pltpu.VMEM((all_rows, feat), BF16),
            pltpu.VMEM((nm, rows, small_pad), BF16),
            pltpu.VMEM((nm, rows, 2 * chan), BF16),
            pltpu.VMEM((nm, rows, window), BF16),
            pltpu.VMEM((nd, rows, 2 * LANES), BF16),
            pltpu.VMEM((rows, feat), BF16),
            pltpu.VMEM((nd, rows, 2 * LANES), BF16),
        ]
        + [
            dma((15,)),
            dma((sends,)),
            dma((nd,)),
            dma((nd,)),
            dma((2, 4)),
            dma((nm,)),
            dma((nm,)),
            dma((nd * ratio,)),
            dma((nd,)),
            dma((1,)),
            dma((nd,)),
        ]
    )
    inside = pl.pallas_call(
        functools.partial(kernel, size),
        out_shape=(
            jax.ShapeDtypeStruct((rows, feat), BF16),
            jax.ShapeDtypeStruct((rows, chan, state), F32),
        ),
        in_specs=[pl.BlockSpec(memory_space=pltpu.HBM)] * 5
        + [pl.BlockSpec(memory_space=pltpu.HBM)] * 10,
        out_specs=(
            pl.BlockSpec(memory_space=pltpu.VMEM),
            pl.BlockSpec(memory_space=pltpu.VMEM),
        ),
        scratch_shapes=scratch,
        compiler_params=pltpu.CompilerParams(
            collective_id=0, has_side_effects=True, vmem_limit_bytes=48 << 20
        ),
    )(*[pltpu.with_memory_space_constraint(a, pltpu.HBM) for a in operands])
    hidden, states = pl.pallas_call(
        functools.partial(store, rows // 2),
        out_shape=(
            jax.ShapeDtypeStruct((rows, feat), BF16),
            jax.ShapeDtypeStruct((rows, chan, state), F32),
        ),
        in_specs=[pl.BlockSpec(memory_space=pltpu.VMEM)] * 2,
        out_specs=(pl.BlockSpec(memory_space=pltpu.HBM),) * 2,
        scratch_shapes=[dma((1 + rows // 2,))],
        compiler_params=pltpu.CompilerParams(vmem_limit_bytes=8 << 20),
    )(*inside)
    return (
        hidden[None],
        states.reshape(1, rows, heads_dev, head, state),
    )


def solution(mesh):
    placed = (
        P("dp", "mp"),
        P("dp"),
        P("dp"),
        P("section", None),
        P("section", None, "dp", "mp"),
        P("section", "dp", "mp"),
        P("section", None, "mp"),
        P("section", None, None),
        P("section", "dp", None, "mp"),
        P("section", "dp", None, None),
        P("section", "dp", "mp", None, None),
        P("section", "mp"),
        P("section", "mp"),
        P("section", "mp"),
        P("section", "mp"),
    )
    return jax.shard_map(
        local,
        mesh=mesh,
        in_specs=placed,
        out_specs=(P("section", "dp", "mp"), P("section", "dp", "mp", None, None)),
        check_vma=False,
    )
```

```python
import functools

import jax
import jax.numpy as jnp
from jax import lax
from jax.experimental import pallas as pl
from jax.experimental.pallas import tpu as pltpu
from jax.sharding import PartitionSpec as P

EPS = 1e-05
F32 = jnp.float32
BF16 = jnp.bfloat16
LANES = 128


def silu(v):
    return v * (1.0 / (1.0 + jnp.exp(-v)))


def softplus(v):
    return jnp.maximum(v, 0.0) + jnp.log1p(jnp.exp(-jnp.abs(v)))


def halves(v):
    top = v.astype(BF16).astype(F32)
    return top, v - top


def iota(shape, dim):
    return lax.broadcasted_iota(jnp.int32, shape, dim)


def mm(a, b):
    return lax.dot_general(a, b, (((1,), (0,)), ((), ())), preferred_element_type=F32)


def mm_t(a, b):
    return lax.dot_general(a, b, (((1,), (1,)), ((), ())), preferred_element_type=F32)


def kernel(
    size,
    len_h,
    slot_h,
    rate_h,
    bias_h,
    skip_h,
    hid_h,
    gain_h,
    w_h,
    wb_h,
    cxw_h,
    cbw_h,
    cxp_h,
    cbp_h,
    st_h,
    gg_h,
    hid_o,
    st_o,
    len_s,
    slot_s,
    rate_s,
    bias_s,
    skip_s,
    hid,
    gain,
    w,
    wb,
    cxw,
    cbw,
    cxp,
    cbp,
    st,
    gg,
    wg,
    perm,
    wsmall,
    h,
    past_x,
    past_b,
    alive,
    expand,
    old16,
    wide_b,
    wide_c,
    outer_l,
    outer_t,
    hid_new,
    acc_s,
    acc_b,
    acc_m,
    send_s,
    send_u,
    send_m,
    send_b,
    send_c,
    recv_x,
    recv_s,
    recv_t,
    recv_u,
    recv_m,
    recv_b,
    recv_c,
    recv_h,
    recv_o,
    load_sem,
    send_sem,
    x_sem,
    w_sem,
    g_sem,
    s_sem,
    t_sem,
    u_sem,
    m_sem,
    b_sem,
    c_sem,
    h_sem,
    o_sem,
):
    nd, nm, ns, rows, feat, chan, head, small, bcw, slots_dev, width, inner = size
    ratio = nm // nd
    pairs = ratio // 2
    pair = 2 * chan
    two = 2 * LANES
    gap = chan - two
    window = 3 * LANES
    half = feat // 2
    side = bcw // 2
    front = wsmall.shape[1] - side
    mark = small - side
    d = lax.axis_index("dp")
    m = lax.axis_index("mp")
    sec = lax.axis_index("section")
    home = m // ratio
    mine = lax.rem(m, ratio)
    odd = lax.rem(mine, 2) == 1
    on_home = home == d
    per_dp = small // nd
    all_rows = nd * rows
    heads_dev = chan // head
    first = sec == 0
    later = sec > 0
    more = sec < ns - 1
    after = jnp.minimum(sec + 1, ns - 1)
    my_rows = pl.ds(pl.multiple_of(d * rows, rows), rows)
    far_first = (2, 1, 3, 0) if nd == 4 else tuple(range(nd))

    srcs = (
        (hid_h, hid),
        (gain_h, gain),
        (wb_h, wb),
        (w_h, w.at[d]),
        (cxw_h, cxw),
        (cbw_h, cbw),
        (cxp_h, cxp),
        (cbp_h, cbp),
        (st_h, st),
        (gg_h, gg),
        (len_h, len_s),
        (slot_h, slot_s),
        (rate_h, rate_s),
        (bias_h, bias_s),
        (skip_h, skip_s),
    )
    loads = [
        pltpu.make_async_copy(src, dst, load_sem.at[i]) for i, (src, dst) in enumerate(srcs)
    ]
    loads[0].start()
    loads[2].start()

    barrier = pltpu.get_barrier_semaphore()

    def tell(dp, mp, section=None):
        where = {"dp": dp, "mp": mp}
        if section is not None:
            where["section"] = section
        pl.semaphore_signal(
            barrier, inc=1, device_id=where, device_id_type=pl.DeviceIdType.MESH
        )

    for k in range(1, nd):
        tell(lax.rem(d + k, nd), m)
    for k in range(1, nm):
        tell(d, lax.rem(m + k, nm))

    @pl.when(first)
    def _():
        for i in range(nm):

            @pl.when(jnp.logical_not(on_home & (m == i)))
            def _():
                tell(home, i)

        for i in range(nd):
            for j in range(ratio):

                @pl.when(jnp.logical_not((d == i) & (m == d * ratio + j)))
                def _():
                    tell(i, d * ratio + j)

    @pl.when(sec == 1)
    def _():
        for k in range(nd):
            tell(k, m, 0)

    @pl.when(sec > 1)
    def _():
        tell(d, m, sec - 1)

    loads[3].start()
    for i in (1, *range(4, len(loads))):
        loads[i].start()

    own = jnp.where(on_home, 1, 0)
    pl.semaphore_wait(
        barrier,
        nd
        - 1
        + nm
        - 1
        + jnp.where(first, 2 * (nm - own) + nd, jnp.where(more, 1, 0)),
    )

    count = 0
    bases = {}
    for name, n in (
        ("x", nd - 1),
        ("w", nd - 1),
        ("g", 8),
        ("s", nm),
        ("m", nm),
        ("b", nm),
        ("c", nd),
        ("h", 1),
        ("o", nd - 1),
        ("t", nd - 1),
        ("u", ratio - 1),
    ):
        bases[name] = count
        count += n

    def block_of(i):
        return pl.ds(pl.multiple_of(i * rows, rows), rows)

    def copies_x():
        for k in range(1, nd):
            there = {"dp": lax.rem(d + k, nd), "mp": m}
            yield hid, recv_x.at[my_rows], x_sem.at[d], there, None

    def copies_w():
        for k in range(1, nd):
            there = {"dp": lax.rem(d + k, nd), "mp": m}
            yield wg.at[d], wg.at[d], w_sem.at[d], there, None

    up = lax.rem(d + 1, nd)
    down = lax.rem(d + nd - 1, nd)
    across = lax.rem(d + 2, nd)

    parts = (slice(0, 2), slice(2, 3))

    def copies_g(part):
        at = parts[part]
        yield w.at[d, at], w.at[d, at], g_sem.at[part, 0], {"dp": up, "mp": m}, None
        if nd == 4:
            yield w.at[d, at], w.at[d, at], g_sem.at[part, 1], {"dp": down, "mp": m}, None

    def copies_g2(part, which):
        at = parts[part]
        if which == 0:
            block = w.at[down, at, 0:half]
            yield block, block, g_sem.at[part, 2], {"dp": up, "mp": m}, None
        else:
            block = w.at[up, at, half:feat]
            yield block, block, g_sem.at[part, 3], {"dp": down, "mp": m}, None

    def pass_on(part):
        at = parts[part]
        arrived(w.at[down, at], g_sem.at[part, 0])
        if nd == 4:
            start(bases["g"] + 4 * part + 2, copies_g2(part, 0))
            arrived(w.at[up, at], g_sem.at[part, 1])
            start(bases["g"] + 4 * part + 3, copies_g2(part, 1))

    def passed_on(part):
        at = parts[part]
        if nd == 4:
            arrived(w.at[across, at, 0:half], g_sem.at[part, 2])
            arrived(w.at[across, at, half:feat], g_sem.at[part, 3])

    others = sorted(range(1, nm), key=lambda k: abs(k - nm // 2))

    def copies_s(lanes):
        for k in others:
            there = {"dp": d, "mp": lax.rem(m + k, nm)}
            yield send_s.at[:, 0:lanes], recv_s.at[m, :, 0:lanes], s_sem.at[m], there, None

    def copies_t():
        for k in range(1, nd):
            to = lax.rem(home + k, nd) * ratio + mine
            part = send_s.at[:, front:]
            yield part, recv_t.at[home], t_sem.at[home], {"dp": d, "mp": to}, None

    def copies_u():
        for k in range(1, ratio):
            to = home * ratio + lax.rem(mine + k, ratio)
            yield send_u, recv_u.at[mine], u_sem.at[mine], {"dp": d, "mp": to}, None

    def copies_m_first(p):
        for k in far_first:
            i = lax.rem(d + k, nd)
            for j in (2 * p, 2 * p + 1):
                there = {"dp": i, "mp": d * ratio + j}
                same = m == d * ratio + j if k == 0 else None
                block = send_m.at[j * nd + i]
                yield block, recv_m.at[m], m_sem.at[m], there, same

    def copies_m_later(k, p):
        i = lax.rem(home + k, nd)
        for j in (2 * p, 2 * p + 1):
            to = i * ratio + j
            same = to == m if k == 0 else None
            yield send_m.at[to], recv_m.at[m], m_sem.at[m], {"dp": d, "mp": to}, same

    def copies_b_first():
        for k in range(nm):
            i = lax.rem(m + nm // 2 + k, nm)
            slot = mine * nd + d
            there = {"dp": home, "mp": i}
            same = on_home if k == nm // 2 else None
            yield send_b, recv_b.at[slot], b_sem.at[slot], there, same

    def copies_b_later():
        for k in others:
            there = {"dp": d, "mp": lax.rem(m + k, nm)}
            yield send_b, recv_b.at[m], b_sem.at[m], there, None

    def copies_c():
        for k in far_first:
            i = lax.rem(d + k, nd)
            there = {"dp": i, "mp": m, "section": after}
            yield send_c.at[i], recv_c.at[d], c_sem.at[d], there, None

    def copies_h(src):
        yield src, recv_h, h_sem.at[0], {"dp": d, "mp": m, "section": after}, None

    def copies_o():
        for k in range(1, nd):
            i = lax.rem(d + k, nd)
            yield send_c.at[i], recv_o.at[d], o_sem.at[d], {"dp": i, "mp": m}, None

    def remote(at, src, dst, recv, where):
        return pltpu.make_async_remote_copy(
            src_ref=src,
            dst_ref=dst,
            send_sem=send_sem.at[at],
            recv_sem=recv,
            device_id=where,
            device_id_type=pl.DeviceIdType.MESH,
        )

    def start(base, items):
        for n, (src, dst, recv, where, same) in enumerate(items):
            copy = remote(base + n, src, dst, recv, where)
            if same is None:
                copy.start()
            else:

                @pl.when(jnp.logical_not(same))
                def _():
                    copy.start()

                @pl.when(same)
                def _():
                    pltpu.make_async_copy(src, dst, recv).start()

    def finish(base, items):
        for n, (src, dst, recv, where, same) in enumerate(items):
            copy = remote(base + n, src, dst, recv, where)
            if same is None:
                copy.wait_send()
            else:

                @pl.when(jnp.logical_not(same))
                def _():
                    copy.wait_send()

    def arrived(ref, sem):
        pltpu.make_async_copy(ref, ref, sem).wait()

    loads[0].wait()

    @pl.when(first)
    def _():
        start(bases["x"], copies_x())

    loads[2].wait()
    group_w = wg.shape[2]
    wg[d] = jnp.zeros((feat, group_w), BF16)
    wg[d, :, 0:per_dp] = wb[...]
    start(bases["w"], copies_w())
    loads[3].wait()

    @pl.when(later)
    def _():
        start(bases["g"], copies_g(0))

    col = iota(perm.shape, 1)
    row = iota(perm.shape, 0)
    group = row // group_w
    inside = row - group * group_w
    source = group * per_dp + inside
    target = jnp.where(source < side, source + front, source - side)
    perm[...] = jnp.where((inside < per_dp) & (col == target), 1.0, 0.0).astype(BF16)
    lane_of = iota((LANES, chan), 1) // head
    expand[...] = jnp.where(
        iota((LANES, chan), 0) == m * heads_dev + lane_of, 1.0, 0.0
    ).astype(BF16)
    wide_b[...] = jnp.zeros_like(wide_b)
    wide_c[...] = jnp.zeros_like(wide_c)
    outer_l[...] = jnp.zeros_like(outer_l)
    loads[1].wait()
    offset = m * feat
    base = offset // LANES
    gain_w = gain[:, pl.ds(pl.multiple_of(base * LANES, LANES), two)]
    gain_w = jnp.broadcast_to(gain_w, (8, two))
    gain_w = pltpu.roll(gain_w, lax.rem(two - (offset - base * LANES), two), 1)
    gain_row = gain_w[0:1, 0:feat]

    def prepare():
        for copy in loads[4:9] + loads[10:]:
            copy.wait()
        tap = iota((3, 1), 0)
        taps_x = cxw[0:3, :]
        taps_b = cbw[0:3, :]

        def one(s, carry):
            slot = jnp.clip(slot_s[s] - d * slots_dev, 0, slots_dev - 1)
            seen = (tap + len_s[s] >= 3).astype(F32)
            past_x[pl.ds(s, 1), :] = jnp.sum(
                cxp[slot].astype(F32) * seen * taps_x, axis=0, keepdims=True
            )
            past_b[pl.ds(s, 1), :] = jnp.sum(
                cbp[slot].astype(F32) * seen * taps_b, axis=0, keepdims=True
            )
            alive[pl.ds(s, 1), :] = jnp.full(
                (1, LANES), jnp.where(len_s[s] > 0, 1.0, 0.0), F32
            )
            old16[s] = st[slot].astype(BF16)
            return carry

        lax.fori_loop(0, rows, one, 0)

    def after_norm(acc, residual):
        lane = iota(acc.shape, 1)
        squares = jnp.sum(
            jnp.where((lane == feat) | (lane == feat + 1), acc, 0.0), axis=1, keepdims=True
        )
        scale = lax.rsqrt(squares / inner + EPS)
        return (residual.astype(F32) + acc[:, 0:feat] * scale).astype(BF16)

    def pack(inner_p, gate_p, even, other, shape):
        lane = iota((inner_p.shape[0], LANES), 1)
        inner_t = inner_p[:, two:window]
        gate_t = pltpu.roll(gate_p[:, two:window], gap, 1)
        for at, side, edge in (
            (even, slice(0, two), jnp.where(lane < gap, inner_t, gate_t)),
            (other, slice(window, pair), jnp.where(lane < gap, gate_t, inner_t)),
        ):
            send_m[at, :, 0:two] = inner_p[:, side].astype(BF16).reshape(*shape, two)
            send_m[at, :, two : 2 * two] = gate_p[:, side].astype(BF16).reshape(*shape, two)
            send_m[at, :, 2 * two : pair] = edge.astype(BF16).reshape(*shape, LANES)

    def with_two(out, squares, at):
        high, low = halves(squares)
        lane = iota(out.shape, 1)
        return jnp.where(lane == at, high, jnp.where(lane == at + 1, low, out))

    def two_of(acc, at):
        lane = iota(acc.shape, 1)
        return jnp.sum(
            jnp.where((lane == at) | (lane == at + 1), acc, 0.0), axis=1, keepdims=True
        )

    def weights_small():
        for k in range(1, nd):
            i = lax.rem(d + k, nd)
            arrived(wg.at[i], w_sem.at[i])
        total = mm(wg[0], perm[0:group_w, :])
        for i in range(1, nd):
            total += mm(wg[i], perm[i * group_w : (i + 1) * group_w, :])
        wsmall[...] = total.astype(BF16)

    def start_small(lanes):
        value = h[...].astype(F32)
        squares = jnp.sum(value * value, axis=1, keepdims=True)
        v = (value * gain_row).astype(BF16)
        send_s[...] = with_two(mm(v, wsmall[...]), squares, mark).astype(BF16)
        start(bases["s"], copies_s(lanes))
        pltpu.make_async_copy(
            send_s.at[:, 0:lanes], recv_s.at[m, :, 0:lanes], s_sem.at[m]
        ).start()
        return v

    @pl.when(first)
    def _():
        for k in range(1, nd):
            i = lax.rem(d + k, nd)
            arrived(recv_x.at[block_of(i)], x_sem.at[i])
        recv_x[my_rows, :] = hid[...]
        h[...] = hid[...]
        v_all = (recv_x[...].astype(F32) * gain_row).astype(BF16)
        for p in range(pairs):
            cols = slice(p * pair, (p + 1) * pair)
            e = 2 * p * nd
            pack(
                mm(v_all, w[d, 1, :, cols]),
                mm(v_all, w[d, 0, :, cols]),
                slice(e, e + nd),
                slice(e + nd, e + 2 * nd),
                (nd, rows),
            )
            start(bases["m"] + e, copies_m_first(p))
        weights_small()
        start_small(front + side)
        start(bases["h"], copies_h(h))
        prepare()

    @pl.when(later)
    def _():
        weights_small()
        prepare()
        pass_on(0)
        start(bases["g"] + 4, copies_g(1))
        passed_on(0)
        arrived(recv_h, h_sem.at[0])

        @pl.when(sec == 1)
        def _():
            acc = None
            for i in range(nd):
                arrived(recv_c.at[i], c_sem.at[i])
                part = recv_c[i].astype(F32)
                acc = part if acc is None else acc + part
            h[...] = after_norm(acc, recv_h[...])

        @pl.when(sec > 1)
        def _():
            h[...] = recv_h[...]

        v = start_small(front)
        start(bases["t"], copies_t())
        for n, k in enumerate(far_first):
            i = lax.rem(home + k, nd)
            for p in range(pairs):
                cols = slice(p * pair, (p + 1) * pair)
                e = i * ratio + 2 * p
                pack(mm(v, w[i, 1, :, cols]), mm(v, w[i, 0, :, cols]), e, e + 1, (rows,))
                start(bases["m"] + n * ratio + 2 * p, copies_m_later(k, p))
        acc = send_s[:, front:].astype(F32)
        for k in range(1, nd):
            i = lax.rem(home + k, nd)
            arrived(recv_t.at[i], t_sem.at[i])
            acc += recv_t[i].astype(F32)
        send_u[...] = acc.astype(BF16)
        start(bases["u"], copies_u())
        pass_on(1)

    loads[9].wait()
    per_head = iota((1, chan), 1) // head
    rate_row = jnp.zeros((1, chan), F32)
    bias_row = jnp.zeros((1, chan), F32)
    skip_row = jnp.zeros((1, chan), F32)
    for i in range(heads_dev):
        rate_row = jnp.where(per_head == i, rate_s[0, i], rate_row)
        bias_row = jnp.where(per_head == i, bias_s[0, i], bias_row)
        skip_row = jnp.where(per_head == i, skip_s[0, i], skip_row)

    def sum_of(ref, sem, lanes):
        acc = None
        for i in range(nm):
            arrived(ref.at[i, :, 0:lanes], sem.at[i])
            part = ref[i, :, 0:lanes].astype(F32)
            acc = part if acc is None else acc + part
        return acc

    @pl.when(first)
    def _():
        acc = sum_of(recv_s, s_sem, front + side)
        acc_s[...] = acc[:, 0:front]
        acc_b[...] = acc[:, front:]

    @pl.when(later)
    def _():
        acc_s[...] = sum_of(recv_s, s_sem, front)

    acc = acc_s[...]
    scale = lax.rsqrt(two_of(acc, mark) / width + EPS)
    c_cur = silu(past_b[:, side:] + acc[:, 0:side] * scale * cbw[3:4, side:])
    c_high, c_low = halves(c_cur)
    c_two = jnp.concatenate([c_high, c_low], axis=0).astype(BF16)
    c_row = lax.rem(iota((2 * rows, 1), 0), rows)

    def ask(s, carry):
        return carry + mm_t(jnp.where(c_row == s, c_two, jnp.zeros_like(c_two)), old16[s])

    both = lax.fori_loop(
        0, rows, ask, jnp.zeros((2 * rows, chan), F32), unroll=True
    )
    read = both[0:rows] + both[rows:]
    high, low = halves(acc[:, side:])
    raw = mm(high.astype(BF16), expand[...]) + mm(low.astype(BF16), expand[...])
    step = softplus(raw * scale + bias_row)
    decay = jnp.exp(-step * rate_row) * alive[:, 0:1]

    @pl.when(first)
    def _():
        acc_m[...] = sum_of(recv_m, m_sem, pair)

    @pl.when(later)
    def _():
        acc = send_u[...].astype(F32)
        for k in range(1, ratio):
            i = lax.rem(mine + k, ratio)
            arrived(recv_u.at[i], u_sem.at[i])
            acc += recv_u[i].astype(F32)
        acc_b[...] = acc
        acc_m[...] = sum_of(recv_m, m_sem, pair)

    b_cur = silu(past_b[:, 0:side] + acc_b[...] * scale * cbw[3:4, 0:side])
    bc_dot = jnp.sum(b_cur * c_cur, axis=1, keepdims=True)
    acc = acc_m[...]
    tile = acc[:, 2 * two :]
    other = pltpu.roll(tile, gap, 1)

    def in_order(part, edge):
        before = jnp.concatenate([edge, part], axis=1)
        behind = jnp.concatenate([part, edge], axis=1)
        return jnp.where(odd, pltpu.roll(before, chan, 1), behind)[:, 0:chan]

    acc_i = in_order(acc[:, 0:two], tile)
    acc_g = in_order(acc[:, two : 2 * two], other)
    x = silu(past_x[...] + acc_i * scale * cxw[3:4, :])
    sx = step * x
    gated = (decay * read + sx * bc_dot + skip_row * x) * silu(acc_g * scale)
    squares = jnp.sum(gated * gated, axis=1, keepdims=True)
    wide_b[:, 0:chan] = gated * gg[...]
    full = wide_b[...]
    high, low = halves(squares)
    lane = iota(full.shape, 1)
    full = jnp.where(lane == chan, high, jnp.where(lane == chan + 1, low, full))
    full = jnp.where(odd, pltpu.roll(full, window - chan, 1), full)
    send_b[...] = full.astype(BF16)

    @pl.when(first)
    def _():
        start(bases["b"], copies_b_first())

    @pl.when(later)
    def _():
        start(bases["b"], copies_b_later())
        pltpu.make_async_copy(send_b, recv_b.at[m], b_sem.at[m]).start()

    s_high, s_low = halves(sx)
    d_high, d_low = halves(decay)
    b_high, b_low = halves(b_cur)
    outer_l[0:rows, 0:chan] = s_high
    outer_l[rows : 2 * rows, 0:chan] = s_high
    outer_l[2 * rows : 3 * rows, 0:chan] = s_low
    outer_l[3 * rows : 4 * rows, 0:chan] = d_high
    outer_l[4 * rows : 5 * rows, 0:chan] = d_low
    outer_t[...] = jnp.transpose(outer_l[...])[0:chan, :].astype(BF16)
    zero = jnp.zeros((rows, LANES), F32)
    one_ = jnp.ones((rows, LANES), F32)
    right = jnp.concatenate(
        [
            jnp.concatenate([b_high, b_low, b_high, zero, zero], axis=0),
            jnp.concatenate([zero, zero, zero, one_, one_], axis=0),
        ],
        axis=1,
    )
    right = jnp.concatenate(
        [right, jnp.zeros((LANES - 5 * rows, two), F32)], axis=0
    ).astype(BF16)
    r_row = lax.rem(iota((LANES, 1), 0), rows)

    def update(s, carry):
        slot = jnp.clip(slot_s[s] - d * slots_dev, 0, slots_dev - 1)
        both = mm(outer_t[...], jnp.where(r_row == s, right, jnp.zeros_like(right)))
        st_o[s] = both[:, LANES:] * st[slot] + both[:, 0:LANES]
        return carry

    before = jnp.where(more, rows // 2, rows)
    lax.fori_loop(0, before, update, 0)

    def gathered(even_s, other_s, count):
        n = count * rows
        lane = iota((n, LANES), 1)
        even_t = recv_b[even_s, :, two:window].astype(F32).reshape(n, LANES)
        odd_t = recv_b[other_s, :, 0:LANES].astype(F32).reshape(n, LANES)
        squares = jnp.sum(
            jnp.where((lane == gap) | (lane == gap + 1), even_t, 0.0)
            + jnp.where(lane < 2, odd_t, 0.0),
            axis=1,
            keepdims=True,
        )
        middle = jnp.where(lane < gap, even_t, odd_t).astype(BF16)
        left = recv_b[even_s, :, 0:two].reshape(n, two)
        right = recv_b[other_s, :, LANES:window].reshape(n, two)
        return jnp.concatenate([left, middle, right], axis=1), squares

    def with_squares(out, squares, n):
        wide_c[0:n, 0:feat] = out
        full = wide_c[0:n, :]
        high, low = halves(squares)
        lane = iota(full.shape, 1)
        return jnp.where(lane == feat, high, jnp.where(lane == feat + 1, low, full))

    @pl.when(first)
    def _():
        out = jnp.zeros((all_rows, feat), F32)
        squares = jnp.zeros((all_rows, 1), F32)
        for p in range(pairs):
            e = 2 * p * nd
            for i in range(2 * nd):
                arrived(recv_b.at[e + i], b_sem.at[e + i])
            lhs, part = gathered(slice(e, e + nd), slice(e + nd, e + 2 * nd), nd)
            squares += part
            out += mm_t(lhs, w[d, 2, :, p * pair : (p + 1) * pair])
        full = with_squares(out, squares, all_rows)
        send_c[...] = full.astype(BF16).reshape(nd, rows, two)
        start(bases["c"], copies_c())
        start(bases["o"], copies_o())
        recv_o[d] = send_c[d]

    @pl.when(later)
    def _():
        passed_on(1)
        out = jnp.zeros((rows, feat), F32)
        squares = jnp.zeros((rows, 1), F32)
        for i in range(nd):
            for p in range(pairs):
                e = i * ratio + 2 * p
                arrived(recv_b.at[e], b_sem.at[e])
                arrived(recv_b.at[e + 1], b_sem.at[e + 1])
                lhs, part = gathered(e, e + 1, 1)
                squares += part
                out += mm_t(lhs, w[i, 2, :, p * pair : (p + 1) * pair])
        hid_new[...] = after_norm(with_squares(out, squares, rows), h[...])

        @pl.when(more)
        def _():
            start(bases["h"], copies_h(hid_new))

    lax.fori_loop(before, rows, update, 0)

    @pl.when(first)
    def _():
        for k in range(1, nd):
            i = lax.rem(d + k, nd)
            arrived(recv_o.at[i], o_sem.at[i])
        acc = recv_o[0].astype(F32)
        for i in range(1, nd):
            acc += recv_o[i].astype(F32)
        hid_new[...] = after_norm(acc, h[...])

    hid_o[...] = hid_new[...]

    finish(bases["w"], copies_w())

    @pl.when(first)
    def _():
        finish(bases["x"], copies_x())
        finish(bases["s"], copies_s(front + side))
        for p in range(pairs):
            finish(bases["m"] + 2 * p * nd, copies_m_first(p))
        finish(bases["h"], copies_h(h))
        finish(bases["b"], copies_b_first())
        finish(bases["c"], copies_c())
        finish(bases["o"], copies_o())

    @pl.when(later)
    def _():
        finish(bases["s"], copies_s(front))
        finish(bases["t"], copies_t())
        finish(bases["u"], copies_u())
        for part in (0, 1):
            finish(bases["g"] + 4 * part, copies_g(part))
            if nd == 4:
                finish(bases["g"] + 4 * part + 2, copies_g2(part, 0))
                finish(bases["g"] + 4 * part + 3, copies_g2(part, 1))
        for n, k in enumerate(far_first):
            for p in range(pairs):
                finish(bases["m"] + n * ratio + 2 * p, copies_m_later(k, p))
        finish(bases["b"], copies_b_later())

        @pl.when(more)
        def _():
            finish(bases["h"], copies_h(hid_new))


def store(parts, hid_v, st_v, hid_o, st_o, sem):
    n = st_v.shape[0] // parts
    copies = [pltpu.make_async_copy(hid_v, hid_o, sem.at[parts])] + [
        pltpu.make_async_copy(
            st_v.at[i * n : (i + 1) * n], st_o.at[i * n : (i + 1) * n], sem.at[i]
        )
        for i in range(parts)
    ]
    for copy in copies:
        copy.start()
    for copy in copies:
        copy.wait()


def local(
    hidden_in,
    lengths,
    slots,
    norm_gain,
    w_zxo,
    w_bcdt,
    conv_x_weight,
    conv_bc_weight,
    conv_x_pool,
    conv_bc_pool,
    state_pool,
    a_rate,
    dt_bias,
    skip_gain,
    gate_gain,
):
    nd, nm, ns = (lax.axis_size(name) for name in ("dp", "mp", "section"))
    rows, feat = hidden_in.shape
    width = norm_gain.shape[1]
    chan_dp = w_zxo.shape[2]
    per_dp = w_bcdt.shape[1]
    slots_dev, heads_dev, head, state = state_pool.shape[1:]
    chan = heads_dev * head
    bcw = conv_bc_weight.shape[2]
    small = per_dp * nd
    small_pad = -(-(small - bcw // 2 + 2) // LANES) * LANES + bcw // 2
    group_w = -(-per_dp // LANES) * LANES
    ratio = nm // nd
    all_rows = nd * rows
    window = 3 * LANES
    size = (
        nd, nm, ns, rows, feat, chan, head, small, bcw, slots_dev, width, chan * nm,
    )
    operands = (
        lengths,
        slots,
        a_rate,
        dt_bias,
        skip_gain,
        hidden_in,
        norm_gain,
        jnp.swapaxes(w_zxo[0], 1, 2),
        jnp.swapaxes(w_bcdt[0], 0, 1),
        conv_x_weight[0],
        conv_bc_weight[0],
        conv_x_pool[0],
        conv_bc_pool[0],
        state_pool.reshape(slots_dev, chan, state),
        gate_gain,
    )
    sends = 5 * nd + ratio + 3 * nm + 4
    dma = pltpu.SemaphoreType.DMA
    scratch = (
        [pltpu.SMEM(a.shape, a.dtype) for a in operands[:5]]
        + [
            pltpu.VMEM((nd, *a.shape) if i == 7 else a.shape, a.dtype)
            for i, a in enumerate(operands)
            if i >= 5
        ]
        + [
            pltpu.VMEM((nd, feat, group_w), BF16),
            pltpu.VMEM((nd * group_w, small_pad), BF16),
            pltpu.VMEM((feat, small_pad), BF16),
            pltpu.VMEM((rows, feat), BF16),
            pltpu.VMEM((rows, chan), F32),
            pltpu.VMEM((rows, bcw), F32),
            pltpu.VMEM((rows, LANES), F32),
            pltpu.VMEM((LANES, chan), BF16),
            pltpu.VMEM((rows, chan, state), BF16),
            pltpu.VMEM((rows, window), F32),
            pltpu.VMEM((all_rows, 2 * LANES), F32),
            pltpu.VMEM((LANES, window), F32),
            pltpu.VMEM((chan, LANES), BF16),
            pltpu.VMEM((rows, feat), BF16),
            pltpu.VMEM((rows, small_pad - bcw // 2), F32),
            pltpu.VMEM((rows, bcw // 2), F32),
            pltpu.VMEM((rows, 2 * chan), F32),
        ]
        + [
            pltpu.VMEM((rows, small_pad), BF16),
            pltpu.VMEM((rows, bcw // 2), BF16),
            pltpu.VMEM((nm, rows, 2 * chan), BF16),
            pltpu.VMEM((rows, window), BF16),
            pltpu.VMEM((nd, rows, 2 * LANES), BF16),
        ]
        + [
            pltpu.VMEM((all_rows, feat), BF16),
            pltpu.VMEM((nm, rows, small_pad), BF16),
            pltpu.VMEM((nd, rows, bcw // 2), BF16),
            pltpu.VMEM((ratio, rows, bcw // 2), BF16),
            pltpu.VMEM((nm, rows, 2 * chan), BF16),
            pltpu.VMEM((nm, rows, window), BF16),
            pltpu.VMEM((nd, rows, 2 * LANES), BF16),
            pltpu.VMEM((rows, feat), BF16),
            pltpu.VMEM((nd, rows, 2 * LANES), BF16),
        ]
        + [
            dma((15,)),
            dma((sends,)),
            dma((nd,)),
            dma((nd,)),
            dma((2, 4)),
            dma((nm,)),
            dma((nd,)),
            dma((ratio,)),
            dma((nm,)),
            dma((nd * ratio,)),
            dma((nd,)),
            dma((1,)),
            dma((nd,)),
        ]
    )
    inside = pl.pallas_call(
        functools.partial(kernel, size),
        out_shape=(
            jax.ShapeDtypeStruct((rows, feat), BF16),
            jax.ShapeDtypeStruct((rows, chan, state), F32),
        ),
        in_specs=[pl.BlockSpec(memory_space=pltpu.HBM)] * 5
        + [pl.BlockSpec(memory_space=pltpu.HBM)] * 10,
        out_specs=(
            pl.BlockSpec(memory_space=pltpu.VMEM),
            pl.BlockSpec(memory_space=pltpu.VMEM),
        ),
        scratch_shapes=scratch,
        compiler_params=pltpu.CompilerParams(
            collective_id=0, has_side_effects=True, vmem_limit_bytes=48 << 20
        ),
    )(*[pltpu.with_memory_space_constraint(a, pltpu.HBM) for a in operands])
    hidden, states = pl.pallas_call(
        functools.partial(store, rows // 2),
        out_shape=(
            jax.ShapeDtypeStruct((rows, feat), BF16),
            jax.ShapeDtypeStruct((rows, chan, state), F32),
        ),
        in_specs=[pl.BlockSpec(memory_space=pltpu.VMEM)] * 2,
        out_specs=(pl.BlockSpec(memory_space=pltpu.HBM),) * 2,
        scratch_shapes=[dma((1 + rows // 2,))],
        compiler_params=pltpu.CompilerParams(vmem_limit_bytes=8 << 20),
    )(*inside)
    return (
        hidden[None],
        states.reshape(1, rows, heads_dev, head, state),
    )


def solution(mesh):
    placed = (
        P("dp", "mp"),
        P("dp"),
        P("dp"),
        P("section", None),
        P("section", None, "dp", "mp"),
        P("section", "dp", "mp"),
        P("section", None, "mp"),
        P("section", None, None),
        P("section", "dp", None, "mp"),
        P("section", "dp", None, None),
        P("section", "dp", "mp", None, None),
        P("section", "mp"),
        P("section", "mp"),
        P("section", "mp"),
        P("section", "mp"),
    )
    return jax.shard_map(
        local,
        mesh=mesh,
        in_specs=placed,
        out_specs=(P("section", "dp", "mp"), P("section", "dp", "mp", None, None)),
        check_vma=False,
    )
```

```python
import functools

import jax
import jax.numpy as jnp
from jax import lax
from jax.experimental import pallas as pl
from jax.experimental.pallas import tpu as pltpu
from jax.sharding import PartitionSpec as P

EPS = 1e-05
F32 = jnp.float32
BF16 = jnp.bfloat16
LANES = 128


def silu(v):
    return v * (1.0 / (1.0 + jnp.exp(-v)))


def softplus(v):
    return jnp.maximum(v, 0.0) + jnp.log1p(jnp.exp(-jnp.abs(v)))


def halves(v):
    top = v.astype(BF16).astype(F32)
    return top, v - top


def iota(shape, dim):
    return lax.broadcasted_iota(jnp.int32, shape, dim)


def mm(a, b):
    return lax.dot_general(a, b, (((1,), (0,)), ((), ())), preferred_element_type=F32)


def mm_t(a, b):
    return lax.dot_general(a, b, (((1,), (1,)), ((), ())), preferred_element_type=F32)


def kernel(
    size,
    len_h,
    slot_h,
    rate_h,
    bias_h,
    skip_h,
    hid_h,
    gain_h,
    w_h,
    wb_h,
    cxw_h,
    cbw_h,
    cxp_h,
    cbp_h,
    st_h,
    gg_h,
    hid_o,
    st_o,
    len_s,
    slot_s,
    rate_s,
    bias_s,
    skip_s,
    hid,
    gain,
    w,
    wb,
    cxw,
    cbw,
    cxp,
    cbp,
    st,
    gg,
    wg,
    perm,
    wsmall,
    h,
    past_x,
    past_b,
    alive,
    expand,
    old16,
    wide_b,
    wide_c,
    outer_l,
    outer_t,
    hid_new,
    acc_s,
    acc_b,
    acc_m,
    send_s,
    send_u,
    send_m,
    send_b,
    send_c,
    recv_x,
    recv_s,
    recv_t,
    recv_u,
    recv_m,
    recv_b,
    recv_c,
    recv_h,
    recv_o,
    load_sem,
    send_sem,
    x_sem,
    w_sem,
    g_sem,
    s_sem,
    t_sem,
    u_sem,
    m_sem,
    b_sem,
    c_sem,
    h_sem,
    o_sem,
):
    nd, nm, ns, rows, feat, chan, head, small, bcw, slots_dev, width, inner = size
    ratio = nm // nd
    pairs = ratio // 2
    pair = 2 * chan
    two = 2 * LANES
    gap = chan - two
    window = 3 * LANES
    half = feat // 2
    side = bcw // 2
    front = wsmall.shape[1] - side
    mark = small - side
    d = lax.axis_index("dp")
    m = lax.axis_index("mp")
    sec = lax.axis_index("section")
    home = m // ratio
    mine = lax.rem(m, ratio)
    odd = lax.rem(mine, 2) == 1
    on_home = home == d
    per_dp = small // nd
    all_rows = nd * rows
    heads_dev = chan // head
    first = sec == 0
    later = sec > 0
    more = sec < ns - 1
    after = jnp.minimum(sec + 1, ns - 1)
    my_rows = pl.ds(pl.multiple_of(d * rows, rows), rows)
    far_first = (2, 1, 3, 0) if nd == 4 else tuple(range(nd))

    srcs = (
        (hid_h, hid),
        (gain_h, gain),
        (wb_h, wb),
        (w_h, w.at[d]),
        (cxw_h, cxw),
        (cbw_h, cbw),
        (cxp_h, cxp),
        (cbp_h, cbp),
        (st_h, st),
        (gg_h, gg),
        (len_h, len_s),
        (slot_h, slot_s),
        (rate_h, rate_s),
        (bias_h, bias_s),
        (skip_h, skip_s),
    )
    loads = [
        pltpu.make_async_copy(src, dst, load_sem.at[i]) for i, (src, dst) in enumerate(srcs)
    ]
    loads[0].start()
    loads[2].start()

    barrier = pltpu.get_barrier_semaphore()

    def tell(dp, mp, section=None):
        where = {"dp": dp, "mp": mp}
        if section is not None:
            where["section"] = section
        pl.semaphore_signal(
            barrier, inc=1, device_id=where, device_id_type=pl.DeviceIdType.MESH
        )

    for k in range(1, nd):
        tell(lax.rem(d + k, nd), m)
    for k in range(1, nm):
        tell(d, lax.rem(m + k, nm))

    @pl.when(first)
    def _():
        for i in range(nm):

            @pl.when(jnp.logical_not(on_home & (m == i)))
            def _():
                tell(home, i)

        for i in range(nd):
            for j in range(ratio):

                @pl.when(jnp.logical_not((d == i) & (m == d * ratio + j)))
                def _():
                    tell(i, d * ratio + j)

    @pl.when(sec == 1)
    def _():
        for k in range(nd):
            tell(k, m, 0)

    @pl.when(sec > 1)
    def _():
        tell(d, m, sec - 1)

    loads[3].start()
    for i in (1, *range(4, len(loads))):
        loads[i].start()

    own = jnp.where(on_home, 1, 0)
    pl.semaphore_wait(
        barrier,
        nd
        - 1
        + nm
        - 1
        + jnp.where(first, 2 * (nm - own) + nd, jnp.where(more, 1, 0)),
    )

    count = 0
    bases = {}
    for name, n in (
        ("x", nd - 1),
        ("w", nd - 1),
        ("g", 12),
        ("s", nm),
        ("m", nm),
        ("b", nm),
        ("c", nd),
        ("h", 1),
        ("o", nd - 1),
        ("t", nd - 1),
        ("u", ratio - 1),
    ):
        bases[name] = count
        count += n

    def block_of(i):
        return pl.ds(pl.multiple_of(i * rows, rows), rows)

    def copies_x():
        for k in range(1, nd):
            there = {"dp": lax.rem(d + k, nd), "mp": m}
            yield hid, recv_x.at[my_rows], x_sem.at[d], there, None

    def copies_w():
        for k in range(1, nd):
            there = {"dp": lax.rem(d + k, nd), "mp": m}
            yield wg.at[d], wg.at[d], w_sem.at[d], there, None

    up = lax.rem(d + 1, nd)
    down = lax.rem(d + nd - 1, nd)
    across = lax.rem(d + 2, nd)

    parts = (slice(1, 2), slice(0, 1), slice(2, 3))

    def copies_g(part):
        at = parts[part]
        yield w.at[d, at], w.at[d, at], g_sem.at[part, 0], {"dp": up, "mp": m}, None
        if nd == 4:
            yield w.at[d, at], w.at[d, at], g_sem.at[part, 1], {"dp": down, "mp": m}, None

    def copies_g2(part, which):
        at = parts[part]
        if which == 0:
            block = w.at[down, at, 0:half]
            yield block, block, g_sem.at[part, 2], {"dp": up, "mp": m}, None
        else:
            block = w.at[up, at, half:feat]
            yield block, block, g_sem.at[part, 3], {"dp": down, "mp": m}, None

    def pass_on(part):
        at = parts[part]
        arrived(w.at[down, at], g_sem.at[part, 0])
        if nd == 4:
            start(bases["g"] + 4 * part + 2, copies_g2(part, 0))
            arrived(w.at[up, at], g_sem.at[part, 1])
            start(bases["g"] + 4 * part + 3, copies_g2(part, 1))

    def passed_on(part):
        at = parts[part]
        if nd == 4:
            arrived(w.at[across, at, 0:half], g_sem.at[part, 2])
            arrived(w.at[across, at, half:feat], g_sem.at[part, 3])

    others = sorted(range(1, nm), key=lambda k: abs(k - nm // 2))

    def copies_s(lanes):
        for k in others:
            there = {"dp": d, "mp": lax.rem(m + k, nm)}
            yield send_s.at[:, 0:lanes], recv_s.at[m, :, 0:lanes], s_sem.at[m], there, None

    def copies_t():
        for k in range(1, nd):
            to = lax.rem(home + k, nd) * ratio + mine
            part = send_s.at[:, front:]
            yield part, recv_t.at[home], t_sem.at[home], {"dp": d, "mp": to}, None

    def copies_u():
        for k in range(1, ratio):
            to = home * ratio + lax.rem(mine + k, ratio)
            yield send_u, recv_u.at[mine], u_sem.at[mine], {"dp": d, "mp": to}, None

    def copies_m_first(p):
        for k in far_first:
            i = lax.rem(d + k, nd)
            for j in (2 * p, 2 * p + 1):
                there = {"dp": i, "mp": d * ratio + j}
                same = m == d * ratio + j if k == 0 else None
                block = send_m.at[j * nd + i]
                yield block, recv_m.at[m], m_sem.at[m], there, same

    def copies_m_later(k, p):
        i = lax.rem(home + k, nd)
        for j in (2 * p, 2 * p + 1):
            to = i * ratio + j
            same = to == m if k == 0 else None
            yield send_m.at[to], recv_m.at[m], m_sem.at[m], {"dp": d, "mp": to}, same

    def copies_b_first():
        for k in range(nm):
            i = lax.rem(m + nm // 2 + k, nm)
            slot = mine * nd + d
            there = {"dp": home, "mp": i}
            same = on_home if k == nm // 2 else None
            yield send_b, recv_b.at[slot], b_sem.at[slot], there, same

    def copies_b_later():
        for k in others:
            there = {"dp": d, "mp": lax.rem(m + k, nm)}
            yield send_b, recv_b.at[m], b_sem.at[m], there, None

    def copies_c():
        for k in far_first:
            i = lax.rem(d + k, nd)
            there = {"dp": i, "mp": m, "section": after}
            yield send_c.at[i], recv_c.at[d], c_sem.at[d], there, None

    def copies_h(src):
        yield src, recv_h, h_sem.at[0], {"dp": d, "mp": m, "section": after}, None

    def copies_o():
        for k in range(1, nd):
            i = lax.rem(d + k, nd)
            yield send_c.at[i], recv_o.at[d], o_sem.at[d], {"dp": i, "mp": m}, None

    def remote(at, src, dst, recv, where):
        return pltpu.make_async_remote_copy(
            src_ref=src,
            dst_ref=dst,
            send_sem=send_sem.at[at],
            recv_sem=recv,
            device_id=where,
            device_id_type=pl.DeviceIdType.MESH,
        )

    def start(base, items):
        for n, (src, dst, recv, where, same) in enumerate(items):
            copy = remote(base + n, src, dst, recv, where)
            if same is None:
                copy.start()
            else:

                @pl.when(jnp.logical_not(same))
                def _():
                    copy.start()

                @pl.when(same)
                def _():
                    pltpu.make_async_copy(src, dst, recv).start()

    def finish(base, items):
        for n, (src, dst, recv, where, same) in enumerate(items):
            copy = remote(base + n, src, dst, recv, where)
            if same is None:
                copy.wait_send()
            else:

                @pl.when(jnp.logical_not(same))
                def _():
                    copy.wait_send()

    def arrived(ref, sem):
        pltpu.make_async_copy(ref, ref, sem).wait()

    loads[0].wait()

    @pl.when(first)
    def _():
        start(bases["x"], copies_x())

    loads[2].wait()
    group_w = wg.shape[2]
    wg[d] = jnp.zeros((feat, group_w), BF16)
    wg[d, :, 0:per_dp] = wb[...]
    start(bases["w"], copies_w())
    loads[3].wait()

    @pl.when(later)
    def _():
        start(bases["g"], copies_g(0))
        start(bases["g"] + 4, copies_g(1))

    col = iota(perm.shape, 1)
    row = iota(perm.shape, 0)
    group = row // group_w
    inside = row - group * group_w
    source = group * per_dp + inside
    target = jnp.where(source < side, source + front, source - side)
    perm[...] = jnp.where((inside < per_dp) & (col == target), 1.0, 0.0).astype(BF16)
    lane_of = iota((LANES, chan), 1) // head
    expand[...] = jnp.where(
        iota((LANES, chan), 0) == m * heads_dev + lane_of, 1.0, 0.0
    ).astype(BF16)
    wide_b[...] = jnp.zeros_like(wide_b)
    wide_c[...] = jnp.zeros_like(wide_c)
    outer_l[...] = jnp.zeros_like(outer_l)
    loads[1].wait()
    offset = m * feat
    base = offset // LANES
    gain_w = gain[:, pl.ds(pl.multiple_of(base * LANES, LANES), two)]
    gain_w = jnp.broadcast_to(gain_w, (8, two))
    gain_w = pltpu.roll(gain_w, lax.rem(two - (offset - base * LANES), two), 1)
    gain_row = gain_w[0:1, 0:feat]

    def prepare():
        for copy in loads[4:9] + loads[10:]:
            copy.wait()
        tap = iota((3, 1), 0)
        taps_x = cxw[0:3, :]
        taps_b = cbw[0:3, :]

        def one(s, carry):
            slot = jnp.clip(slot_s[s] - d * slots_dev, 0, slots_dev - 1)
            seen = (tap + len_s[s] >= 3).astype(F32)
            past_x[pl.ds(s, 1), :] = jnp.sum(
                cxp[slot].astype(F32) * seen * taps_x, axis=0, keepdims=True
            )
            past_b[pl.ds(s, 1), :] = jnp.sum(
                cbp[slot].astype(F32) * seen * taps_b, axis=0, keepdims=True
            )
            alive[pl.ds(s, 1), :] = jnp.full(
                (1, LANES), jnp.where(len_s[s] > 0, 1.0, 0.0), F32
            )
            old16[s] = st[slot].astype(BF16)
            return carry

        lax.fori_loop(0, rows, one, 0)

    def after_norm(acc, residual):
        lane = iota(acc.shape, 1)
        squares = jnp.sum(
            jnp.where((lane == feat) | (lane == feat + 1), acc, 0.0), axis=1, keepdims=True
        )
        scale = lax.rsqrt(squares / inner + EPS)
        return (residual.astype(F32) + acc[:, 0:feat] * scale).astype(BF16)

    def pack(inner_p, gate_p, even, other, shape):
        lane = iota((inner_p.shape[0], LANES), 1)
        inner_t = inner_p[:, two:window]
        gate_t = pltpu.roll(gate_p[:, two:window], gap, 1)
        for at, side, edge in (
            (even, slice(0, two), jnp.where(lane < gap, inner_t, gate_t)),
            (other, slice(window, pair), jnp.where(lane < gap, gate_t, inner_t)),
        ):
            send_m[at, :, 0:two] = inner_p[:, side].astype(BF16).reshape(*shape, two)
            send_m[at, :, two : 2 * two] = gate_p[:, side].astype(BF16).reshape(*shape, two)
            send_m[at, :, 2 * two : pair] = edge.astype(BF16).reshape(*shape, LANES)

    def with_two(out, squares, at):
        high, low = halves(squares)
        lane = iota(out.shape, 1)
        return jnp.where(lane == at, high, jnp.where(lane == at + 1, low, out))

    def two_of(acc, at):
        lane = iota(acc.shape, 1)
        return jnp.sum(
            jnp.where((lane == at) | (lane == at + 1), acc, 0.0), axis=1, keepdims=True
        )

    def weights_small():
        for k in range(1, nd):
            i = lax.rem(d + k, nd)
            arrived(wg.at[i], w_sem.at[i])
        total = mm(wg[0], perm[0:group_w, :])
        for i in range(1, nd):
            total += mm(wg[i], perm[i * group_w : (i + 1) * group_w, :])
        wsmall[...] = total.astype(BF16)

    def start_small(lanes):
        value = h[...].astype(F32)
        squares = jnp.sum(value * value, axis=1, keepdims=True)
        v = (value * gain_row).astype(BF16)
        send_s[...] = with_two(mm(v, wsmall[...]), squares, mark).astype(BF16)
        start(bases["s"], copies_s(lanes))
        pltpu.make_async_copy(
            send_s.at[:, 0:lanes], recv_s.at[m, :, 0:lanes], s_sem.at[m]
        ).start()
        return v

    @pl.when(first)
    def _():
        for k in range(1, nd):
            i = lax.rem(d + k, nd)
            arrived(recv_x.at[block_of(i)], x_sem.at[i])
        recv_x[my_rows, :] = hid[...]
        h[...] = hid[...]
        v_all = (recv_x[...].astype(F32) * gain_row).astype(BF16)
        for p in range(pairs):
            cols = slice(p * pair, (p + 1) * pair)
            e = 2 * p * nd
            pack(
                mm(v_all, w[d, 1, :, cols]),
                mm(v_all, w[d, 0, :, cols]),
                slice(e, e + nd),
                slice(e + nd, e + 2 * nd),
                (nd, rows),
            )
            start(bases["m"] + e, copies_m_first(p))
        weights_small()
        start_small(front + side)
        start(bases["h"], copies_h(h))
        prepare()

    @pl.when(later)
    def _():
        weights_small()
        prepare()
        pass_on(0)
        pass_on(1)
        start(bases["g"] + 8, copies_g(2))
        passed_on(0)
        passed_on(1)
        arrived(recv_h, h_sem.at[0])

        @pl.when(sec == 1)
        def _():
            acc = None
            for i in range(nd):
                arrived(recv_c.at[i], c_sem.at[i])
                part = recv_c[i].astype(F32)
                acc = part if acc is None else acc + part
            h[...] = after_norm(acc, recv_h[...])

        @pl.when(sec > 1)
        def _():
            h[...] = recv_h[...]

        v = start_small(front)
        start(bases["t"], copies_t())
        for n, k in enumerate(far_first):
            i = lax.rem(home + k, nd)
            for p in range(pairs):
                cols = slice(p * pair, (p + 1) * pair)
                e = i * ratio + 2 * p
                pack(mm(v, w[i, 1, :, cols]), mm(v, w[i, 0, :, cols]), e, e + 1, (rows,))
                start(bases["m"] + n * ratio + 2 * p, copies_m_later(k, p))
        acc = send_s[:, front:].astype(F32)
        for k in range(1, nd):
            i = lax.rem(home + k, nd)
            arrived(recv_t.at[i], t_sem.at[i])
            acc += recv_t[i].astype(F32)
        send_u[...] = acc.astype(BF16)
        start(bases["u"], copies_u())
        pass_on(2)

    loads[9].wait()
    per_head = iota((1, chan), 1) // head
    rate_row = jnp.zeros((1, chan), F32)
    bias_row = jnp.zeros((1, chan), F32)
    skip_row = jnp.zeros((1, chan), F32)
    for i in range(heads_dev):
        rate_row = jnp.where(per_head == i, rate_s[0, i], rate_row)
        bias_row = jnp.where(per_head == i, bias_s[0, i], bias_row)
        skip_row = jnp.where(per_head == i, skip_s[0, i], skip_row)

    def sum_of(ref, sem, lanes):
        acc = None
        for i in range(nm):
            arrived(ref.at[i, :, 0:lanes], sem.at[i])
            part = ref[i, :, 0:lanes].astype(F32)
            acc = part if acc is None else acc + part
        return acc

    @pl.when(first)
    def _():
        acc = sum_of(recv_s, s_sem, front + side)
        acc_s[...] = acc[:, 0:front]
        acc_b[...] = acc[:, front:]

    @pl.when(later)
    def _():
        acc_s[...] = sum_of(recv_s, s_sem, front)

    acc = acc_s[...]
    scale = lax.rsqrt(two_of(acc, mark) / width + EPS)
    c_cur = silu(past_b[:, side:] + acc[:, 0:side] * scale * cbw[3:4, side:])
    c_high, c_low = halves(c_cur)
    c_two = jnp.concatenate([c_high, c_low], axis=0).astype(BF16)
    c_row = lax.rem(iota((2 * rows, 1), 0), rows)

    def ask(s, carry):
        return carry + mm_t(jnp.where(c_row == s, c_two, jnp.zeros_like(c_two)), old16[s])

    both = lax.fori_loop(
        0, rows, ask, jnp.zeros((2 * rows, chan), F32), unroll=True
    )
    read = both[0:rows] + both[rows:]
    high, low = halves(acc[:, side:])
    raw = mm(high.astype(BF16), expand[...]) + mm(low.astype(BF16), expand[...])
    step = softplus(raw * scale + bias_row)
    decay = jnp.exp(-step * rate_row) * alive[:, 0:1]

    @pl.when(first)
    def _():
        acc_m[...] = sum_of(recv_m, m_sem, pair)

    @pl.when(later)
    def _():
        acc = send_u[...].astype(F32)
        for k in range(1, ratio):
            i = lax.rem(mine + k, ratio)
            arrived(recv_u.at[i], u_sem.at[i])
            acc += recv_u[i].astype(F32)
        acc_b[...] = acc
        acc_m[...] = sum_of(recv_m, m_sem, pair)

    b_cur = silu(past_b[:, 0:side] + acc_b[...] * scale * cbw[3:4, 0:side])
    bc_dot = jnp.sum(b_cur * c_cur, axis=1, keepdims=True)
    acc = acc_m[...]
    tile = acc[:, 2 * two :]
    other = pltpu.roll(tile, gap, 1)

    def in_order(part, edge):
        before = jnp.concatenate([edge, part], axis=1)
        behind = jnp.concatenate([part, edge], axis=1)
        return jnp.where(odd, pltpu.roll(before, chan, 1), behind)[:, 0:chan]

    acc_i = in_order(acc[:, 0:two], tile)
    acc_g = in_order(acc[:, two : 2 * two], other)
    x = silu(past_x[...] + acc_i * scale * cxw[3:4, :])
    sx = step * x
    gated = (decay * read + sx * bc_dot + skip_row * x) * silu(acc_g * scale)
    squares = jnp.sum(gated * gated, axis=1, keepdims=True)
    wide_b[:, 0:chan] = gated * gg[...]
    full = wide_b[...]
    high, low = halves(squares)
    lane = iota(full.shape, 1)
    full = jnp.where(lane == chan, high, jnp.where(lane == chan + 1, low, full))
    full = jnp.where(odd, pltpu.roll(full, window - chan, 1), full)
    send_b[...] = full.astype(BF16)

    @pl.when(first)
    def _():
        start(bases["b"], copies_b_first())

    @pl.when(later)
    def _():
        start(bases["b"], copies_b_later())
        pltpu.make_async_copy(send_b, recv_b.at[m], b_sem.at[m]).start()

    s_high, s_low = halves(sx)
    d_high, d_low = halves(decay)
    b_high, b_low = halves(b_cur)
    outer_l[0:rows, 0:chan] = s_high
    outer_l[rows : 2 * rows, 0:chan] = s_high
    outer_l[2 * rows : 3 * rows, 0:chan] = s_low
    outer_l[3 * rows : 4 * rows, 0:chan] = d_high
    outer_l[4 * rows : 5 * rows, 0:chan] = d_low
    outer_t[...] = jnp.transpose(outer_l[...])[0:chan, :].astype(BF16)
    zero = jnp.zeros((rows, LANES), F32)
    one_ = jnp.ones((rows, LANES), F32)
    right = jnp.concatenate(
        [
            jnp.concatenate([b_high, b_low, b_high, zero, zero], axis=0),
            jnp.concatenate([zero, zero, zero, one_, one_], axis=0),
        ],
        axis=1,
    )
    right = jnp.concatenate(
        [right, jnp.zeros((LANES - 5 * rows, two), F32)], axis=0
    ).astype(BF16)
    r_row = lax.rem(iota((LANES, 1), 0), rows)

    def update(s, carry):
        slot = jnp.clip(slot_s[s] - d * slots_dev, 0, slots_dev - 1)
        both = mm(outer_t[...], jnp.where(r_row == s, right, jnp.zeros_like(right)))
        st_o[s] = both[:, LANES:] * st[slot] + both[:, 0:LANES]
        return carry

    before = jnp.where(more, rows // 2, rows)
    lax.fori_loop(0, before, update, 0)

    def gathered(even_s, other_s, count):
        n = count * rows
        lane = iota((n, LANES), 1)
        even_t = recv_b[even_s, :, two:window].astype(F32).reshape(n, LANES)
        odd_t = recv_b[other_s, :, 0:LANES].astype(F32).reshape(n, LANES)
        squares = jnp.sum(
            jnp.where((lane == gap) | (lane == gap + 1), even_t, 0.0)
            + jnp.where(lane < 2, odd_t, 0.0),
            axis=1,
            keepdims=True,
        )
        middle = jnp.where(lane < gap, even_t, odd_t).astype(BF16)
        left = recv_b[even_s, :, 0:two].reshape(n, two)
        right = recv_b[other_s, :, LANES:window].reshape(n, two)
        return jnp.concatenate([left, middle, right], axis=1), squares

    def with_squares(out, squares, n):
        wide_c[0:n, 0:feat] = out
        full = wide_c[0:n, :]
        high, low = halves(squares)
        lane = iota(full.shape, 1)
        return jnp.where(lane == feat, high, jnp.where(lane == feat + 1, low, full))

    @pl.when(first)
    def _():
        out = jnp.zeros((all_rows, feat), F32)
        squares = jnp.zeros((all_rows, 1), F32)
        for p in range(pairs):
            e = 2 * p * nd
            for i in range(2 * nd):
                arrived(recv_b.at[e + i], b_sem.at[e + i])
            lhs, part = gathered(slice(e, e + nd), slice(e + nd, e + 2 * nd), nd)
            squares += part
            out += mm_t(lhs, w[d, 2, :, p * pair : (p + 1) * pair])
        full = with_squares(out, squares, all_rows)
        send_c[...] = full.astype(BF16).reshape(nd, rows, two)
        start(bases["c"], copies_c())
        start(bases["o"], copies_o())
        recv_o[d] = send_c[d]

    @pl.when(later)
    def _():
        passed_on(2)
        out = jnp.zeros((rows, feat), F32)
        squares = jnp.zeros((rows, 1), F32)
        for i in range(nd):
            for p in range(pairs):
                e = i * ratio + 2 * p
                arrived(recv_b.at[e], b_sem.at[e])
                arrived(recv_b.at[e + 1], b_sem.at[e + 1])
                lhs, part = gathered(e, e + 1, 1)
                squares += part
                out += mm_t(lhs, w[i, 2, :, p * pair : (p + 1) * pair])
        hid_new[...] = after_norm(with_squares(out, squares, rows), h[...])

        @pl.when(more)
        def _():
            start(bases["h"], copies_h(hid_new))

    lax.fori_loop(before, rows, update, 0)

    @pl.when(first)
    def _():
        for k in range(1, nd):
            i = lax.rem(d + k, nd)
            arrived(recv_o.at[i], o_sem.at[i])
        acc = recv_o[0].astype(F32)
        for i in range(1, nd):
            acc += recv_o[i].astype(F32)
        hid_new[...] = after_norm(acc, h[...])

    hid_o[...] = hid_new[...]

    finish(bases["w"], copies_w())

    @pl.when(first)
    def _():
        finish(bases["x"], copies_x())
        finish(bases["s"], copies_s(front + side))
        for p in range(pairs):
            finish(bases["m"] + 2 * p * nd, copies_m_first(p))
        finish(bases["h"], copies_h(h))
        finish(bases["b"], copies_b_first())
        finish(bases["c"], copies_c())
        finish(bases["o"], copies_o())

    @pl.when(later)
    def _():
        finish(bases["s"], copies_s(front))
        finish(bases["t"], copies_t())
        finish(bases["u"], copies_u())
        for part in (0, 1, 2):
            finish(bases["g"] + 4 * part, copies_g(part))
            if nd == 4:
                finish(bases["g"] + 4 * part + 2, copies_g2(part, 0))
                finish(bases["g"] + 4 * part + 3, copies_g2(part, 1))
        for n, k in enumerate(far_first):
            for p in range(pairs):
                finish(bases["m"] + n * ratio + 2 * p, copies_m_later(k, p))
        finish(bases["b"], copies_b_later())

        @pl.when(more)
        def _():
            finish(bases["h"], copies_h(hid_new))


def store(parts, hid_v, st_v, hid_o, st_o, sem):
    n = st_v.shape[0] // parts
    copies = [pltpu.make_async_copy(hid_v, hid_o, sem.at[parts])] + [
        pltpu.make_async_copy(
            st_v.at[i * n : (i + 1) * n], st_o.at[i * n : (i + 1) * n], sem.at[i]
        )
        for i in range(parts)
    ]
    for copy in copies:
        copy.start()
    for copy in copies:
        copy.wait()


def local(
    hidden_in,
    lengths,
    slots,
    norm_gain,
    w_zxo,
    w_bcdt,
    conv_x_weight,
    conv_bc_weight,
    conv_x_pool,
    conv_bc_pool,
    state_pool,
    a_rate,
    dt_bias,
    skip_gain,
    gate_gain,
):
    nd, nm, ns = (lax.axis_size(name) for name in ("dp", "mp", "section"))
    rows, feat = hidden_in.shape
    width = norm_gain.shape[1]
    chan_dp = w_zxo.shape[2]
    per_dp = w_bcdt.shape[1]
    slots_dev, heads_dev, head, state = state_pool.shape[1:]
    chan = heads_dev * head
    bcw = conv_bc_weight.shape[2]
    small = per_dp * nd
    small_pad = -(-(small - bcw // 2 + 2) // LANES) * LANES + bcw // 2
    group_w = -(-per_dp // LANES) * LANES
    ratio = nm // nd
    all_rows = nd * rows
    window = 3 * LANES
    size = (
        nd, nm, ns, rows, feat, chan, head, small, bcw, slots_dev, width, chan * nm,
    )
    operands = (
        lengths,
        slots,
        a_rate,
        dt_bias,
        skip_gain,
        hidden_in,
        norm_gain,
        jnp.swapaxes(w_zxo[0], 1, 2),
        jnp.swapaxes(w_bcdt[0], 0, 1),
        conv_x_weight[0],
        conv_bc_weight[0],
        conv_x_pool[0],
        conv_bc_pool[0],
        state_pool.reshape(slots_dev, chan, state),
        gate_gain,
    )
    sends = 5 * nd + ratio + 3 * nm + 8
    dma = pltpu.SemaphoreType.DMA
    scratch = (
        [pltpu.SMEM(a.shape, a.dtype) for a in operands[:5]]
        + [
            pltpu.VMEM((nd, *a.shape) if i == 7 else a.shape, a.dtype)
            for i, a in enumerate(operands)
            if i >= 5
        ]
        + [
            pltpu.VMEM((nd, feat, group_w), BF16),
            pltpu.VMEM((nd * group_w, small_pad), BF16),
            pltpu.VMEM((feat, small_pad), BF16),
            pltpu.VMEM((rows, feat), BF16),
            pltpu.VMEM((rows, chan), F32),
            pltpu.VMEM((rows, bcw), F32),
            pltpu.VMEM((rows, LANES), F32),
            pltpu.VMEM((LANES, chan), BF16),
            pltpu.VMEM((rows, chan, state), BF16),
            pltpu.VMEM((rows, window), F32),
            pltpu.VMEM((all_rows, 2 * LANES), F32),
            pltpu.VMEM((LANES, window), F32),
            pltpu.VMEM((chan, LANES), BF16),
            pltpu.VMEM((rows, feat), BF16),
            pltpu.VMEM((rows, small_pad - bcw // 2), F32),
            pltpu.VMEM((rows, bcw // 2), F32),
            pltpu.VMEM((rows, 2 * chan), F32),
        ]
        + [
            pltpu.VMEM((rows, small_pad), BF16),
            pltpu.VMEM((rows, bcw // 2), BF16),
            pltpu.VMEM((nm, rows, 2 * chan), BF16),
            pltpu.VMEM((rows, window), BF16),
            pltpu.VMEM((nd, rows, 2 * LANES), BF16),
        ]
        + [
            pltpu.VMEM((all_rows, feat), BF16),
            pltpu.VMEM((nm, rows, small_pad), BF16),
            pltpu.VMEM((nd, rows, bcw // 2), BF16),
            pltpu.VMEM((ratio, rows, bcw // 2), BF16),
            pltpu.VMEM((nm, rows, 2 * chan), BF16),
            pltpu.VMEM((nm, rows, window), BF16),
            pltpu.VMEM((nd, rows, 2 * LANES), BF16),
            pltpu.VMEM((rows, feat), BF16),
            pltpu.VMEM((nd, rows, 2 * LANES), BF16),
        ]
        + [
            dma((15,)),
            dma((sends,)),
            dma((nd,)),
            dma((nd,)),
            dma((3, 4)),
            dma((nm,)),
            dma((nd,)),
            dma((ratio,)),
            dma((nm,)),
            dma((nd * ratio,)),
            dma((nd,)),
            dma((1,)),
            dma((nd,)),
        ]
    )
    inside = pl.pallas_call(
        functools.partial(kernel, size),
        out_shape=(
            jax.ShapeDtypeStruct((rows, feat), BF16),
            jax.ShapeDtypeStruct((rows, chan, state), F32),
        ),
        in_specs=[pl.BlockSpec(memory_space=pltpu.HBM)] * 5
        + [pl.BlockSpec(memory_space=pltpu.HBM)] * 10,
        out_specs=(
            pl.BlockSpec(memory_space=pltpu.VMEM),
            pl.BlockSpec(memory_space=pltpu.VMEM),
        ),
        scratch_shapes=scratch,
        compiler_params=pltpu.CompilerParams(
            collective_id=0, has_side_effects=True, vmem_limit_bytes=48 << 20
        ),
    )(*[pltpu.with_memory_space_constraint(a, pltpu.HBM) for a in operands])
    hidden, states = pl.pallas_call(
        functools.partial(store, rows // 2),
        out_shape=(
            jax.ShapeDtypeStruct((rows, feat), BF16),
            jax.ShapeDtypeStruct((rows, chan, state), F32),
        ),
        in_specs=[pl.BlockSpec(memory_space=pltpu.VMEM)] * 2,
        out_specs=(pl.BlockSpec(memory_space=pltpu.HBM),) * 2,
        scratch_shapes=[dma((1 + rows // 2,))],
        compiler_params=pltpu.CompilerParams(vmem_limit_bytes=8 << 20),
    )(*inside)
    return (
        hidden[None],
        states.reshape(1, rows, heads_dev, head, state),
    )


def solution(mesh):
    placed = (
        P("dp", "mp"),
        P("dp"),
        P("dp"),
        P("section", None),
        P("section", None, "dp", "mp"),
        P("section", "dp", "mp"),
        P("section", None, "mp"),
        P("section", None, None),
        P("section", "dp", None, "mp"),
        P("section", "dp", None, None),
        P("section", "dp", "mp", None, None),
        P("section", "mp"),
        P("section", "mp"),
        P("section", "mp"),
        P("section", "mp"),
    )
    return jax.shard_map(
        local,
        mesh=mesh,
        in_specs=placed,
        out_specs=(P("section", "dp", "mp"), P("section", "dp", "mp", None, None)),
        check_vma=False,
    )
```

```python
import functools

import jax
import jax.numpy as jnp
from jax import lax
from jax.experimental import pallas as pl
from jax.experimental.pallas import tpu as pltpu
from jax.sharding import PartitionSpec as P

EPS = 1e-05
F32 = jnp.float32
BF16 = jnp.bfloat16
LANES = 128


def silu(v):
    return v * (1.0 / (1.0 + jnp.exp(-v)))


def softplus(v):
    return jnp.maximum(v, 0.0) + jnp.log1p(jnp.exp(-jnp.abs(v)))


def halves(v):
    top = v.astype(BF16).astype(F32)
    return top, v - top


def iota(shape, dim):
    return lax.broadcasted_iota(jnp.int32, shape, dim)


def mm(a, b):
    return lax.dot_general(a, b, (((1,), (0,)), ((), ())), preferred_element_type=F32)


def mm_t(a, b):
    return lax.dot_general(a, b, (((1,), (1,)), ((), ())), preferred_element_type=F32)


def kernel(
    size,
    len_h,
    slot_h,
    rate_h,
    bias_h,
    skip_h,
    hid_h,
    gain_h,
    w_h,
    wb_h,
    cxw_h,
    cbw_h,
    cxp_h,
    cbp_h,
    st_h,
    gg_h,
    hid_o,
    st_o,
    len_s,
    slot_s,
    rate_s,
    bias_s,
    skip_s,
    hid,
    gain,
    w,
    wb,
    cxw,
    cbw,
    cxp,
    cbp,
    st,
    gg,
    wg,
    perm,
    wsmall,
    h,
    past_x,
    past_b,
    alive,
    expand,
    old16,
    wide_b,
    wide_c,
    outer_l,
    outer_t,
    hid_new,
    acc_s,
    acc_b,
    acc_m,
    send_s,
    send_u,
    send_m,
    send_b,
    send_c,
    recv_x,
    recv_s,
    recv_t,
    recv_u,
    recv_m,
    recv_b,
    recv_c,
    recv_h,
    recv_o,
    load_sem,
    send_sem,
    x_sem,
    w_sem,
    g_sem,
    s_sem,
    t_sem,
    u_sem,
    m_sem,
    b_sem,
    c_sem,
    h_sem,
    o_sem,
):
    nd, nm, ns, rows, feat, chan, head, small, bcw, slots_dev, width, inner = size
    ratio = nm // nd
    pairs = ratio // 2
    pair = 2 * chan
    two = 2 * LANES
    gap = chan - two
    window = 3 * LANES
    half = feat // 2
    side = bcw // 2
    front = wsmall.shape[1] - side
    mark = small - side
    d = lax.axis_index("dp")
    m = lax.axis_index("mp")
    sec = lax.axis_index("section")
    home = m // ratio
    mine = lax.rem(m, ratio)
    odd = lax.rem(mine, 2) == 1
    on_home = home == d
    per_dp = small // nd
    all_rows = nd * rows
    heads_dev = chan // head
    first = sec == 0
    later = sec > 0
    more = sec < ns - 1
    after = jnp.minimum(sec + 1, ns - 1)
    my_rows = pl.ds(pl.multiple_of(d * rows, rows), rows)
    far_first = (2, 1, 3, 0) if nd == 4 else tuple(range(nd))

    srcs = (
        (hid_h, hid),
        (gain_h, gain),
        (wb_h, wb),
        (w_h, w.at[d]),
        (cxw_h, cxw),
        (cbw_h, cbw),
        (cxp_h, cxp),
        (cbp_h, cbp),
        (st_h, st),
        (gg_h, gg),
        (len_h, len_s),
        (slot_h, slot_s),
        (rate_h, rate_s),
        (bias_h, bias_s),
        (skip_h, skip_s),
    )
    loads = [
        pltpu.make_async_copy(src, dst, load_sem.at[i]) for i, (src, dst) in enumerate(srcs)
    ]
    loads[0].start()
    loads[2].start()

    barrier = pltpu.get_barrier_semaphore()

    def tell(dp, mp, section=None):
        where = {"dp": dp, "mp": mp}
        if section is not None:
            where["section"] = section
        pl.semaphore_signal(
            barrier, inc=1, device_id=where, device_id_type=pl.DeviceIdType.MESH
        )

    for k in range(1, nd):
        tell(lax.rem(d + k, nd), m)
    for k in range(1, nm):
        tell(d, lax.rem(m + k, nm))

    @pl.when(first)
    def _():
        for i in range(nm):

            @pl.when(jnp.logical_not(on_home & (m == i)))
            def _():
                tell(home, i)

        for i in range(nd):
            for j in range(ratio):

                @pl.when(jnp.logical_not((d == i) & (m == d * ratio + j)))
                def _():
                    tell(i, d * ratio + j)

    @pl.when(sec == 1)
    def _():
        for k in range(nd):
            tell(k, m, 0)

    @pl.when(sec > 1)
    def _():
        tell(d, m, sec - 1)

    loads[3].start()
    for i in (1, *range(4, len(loads))):
        loads[i].start()

    own = jnp.where(on_home, 1, 0)
    pl.semaphore_wait(
        barrier,
        nd
        - 1
        + nm
        - 1
        + jnp.where(first, 2 * (nm - own) + nd, jnp.where(more, 1, 0)),
    )

    count = 0
    bases = {}
    for name, n in (
        ("x", nd - 1),
        ("w", nd - 1),
        ("g", 12),
        ("s", nm),
        ("m", nm),
        ("b", nm),
        ("c", nd),
        ("h", 1),
        ("o", nd - 1),
        ("t", nd - 1),
        ("u", ratio - 1),
    ):
        bases[name] = count
        count += n

    def block_of(i):
        return pl.ds(pl.multiple_of(i * rows, rows), rows)

    def copies_x():
        for k in range(1, nd):
            there = {"dp": lax.rem(d + k, nd), "mp": m}
            yield hid, recv_x.at[my_rows], x_sem.at[d], there, None

    def copies_w():
        for k in range(1, nd):
            there = {"dp": lax.rem(d + k, nd), "mp": m}
            yield wg.at[d], wg.at[d], w_sem.at[d], there, None

    up = lax.rem(d + 1, nd)
    down = lax.rem(d + nd - 1, nd)
    across = lax.rem(d + 2, nd)

    parts = (slice(1, 2), slice(0, 1), slice(2, 3))

    def copies_g(part):
        at = parts[part]
        yield w.at[d, at], w.at[d, at], g_sem.at[part, 0], {"dp": up, "mp": m}, None
        if nd == 4:
            yield w.at[d, at], w.at[d, at], g_sem.at[part, 1], {"dp": down, "mp": m}, None

    def copies_g2(part, which):
        at = parts[part]
        if which == 0:
            block = w.at[down, at, 0:half]
            yield block, block, g_sem.at[part, 2], {"dp": up, "mp": m}, None
        else:
            block = w.at[up, at, half:feat]
            yield block, block, g_sem.at[part, 3], {"dp": down, "mp": m}, None

    def pass_on(part):
        at = parts[part]
        arrived(w.at[down, at], g_sem.at[part, 0])
        if nd == 4:
            start(bases["g"] + 4 * part + 2, copies_g2(part, 0))
            arrived(w.at[up, at], g_sem.at[part, 1])
            start(bases["g"] + 4 * part + 3, copies_g2(part, 1))

    def passed_on(part):
        at = parts[part]
        if nd == 4:
            arrived(w.at[across, at, 0:half], g_sem.at[part, 2])
            arrived(w.at[across, at, half:feat], g_sem.at[part, 3])

    others = sorted(range(1, nm), key=lambda k: abs(k - nm // 2))

    def copies_s(lanes):
        for k in others:
            there = {"dp": d, "mp": lax.rem(m + k, nm)}
            yield send_s.at[:, 0:lanes], recv_s.at[m, :, 0:lanes], s_sem.at[m], there, None

    def copies_t():
        for k in range(1, nd):
            to = lax.rem(home + k, nd) * ratio + mine
            part = send_s.at[:, front:]
            yield part, recv_t.at[home], t_sem.at[home], {"dp": d, "mp": to}, None

    def copies_u():
        for k in range(1, ratio):
            to = home * ratio + lax.rem(mine + k, ratio)
            yield send_u, recv_u.at[mine], u_sem.at[mine], {"dp": d, "mp": to}, None

    def copies_m_first(p):
        for k in far_first:
            i = lax.rem(d + k, nd)
            for j in (2 * p, 2 * p + 1):
                there = {"dp": i, "mp": d * ratio + j}
                same = m == d * ratio + j if k == 0 else None
                block = send_m.at[j * nd + i]
                yield block, recv_m.at[m], m_sem.at[m], there, same

    def copies_m_later(k, p):
        i = lax.rem(home + k, nd)
        for j in (2 * p, 2 * p + 1):
            to = i * ratio + j
            same = to == m if k == 0 else None
            yield send_m.at[to], recv_m.at[m], m_sem.at[m], {"dp": d, "mp": to}, same

    def copies_b_first():
        for k in range(nm):
            i = lax.rem(m + nm // 2 + k, nm)
            slot = mine * nd + d
            there = {"dp": home, "mp": i}
            same = on_home if k == nm // 2 else None
            yield send_b, recv_b.at[slot], b_sem.at[slot], there, same

    def copies_b_later():
        for k in others:
            there = {"dp": d, "mp": lax.rem(m + k, nm)}
            yield send_b, recv_b.at[m], b_sem.at[m], there, None

    def copies_c():
        for k in far_first:
            i = lax.rem(d + k, nd)
            there = {"dp": i, "mp": m, "section": after}
            yield send_c.at[i], recv_c.at[d], c_sem.at[d], there, None

    def copies_h(src):
        yield src, recv_h, h_sem.at[0], {"dp": d, "mp": m, "section": after}, None

    def copies_o():
        for k in range(1, nd):
            i = lax.rem(d + k, nd)
            yield send_c.at[i], recv_o.at[d], o_sem.at[d], {"dp": i, "mp": m}, None

    def remote(at, src, dst, recv, where):
        return pltpu.make_async_remote_copy(
            src_ref=src,
            dst_ref=dst,
            send_sem=send_sem.at[at],
            recv_sem=recv,
            device_id=where,
            device_id_type=pl.DeviceIdType.MESH,
        )

    def start(base, items):
        for n, (src, dst, recv, where, same) in enumerate(items):
            copy = remote(base + n, src, dst, recv, where)
            if same is None:
                copy.start()
            else:

                @pl.when(jnp.logical_not(same))
                def _():
                    copy.start()

                @pl.when(same)
                def _():
                    pltpu.make_async_copy(src, dst, recv).start()

    def finish(base, items):
        for n, (src, dst, recv, where, same) in enumerate(items):
            copy = remote(base + n, src, dst, recv, where)
            if same is None:
                copy.wait_send()
            else:

                @pl.when(jnp.logical_not(same))
                def _():
                    copy.wait_send()

    def arrived(ref, sem):
        pltpu.make_async_copy(ref, ref, sem).wait()

    loads[0].wait()

    @pl.when(first)
    def _():
        start(bases["x"], copies_x())

    loads[2].wait()
    group_w = wg.shape[2]
    wg[d] = jnp.zeros((feat, group_w), BF16)
    wg[d, :, 0:per_dp] = wb[...]
    start(bases["w"], copies_w())
    loads[3].wait()

    @pl.when(later)
    def _():
        start(bases["g"], copies_g(0))
        start(bases["g"] + 4, copies_g(1))

    col = iota(perm.shape, 1)
    row = iota(perm.shape, 0)
    group = row // group_w
    inside = row - group * group_w
    source = group * per_dp + inside
    target = jnp.where(source < side, source + front, source - side)
    perm[...] = jnp.where((inside < per_dp) & (col == target), 1.0, 0.0).astype(BF16)
    lane_of = iota((LANES, chan), 1) // head
    expand[...] = jnp.where(
        iota((LANES, chan), 0) == m * heads_dev + lane_of, 1.0, 0.0
    ).astype(BF16)
    wide_b[...] = jnp.zeros_like(wide_b)
    wide_c[...] = jnp.zeros_like(wide_c)
    outer_l[...] = jnp.zeros_like(outer_l)
    loads[1].wait()
    offset = m * feat
    base = offset // LANES
    gain_w = gain[:, pl.ds(pl.multiple_of(base * LANES, LANES), two)]
    gain_w = jnp.broadcast_to(gain_w, (8, two))
    gain_w = pltpu.roll(gain_w, lax.rem(two - (offset - base * LANES), two), 1)
    gain_row = gain_w[0:1, 0:feat]

    def prepare():
        for copy in loads[4:9] + loads[10:]:
            copy.wait()
        tap = iota((3, 1), 0)
        taps_x = cxw[0:3, :]
        taps_b = cbw[0:3, :]

        def one(s, carry):
            slot = jnp.clip(slot_s[s] - d * slots_dev, 0, slots_dev - 1)
            seen = (tap + len_s[s] >= 3).astype(F32)
            past_x[pl.ds(s, 1), :] = jnp.sum(
                cxp[slot].astype(F32) * seen * taps_x, axis=0, keepdims=True
            )
            past_b[pl.ds(s, 1), :] = jnp.sum(
                cbp[slot].astype(F32) * seen * taps_b, axis=0, keepdims=True
            )
            alive[pl.ds(s, 1), :] = jnp.full(
                (1, LANES), jnp.where(len_s[s] > 0, 1.0, 0.0), F32
            )
            old16[s] = st[slot].astype(BF16)
            return carry

        lax.fori_loop(0, rows, one, 0)

    def after_norm(acc, residual):
        lane = iota(acc.shape, 1)
        squares = jnp.sum(
            jnp.where((lane == feat) | (lane == feat + 1), acc, 0.0), axis=1, keepdims=True
        )
        scale = lax.rsqrt(squares / inner + EPS)
        return (residual.astype(F32) + acc[:, 0:feat] * scale).astype(BF16)

    def pack(inner_p, gate_p, even, other, shape):
        lane = iota((inner_p.shape[0], LANES), 1)
        inner_t = inner_p[:, two:window]
        gate_t = pltpu.roll(gate_p[:, two:window], gap, 1)
        for at, side, edge in (
            (even, slice(0, two), jnp.where(lane < gap, inner_t, gate_t)),
            (other, slice(window, pair), jnp.where(lane < gap, gate_t, inner_t)),
        ):
            send_m[at, :, 0:two] = inner_p[:, side].astype(BF16).reshape(*shape, two)
            send_m[at, :, two : 2 * two] = gate_p[:, side].astype(BF16).reshape(*shape, two)
            send_m[at, :, 2 * two : pair] = edge.astype(BF16).reshape(*shape, LANES)

    def with_two(out, squares, at):
        high, low = halves(squares)
        lane = iota(out.shape, 1)
        return jnp.where(lane == at, high, jnp.where(lane == at + 1, low, out))

    def two_of(acc, at):
        lane = iota(acc.shape, 1)
        return jnp.sum(
            jnp.where((lane == at) | (lane == at + 1), acc, 0.0), axis=1, keepdims=True
        )

    def weights_small():
        for k in range(1, nd):
            i = lax.rem(d + k, nd)
            arrived(wg.at[i], w_sem.at[i])
        total = mm(wg[0], perm[0:group_w, :])
        for i in range(1, nd):
            total += mm(wg[i], perm[i * group_w : (i + 1) * group_w, :])
        wsmall[...] = total.astype(BF16)

    def start_small(lanes):
        value = h[...].astype(F32)
        squares = jnp.sum(value * value, axis=1, keepdims=True)
        v = (value * gain_row).astype(BF16)
        send_s[...] = with_two(mm(v, wsmall[...]), squares, mark).astype(BF16)
        start(bases["s"], copies_s(lanes))
        pltpu.make_async_copy(
            send_s.at[:, 0:lanes], recv_s.at[m, :, 0:lanes], s_sem.at[m]
        ).start()
        return v

    @pl.when(first)
    def _():
        for k in range(1, nd):
            i = lax.rem(d + k, nd)
            arrived(recv_x.at[block_of(i)], x_sem.at[i])
        recv_x[my_rows, :] = hid[...]
        h[...] = hid[...]
        v_all = (recv_x[...].astype(F32) * gain_row).astype(BF16)
        for p in range(pairs):
            cols = slice(p * pair, (p + 1) * pair)
            e = 2 * p * nd
            pack(
                mm(v_all, w[d, 1, :, cols]),
                mm(v_all, w[d, 0, :, cols]),
                slice(e, e + nd),
                slice(e + nd, e + 2 * nd),
                (nd, rows),
            )
            start(bases["m"] + e, copies_m_first(p))
        weights_small()
        start_small(front + side)
        start(bases["h"], copies_h(h))
        prepare()

    @pl.when(later)
    def _():
        weights_small()
        prepare()
        pass_on(0)
        pass_on(1)
        start(bases["g"] + 8, copies_g(2))
        passed_on(0)
        passed_on(1)
        arrived(recv_h, h_sem.at[0])

        @pl.when(sec == 1)
        def _():
            acc = None
            for i in range(nd):
                arrived(recv_c.at[i], c_sem.at[i])
                part = recv_c[i].astype(F32)
                acc = part if acc is None else acc + part
            h[...] = after_norm(acc, recv_h[...])

        @pl.when(sec > 1)
        def _():
            h[...] = recv_h[...]

        v = start_small(front)
        start(bases["t"], copies_t())
        for n, k in enumerate(far_first):
            i = lax.rem(home + k, nd)
            for p in range(pairs):
                cols = slice(p * pair, (p + 1) * pair)
                e = i * ratio + 2 * p
                pack(mm(v, w[i, 1, :, cols]), mm(v, w[i, 0, :, cols]), e, e + 1, (rows,))
                start(bases["m"] + n * ratio + 2 * p, copies_m_later(k, p))
        acc = send_s[:, front:].astype(F32)
        for k in range(1, nd):
            i = lax.rem(home + k, nd)
            arrived(recv_t.at[i], t_sem.at[i])
            acc += recv_t[i].astype(F32)
        send_u[...] = acc.astype(BF16)
        start(bases["u"], copies_u())
        pass_on(2)

    loads[9].wait()
    per_head = iota((1, chan), 1) // head
    rate_row = jnp.zeros((1, chan), F32)
    bias_row = jnp.zeros((1, chan), F32)
    skip_row = jnp.zeros((1, chan), F32)
    for i in range(heads_dev):
        rate_row = jnp.where(per_head == i, rate_s[0, i], rate_row)
        bias_row = jnp.where(per_head == i, bias_s[0, i], bias_row)
        skip_row = jnp.where(per_head == i, skip_s[0, i], skip_row)

    def sum_of(ref, sem, lanes):
        acc = None
        for i in range(nm):
            arrived(ref.at[i, :, 0:lanes], sem.at[i])
            part = ref[i, :, 0:lanes].astype(F32)
            acc = part if acc is None else acc + part
        return acc

    @pl.when(first)
    def _():
        acc = sum_of(recv_s, s_sem, front + side)
        acc_s[...] = acc[:, 0:front]
        acc_b[...] = acc[:, front:]

    @pl.when(later)
    def _():
        acc_s[...] = sum_of(recv_s, s_sem, front)

    acc = acc_s[...]
    scale = lax.rsqrt(two_of(acc, mark) / width + EPS)
    c_cur = silu(past_b[:, side:] + acc[:, 0:side] * scale * cbw[3:4, side:])
    c_high, c_low = halves(c_cur)
    c_two = jnp.concatenate([c_high, c_low], axis=0).astype(BF16)
    c_row = lax.rem(iota((2 * rows, 1), 0), rows)

    def ask(s, carry):
        return carry + mm_t(jnp.where(c_row == s, c_two, jnp.zeros_like(c_two)), old16[s])

    both = lax.fori_loop(
        0, rows, ask, jnp.zeros((2 * rows, chan), F32), unroll=True
    )
    read = both[0:rows] + both[rows:]
    high, low = halves(acc[:, side:])
    raw = mm(high.astype(BF16), expand[...]) + mm(low.astype(BF16), expand[...])
    step = softplus(raw * scale + bias_row)
    decay = jnp.exp(-step * rate_row) * alive[:, 0:1]

    @pl.when(first)
    def _():
        acc_m[...] = sum_of(recv_m, m_sem, pair)

    @pl.when(later)
    def _():
        acc = send_u[...].astype(F32)
        for k in range(1, ratio):
            i = lax.rem(mine + k, ratio)
            arrived(recv_u.at[i], u_sem.at[i])
            acc += recv_u[i].astype(F32)
        acc_b[...] = acc
        acc_m[...] = sum_of(recv_m, m_sem, pair)

    b_cur = silu(past_b[:, 0:side] + acc_b[...] * scale * cbw[3:4, 0:side])
    bc_dot = jnp.sum(b_cur * c_cur, axis=1, keepdims=True)
    acc = acc_m[...]
    tile = acc[:, 2 * two :]
    other = pltpu.roll(tile, gap, 1)

    def in_order(part, edge):
        before = jnp.concatenate([edge, part], axis=1)
        behind = jnp.concatenate([part, edge], axis=1)
        return jnp.where(odd, pltpu.roll(before, chan, 1), behind)[:, 0:chan]

    acc_i = in_order(acc[:, 0:two], tile)
    acc_g = in_order(acc[:, two : 2 * two], other)
    x = silu(past_x[...] + acc_i * scale * cxw[3:4, :])
    sx = step * x
    gated = (decay * read + sx * bc_dot + skip_row * x) * silu(acc_g * scale)
    squares = jnp.sum(gated * gated, axis=1, keepdims=True)
    wide_b[:, 0:chan] = gated * gg[...]
    full = wide_b[...]
    high, low = halves(squares)
    lane = iota(full.shape, 1)
    full = jnp.where(lane == chan, high, jnp.where(lane == chan + 1, low, full))
    full = jnp.where(odd, pltpu.roll(full, window - chan, 1), full)
    send_b[...] = full.astype(BF16)

    @pl.when(first)
    def _():
        start(bases["b"], copies_b_first())

    @pl.when(later)
    def _():
        start(bases["b"], copies_b_later())
        pltpu.make_async_copy(send_b, recv_b.at[m], b_sem.at[m]).start()

    s_high, s_low = halves(sx)
    d_high, d_low = halves(decay)
    b_high, b_low = halves(b_cur)
    outer_l[0:rows, 0:chan] = s_high
    outer_l[rows : 2 * rows, 0:chan] = s_high
    outer_l[2 * rows : 3 * rows, 0:chan] = s_low
    outer_l[3 * rows : 4 * rows, 0:chan] = d_high
    outer_l[4 * rows : 5 * rows, 0:chan] = d_low
    outer_t[...] = jnp.transpose(outer_l[...])[0:chan, :].astype(BF16)
    zero = jnp.zeros((rows, LANES), F32)
    one_ = jnp.ones((rows, LANES), F32)
    right = jnp.concatenate(
        [
            jnp.concatenate([b_high, b_low, b_high, zero, zero], axis=0),
            jnp.concatenate([zero, zero, zero, one_, one_], axis=0),
        ],
        axis=1,
    )
    right = jnp.concatenate(
        [right, jnp.zeros((LANES - 5 * rows, two), F32)], axis=0
    ).astype(BF16)
    r_row = lax.rem(iota((LANES, 1), 0), rows)

    def update(s, carry):
        slot = jnp.clip(slot_s[s] - d * slots_dev, 0, slots_dev - 1)
        both = mm(outer_t[...], jnp.where(r_row == s, right, jnp.zeros_like(right)))
        st_o[s] = both[:, LANES:] * st[slot] + both[:, 0:LANES]
        return carry

    before = jnp.where(more, rows // 2, rows)
    lax.fori_loop(0, before, update, 0)

    def gathered(even_s, other_s, count):
        n = count * rows
        lane = iota((n, LANES), 1)
        even_t = recv_b[even_s, :, two:window].astype(F32).reshape(n, LANES)
        odd_t = recv_b[other_s, :, 0:LANES].astype(F32).reshape(n, LANES)
        squares = jnp.sum(
            jnp.where((lane == gap) | (lane == gap + 1), even_t, 0.0)
            + jnp.where(lane < 2, odd_t, 0.0),
            axis=1,
            keepdims=True,
        )
        middle = jnp.where(lane < gap, even_t, odd_t).astype(BF16)
        left = recv_b[even_s, :, 0:two].reshape(n, two)
        right = recv_b[other_s, :, LANES:window].reshape(n, two)
        return jnp.concatenate([left, middle, right], axis=1), squares

    def with_squares(out, squares, n):
        wide_c[0:n, 0:feat] = out
        full = wide_c[0:n, :]
        high, low = halves(squares)
        lane = iota(full.shape, 1)
        return jnp.where(lane == feat, high, jnp.where(lane == feat + 1, low, full))

    @pl.when(first)
    def _():
        out = jnp.zeros((all_rows, feat), F32)
        squares = jnp.zeros((all_rows, 1), F32)
        for p in range(pairs):
            e = 2 * p * nd
            for i in range(2 * nd):
                arrived(recv_b.at[e + i], b_sem.at[e + i])
            lhs, part = gathered(slice(e, e + nd), slice(e + nd, e + 2 * nd), nd)
            squares += part
            out += mm_t(lhs, w[d, 2, :, p * pair : (p + 1) * pair])
        full = with_squares(out, squares, all_rows)
        send_c[...] = full.astype(BF16).reshape(nd, rows, two)
        start(bases["c"], copies_c())
        start(bases["o"], copies_o())
        recv_o[d] = send_c[d]

    @pl.when(later)
    def _():
        passed_on(2)
        finish(bases["s"], copies_s(front))
        finish(bases["t"], copies_t())
        finish(bases["u"], copies_u())
        for part in (0, 1, 2):
            finish(bases["g"] + 4 * part, copies_g(part))
            if nd == 4:
                finish(bases["g"] + 4 * part + 2, copies_g2(part, 0))
                finish(bases["g"] + 4 * part + 3, copies_g2(part, 1))
        for n, k in enumerate(far_first):
            for p in range(pairs):
                finish(bases["m"] + n * ratio + 2 * p, copies_m_later(k, p))
        out = jnp.zeros((rows, feat), F32)
        squares = jnp.zeros((rows, 1), F32)
        for i in range(nd):
            for p in range(pairs):
                e = i * ratio + 2 * p
                arrived(recv_b.at[e], b_sem.at[e])
                arrived(recv_b.at[e + 1], b_sem.at[e + 1])
                lhs, part = gathered(e, e + 1, 1)
                squares += part
                out += mm_t(lhs, w[i, 2, :, p * pair : (p + 1) * pair])
        hid_new[...] = after_norm(with_squares(out, squares, rows), h[...])

        @pl.when(more)
        def _():
            start(bases["h"], copies_h(hid_new))

    lax.fori_loop(before, rows, update, 0)

    @pl.when(first)
    def _():
        for k in range(1, nd):
            i = lax.rem(d + k, nd)
            arrived(recv_o.at[i], o_sem.at[i])
        acc = recv_o[0].astype(F32)
        for i in range(1, nd):
            acc += recv_o[i].astype(F32)
        hid_new[...] = after_norm(acc, h[...])

    hid_o[...] = hid_new[...]

    finish(bases["w"], copies_w())

    @pl.when(first)
    def _():
        finish(bases["x"], copies_x())
        finish(bases["s"], copies_s(front + side))
        for p in range(pairs):
            finish(bases["m"] + 2 * p * nd, copies_m_first(p))
        finish(bases["h"], copies_h(h))
        finish(bases["b"], copies_b_first())
        finish(bases["c"], copies_c())
        finish(bases["o"], copies_o())

    @pl.when(later)
    def _():
        finish(bases["b"], copies_b_later())

        @pl.when(more)
        def _():
            finish(bases["h"], copies_h(hid_new))


def store(parts, hid_v, st_v, hid_o, st_o, sem):
    n = st_v.shape[0] // parts
    copies = [pltpu.make_async_copy(hid_v, hid_o, sem.at[parts])] + [
        pltpu.make_async_copy(
            st_v.at[i * n : (i + 1) * n], st_o.at[i * n : (i + 1) * n], sem.at[i]
        )
        for i in range(parts)
    ]
    for copy in copies:
        copy.start()
    for copy in copies:
        copy.wait()


def local(
    hidden_in,
    lengths,
    slots,
    norm_gain,
    w_zxo,
    w_bcdt,
    conv_x_weight,
    conv_bc_weight,
    conv_x_pool,
    conv_bc_pool,
    state_pool,
    a_rate,
    dt_bias,
    skip_gain,
    gate_gain,
):
    nd, nm, ns = (lax.axis_size(name) for name in ("dp", "mp", "section"))
    rows, feat = hidden_in.shape
    width = norm_gain.shape[1]
    chan_dp = w_zxo.shape[2]
    per_dp = w_bcdt.shape[1]
    slots_dev, heads_dev, head, state = state_pool.shape[1:]
    chan = heads_dev * head
    bcw = conv_bc_weight.shape[2]
    small = per_dp * nd
    small_pad = -(-(small - bcw // 2 + 2) // LANES) * LANES + bcw // 2
    group_w = -(-per_dp // LANES) * LANES
    ratio = nm // nd
    all_rows = nd * rows
    window = 3 * LANES
    size = (
        nd, nm, ns, rows, feat, chan, head, small, bcw, slots_dev, width, chan * nm,
    )
    operands = (
        lengths,
        slots,
        a_rate,
        dt_bias,
        skip_gain,
        hidden_in,
        norm_gain,
        jnp.swapaxes(w_zxo[0], 1, 2),
        jnp.swapaxes(w_bcdt[0], 0, 1),
        conv_x_weight[0],
        conv_bc_weight[0],
        conv_x_pool[0],
        conv_bc_pool[0],
        state_pool.reshape(slots_dev, chan, state),
        gate_gain,
    )
    sends = 5 * nd + ratio + 3 * nm + 8
    dma = pltpu.SemaphoreType.DMA
    scratch = (
        [pltpu.SMEM(a.shape, a.dtype) for a in operands[:5]]
        + [
            pltpu.VMEM((nd, *a.shape) if i == 7 else a.shape, a.dtype)
            for i, a in enumerate(operands)
            if i >= 5
        ]
        + [
            pltpu.VMEM((nd, feat, group_w), BF16),
            pltpu.VMEM((nd * group_w, small_pad), BF16),
            pltpu.VMEM((feat, small_pad), BF16),
            pltpu.VMEM((rows, feat), BF16),
            pltpu.VMEM((rows, chan), F32),
            pltpu.VMEM((rows, bcw), F32),
            pltpu.VMEM((rows, LANES), F32),
            pltpu.VMEM((LANES, chan), BF16),
            pltpu.VMEM((rows, chan, state), BF16),
            pltpu.VMEM((rows, window), F32),
            pltpu.VMEM((all_rows, 2 * LANES), F32),
            pltpu.VMEM((LANES, window), F32),
            pltpu.VMEM((chan, LANES), BF16),
            pltpu.VMEM((rows, feat), BF16),
            pltpu.VMEM((rows, small_pad - bcw // 2), F32),
            pltpu.VMEM((rows, bcw // 2), F32),
            pltpu.VMEM((rows, 2 * chan), F32),
        ]
        + [
            pltpu.VMEM((rows, small_pad), BF16),
            pltpu.VMEM((rows, bcw // 2), BF16),
            pltpu.VMEM((nm, rows, 2 * chan), BF16),
            pltpu.VMEM((rows, window), BF16),
            pltpu.VMEM((nd, rows, 2 * LANES), BF16),
        ]
        + [
            pltpu.VMEM((all_rows, feat), BF16),
            pltpu.VMEM((nm, rows, small_pad), BF16),
            pltpu.VMEM((nd, rows, bcw // 2), BF16),
            pltpu.VMEM((ratio, rows, bcw // 2), BF16),
            pltpu.VMEM((nm, rows, 2 * chan), BF16),
            pltpu.VMEM((nm, rows, window), BF16),
            pltpu.VMEM((nd, rows, 2 * LANES), BF16),
            pltpu.VMEM((rows, feat), BF16),
            pltpu.VMEM((nd, rows, 2 * LANES), BF16),
        ]
        + [
            dma((15,)),
            dma((sends,)),
            dma((nd,)),
            dma((nd,)),
            dma((3, 4)),
            dma((nm,)),
            dma((nd,)),
            dma((ratio,)),
            dma((nm,)),
            dma((nd * ratio,)),
            dma((nd,)),
            dma((1,)),
            dma((nd,)),
        ]
    )
    inside = pl.pallas_call(
        functools.partial(kernel, size),
        out_shape=(
            jax.ShapeDtypeStruct((rows, feat), BF16),
            jax.ShapeDtypeStruct((rows, chan, state), F32),
        ),
        in_specs=[pl.BlockSpec(memory_space=pltpu.HBM)] * 5
        + [pl.BlockSpec(memory_space=pltpu.HBM)] * 10,
        out_specs=(
            pl.BlockSpec(memory_space=pltpu.VMEM),
            pl.BlockSpec(memory_space=pltpu.VMEM),
        ),
        scratch_shapes=scratch,
        compiler_params=pltpu.CompilerParams(
            collective_id=0, has_side_effects=True, vmem_limit_bytes=48 << 20
        ),
    )(*[pltpu.with_memory_space_constraint(a, pltpu.HBM) for a in operands])
    hidden, states = pl.pallas_call(
        functools.partial(store, rows // 2),
        out_shape=(
            jax.ShapeDtypeStruct((rows, feat), BF16),
            jax.ShapeDtypeStruct((rows, chan, state), F32),
        ),
        in_specs=[pl.BlockSpec(memory_space=pltpu.VMEM)] * 2,
        out_specs=(pl.BlockSpec(memory_space=pltpu.HBM),) * 2,
        scratch_shapes=[dma((1 + rows // 2,))],
        compiler_params=pltpu.CompilerParams(vmem_limit_bytes=8 << 20),
    )(*inside)
    return (
        hidden[None],
        states.reshape(1, rows, heads_dev, head, state),
    )


def solution(mesh):
    placed = (
        P("dp", "mp"),
        P("dp"),
        P("dp"),
        P("section", None),
        P("section", None, "dp", "mp"),
        P("section", "dp", "mp"),
        P("section", None, "mp"),
        P("section", None, None),
        P("section", "dp", None, "mp"),
        P("section", "dp", None, None),
        P("section", "dp", "mp", None, None),
        P("section", "mp"),
        P("section", "mp"),
        P("section", "mp"),
        P("section", "mp"),
    )
    return jax.shard_map(
        local,
        mesh=mesh,
        in_specs=placed,
        out_specs=(P("section", "dp", "mp"), P("section", "dp", "mp", None, None)),
        check_vma=False,
    )
```
